128 devices in a mesh: front: 32 (over y, x, core), enc: 4 (over z).
Axes of the slice: x: 4, y: 4, z: 4, core: 2. Of those that a mesh axis runs over, the one named last changes fastest.
Arguments:
- spectra: bfloat16 [4096, 56, 80], P('front'), may hold values from -6 to 6
- sub_weight: bfloat16 [640, 1024], P(None, 'enc'), may hold values from -0.25 to 0.25
- sub_bias: bfloat16 [1024], P('enc'), may hold values from -4 to 4
- key_cache: bfloat16 [4096, 70, 1024], P('front', None, 'enc'), may hold values from -1000 to 1000
- value_cache: bfloat16 [4096, 70, 1024], P('front', None, 'enc'), may hold values from -6 to 6
- conv_cache: bfloat16 [4096, 8, 1024], P('front', None, 'enc'), may hold values from -6 to 6
- new_slot: int32 [4096], P('front'), may hold values from 0 to 4095, as said below
- old_slot: int32 [4096], P('front'), may hold values from 0 to 4095, as said below
- valid_new: int32 [4096], P('front'), may hold values from 1 to 7
- cache_fill: int32 [4096], P('front'), may hold values from 0 to 70
- ln1_gain: float32 [1024], replicated, may hold values from 0.5 to 1.5
- w_query: bfloat16 [1024, 1024], P(None, 'enc'), may hold values from -0.1875 to 0.1875
- w_key: bfloat16 [1024, 1024], P(None, 'enc'), may hold values from -0.1875 to 0.1875
- w_value: bfloat16 [1024, 1024], P(None, 'enc'), may hold values from -0.1875 to 0.1875
- w_attn_out: bfloat16 [1024, 1024], P('enc'), may hold values from -0.1875 to 0.1875
- ln2_gain: float32 [1024], replicated, may hold values from 0.5 to 1.5
- w_glu_value: bfloat16 [1024, 1024], P(None, 'enc'), may hold values from -0.1875 to 0.1875
- w_glu_gate: bfloat16 [1024, 1024], P(None, 'enc'), may hold values from -0.1875 to 0.1875
- depth_kernel: float32 [9, 1024], P(None, 'enc'), may hold values from -2 to 2
- norm_scale: float32 [1024], P('enc'), may hold values from 0.1 to 1.9
- norm_shift: float32 [1024], P('enc'), may hold values from -3 to 3
- w_conv_out: bfloat16 [1024, 1024], P('enc'), may hold values from -0.1875 to 0.1875
Outputs:
- encoded: bfloat16 [4096, 7, 1024], P('front', None, 'enc')
- key_out: bfloat16 [4096, 70, 1024], P('front', None, 'enc')
- value_out: bfloat16 [4096, 70, 1024], P('front', None, 'enc')
- conv_out: bfloat16 [4096, 8, 1024], P('front', None, 'enc')
The draws below stay inside these ranges and needn't reach their ends.
Inputs may be any that keep to these rules, and one draw needn't show every extreme that they name: `new_slot`: A permutation of the stream slots. Device f of front holds old slots and new slots f * 128 to (f + 1) * 128 - 1; a stream that stays on its device keeps its slot; each device hands at most 2 streams to any other device, to at most 16 other devices, and receives as many streams as it hands away. `old_slot`: the inverse permutation of new_slot.
All inputs are finite; a program needn't handle non-finite values.
Results may differ from the reference program's by a relative error of at most 0.0095.
Values may be sent and summed in bfloat16 or wider, within the bound.
No kernel may reach another device: no remote copies, remote signals or barrier semaphores. Data moves between devices by JAX's collectives and lax.ppermute only.
A program may use at most 128 MiB of HBM per device.

```python
import math
import jax
import jax.numpy as jnp
from jax import lax

D = 1024
HEADS = 8
MELS = 80
KERNEL = 9
SUB = 8
FRAMES = 7
CACHE = 70
CAP = 2
S_DEV = 128
HEAD = 128
MEL_FRAMES = 56
CONV_CACHE = 8
STREAMS = 4096
N_ENC = 4


def slot_tables(key):
    base_key = jax.random.fold_in(key, 1234)
    owners = STREAMS // S_DEV
    rounds = owners // 2
    key_relabel, key_shift, key_count, key_order = jax.random.split(base_key, 4)
    relabel = jax.random.permutation(key_relabel, owners)
    inverse = jnp.argsort(relabel)
    shifts = 1 + jax.random.permutation(key_shift, owners - 1)[:rounds]
    counts = jax.random.randint(key_count, (rounds,), 1, CAP + 1).at[0].set(CAP)
    round_ends = jnp.cumsum(counts)
    orders = jax.vmap(lambda sub_key: jax.random.permutation(sub_key, S_DEV))(jax.random.split(key_order, owners))
    place_index = jnp.arange(S_DEV, dtype=jnp.int32)
    round_of = jnp.sum((place_index[:, None] >= round_ends[None, :]).astype(jnp.int32), axis=1)
    moving = place_index < round_ends[-1]
    round_clip = jnp.minimum(round_of, rounds - 1)
    device_index = jnp.arange(owners, dtype=jnp.int32)
    target = inverse[(relabel[:, None] + shifts[round_clip][None, :]) % owners]
    target = jnp.where(moving[None, :], target, device_index[:, None])
    dest_local = orders[target, jnp.broadcast_to(place_index[None, :], target.shape)]
    dest_slot = target * S_DEV + dest_local
    source_slot = device_index[:, None] * S_DEV + orders
    new_table = jnp.zeros((STREAMS,), jnp.int32).at[source_slot.reshape(-1)].set(dest_slot.reshape(-1).astype(jnp.int32))
    old_table = jnp.zeros((STREAMS,), jnp.int32).at[new_table].set(jnp.arange(STREAMS, dtype=jnp.int32))
    return (new_table, old_table)


def draw_new_slot(key, part):
    return slot_tables(key)[0]


def draw_old_slot(key, part):
    return slot_tables(key)[1]


def draw_key_cache(key, part):
    key_base = jax.random.fold_in(jax.random.fold_in(key, 99), 0)
    drawn = jnp.clip(jax.random.normal(key_base, (STREAMS, CACHE, D), jnp.float32), -6.0, 6.0)
    return drawn.astype(jnp.bfloat16)


def touch_ends(entries, stream_key, smallest, top_value):
    longest = entries.shape.index(max(entries.shape))
    spots = []
    for shift in (0, 1):
        where = [jax.random.randint(jax.random.fold_in(stream_key, axis), (), 0, length) for axis, length in enumerate(entries.shape)]
        where[longest] = (where[longest] + shift) % entries.shape[longest]
        spots.append(tuple(where))
    return entries.at[spots[0]].set(smallest).at[spots[1]].set(top_value)


def level_of(own_key, dims, shards, least, largest):
    def one(axis_at, shards_of):
        heights = jax.random.uniform(jax.random.fold_in(jax.random.fold_in(own_key, 6), axis_at), (shards_of,), jnp.float32, least / len(shards), largest / len(shards))
        return jnp.repeat(jnp.exp(heights), dims[axis_at] // shards_of).reshape((-1,) + (1,) * (len(dims) - axis_at - 1))

    gain = one(*shards[0])
    for cut in shards[1:]:
        gain = gain * one(*cut)
    return gain


def bell_draw(own_key, extent, deviation, limit, cuts=(), kind=jnp.bfloat16):
    level = level_of(own_key, extent, cuts, -0.22, 0.18) if cuts else 1.0
    entries = jax.random.normal(own_key, extent, jnp.float32) * deviation * level
    return jnp.minimum(jnp.maximum(entries, -limit), limit).astype(kind)


def setup_inputs(seed: int = 0) -> dict:
    arg_keys = jax.random.split(jax.random.key(seed), 23)
    return {
        "spectra": bell_draw(arg_keys[0], (STREAMS, MEL_FRAMES, MELS), 1.0, 6.0, ((0, 32),)),
        "sub_weight": bell_draw(arg_keys[1], (SUB * MELS, D), (SUB * MELS) ** -0.5, 0.25, ((1, 4),)),
        "sub_bias": bell_draw(arg_keys[2], (D,), 1.0, 4.0, ((0, 4),)),
        "key_cache": draw_key_cache(jax.random.fold_in(arg_keys[22], 71), 0),
        "value_cache": bell_draw(arg_keys[4], (STREAMS, CACHE, D), 1.0, 6.0, ((0, 32), (2, 4))),
        "conv_cache": bell_draw(arg_keys[5], (STREAMS, CONV_CACHE, D), 1.0, 6.0, ((0, 32), (2, 4))),
        "new_slot": draw_new_slot(jax.random.fold_in(arg_keys[22], 71), 0),
        "old_slot": draw_old_slot(jax.random.fold_in(arg_keys[22], 71), 0),
        "valid_new": touch_ends(jax.random.randint(arg_keys[8], (STREAMS,), 1, FRAMES + 1), jax.random.fold_in(arg_keys[8], 1), 1, FRAMES).astype(jnp.int32),
        "cache_fill": touch_ends(jax.random.randint(arg_keys[9], (STREAMS,), 0, CACHE + 1), jax.random.fold_in(arg_keys[9], 1), 0, CACHE).astype(jnp.int32),
        "ln1_gain": jnp.clip(1.0 + 0.1 * jax.random.normal(arg_keys[10], (D,), jnp.float32), 0.5, 1.5),
        "w_query": bell_draw(arg_keys[11], (D, D), D ** -0.5, 0.1875, ((1, 4),)),
        "w_key": bell_draw(arg_keys[12], (D, D), D ** -0.5, 0.1875, ((1, 4),)),
        "w_value": bell_draw(arg_keys[13], (D, D), D ** -0.5, 0.1875, ((1, 4),)),
        "w_attn_out": bell_draw(arg_keys[14], (D, D), D ** -0.5, 0.1875, ((0, 4),)),
        "ln2_gain": jnp.clip(1.0 + 0.1 * jax.random.normal(arg_keys[15], (D,), jnp.float32), 0.5, 1.5),
        "w_glu_value": bell_draw(arg_keys[16], (D, D), D ** -0.5, 0.1875, ((1, 4),)),
        "w_glu_gate": bell_draw(arg_keys[17], (D, D), D ** -0.5, 0.1875, ((1, 4),)),
        "depth_kernel": bell_draw(arg_keys[18], (KERNEL, D), KERNEL ** -0.5, 2.0, ((1, 4),), jnp.float32),
        "norm_scale": jnp.clip(1.0 + 0.18 * jax.random.normal(arg_keys[19], (D,), jnp.float32), 0.1, 1.9),
        "norm_shift": bell_draw(arg_keys[20], (D,), 0.5, 3.0, ((0, 4),), jnp.float32),
        "w_conv_out": bell_draw(arg_keys[21], (D, D), D ** -0.5, 0.1875, ((0, 4),)),
    }


masked_score = -1e+30

def layer_norm(values_in, scale_gain):
    average = lax.optimization_barrier(jnp.mean(values_in, axis=-1, keepdims=True))
    centered = values_in - average
    spread = lax.optimization_barrier(jnp.mean(centered * centered, axis=-1, keepdims=True))
    return centered * lax.rsqrt(spread + 1e-05) * scale_gain

def grouped_sum(operand, matrix):
    slice_width = operand.shape[1] // N_ENC
    summed = jnp.zeros((operand.shape[0], matrix.shape[1]), jnp.float32)
    for member in range(N_ENC):
        portion = jnp.dot(operand[:, member * slice_width:(member + 1) * slice_width], matrix[member * slice_width:(member + 1) * slice_width], preferred_element_type=jnp.float32)
        rounded = lax.optimization_barrier(portion.astype(jnp.bfloat16))
        summed = summed + rounded.astype(jnp.float32)
    return summed

def trim_rows(block_all, offsets, length):
    return jax.vmap(lambda block_rows, offset_rows: lax.dynamic_slice_in_dim(block_rows, offset_rows, length, 0))(block_all, offsets)

def reference(spectra, sub_weight, sub_bias, key_cache, value_cache, conv_cache, new_slot, old_slot, valid_new, cache_fill, ln1_gain, w_query, w_key, w_value, w_attn_out, ln2_gain, w_glu_value, w_glu_gate, depth_kernel, norm_scale, norm_shift, w_conv_out):
    streams = spectra.shape[0]
    stacked = spectra.reshape(streams * FRAMES, SUB * MELS)
    subsampled = (jnp.dot(stacked, sub_weight, preferred_element_type=jnp.float32) + sub_bias.astype(jnp.float32)).astype(jnp.bfloat16)
    subsampled = subsampled.reshape(streams, FRAMES, D)
    inputs = jnp.take(subsampled, old_slot, axis=0)
    keys_old = jnp.zeros_like(key_cache).at[new_slot].set(key_cache)
    values_old = jnp.zeros_like(value_cache).at[new_slot].set(value_cache)
    conv_old = jnp.zeros_like(conv_cache).at[new_slot].set(conv_cache)
    flat_in = inputs.reshape(streams * FRAMES, D)
    normed = layer_norm(flat_in.astype(jnp.float32), ln1_gain).astype(jnp.bfloat16)
    queries = jnp.dot(normed, w_query, preferred_element_type=jnp.float32).astype(jnp.bfloat16).reshape(streams, FRAMES, HEADS, HEAD)
    key_new = jnp.dot(normed, w_key, preferred_element_type=jnp.float32).astype(jnp.bfloat16).reshape(streams, FRAMES, HEADS, HEAD)
    value_new = jnp.dot(normed, w_value, preferred_element_type=jnp.float32).astype(jnp.bfloat16).reshape(streams, FRAMES, HEADS, HEAD)
    keys_all = jnp.concatenate([keys_old.reshape(streams, CACHE, HEADS, HEAD), key_new], axis=1)
    values_all = jnp.concatenate([values_old.reshape(streams, CACHE, HEADS, HEAD), value_new], axis=1)
    scores = jnp.einsum('sthd,sjhd->shtj', queries.astype(jnp.float32), keys_all.astype(jnp.float32)) / math.sqrt(HEAD)
    position = jnp.arange(CACHE + FRAMES, dtype=jnp.int32)[None, :]
    cache_ok = (position < CACHE) & (position >= CACHE - cache_fill[:, None])
    new_ok = (position >= CACHE) & (position - CACHE < valid_new[:, None])
    allowed = (cache_ok | new_ok)[:, None, None, :]
    scores = jnp.where(allowed, scores, masked_score)
    row_peak = lax.optimization_barrier(jnp.max(scores, axis=-1, keepdims=True))
    exponent = jnp.where(allowed, jnp.exp(scores - row_peak), 0.0)
    weights = (exponent / lax.optimization_barrier(jnp.sum(exponent, axis=-1, keepdims=True))).astype(jnp.bfloat16)
    context = jnp.einsum('shtj,sjhd->sthd', weights.astype(jnp.float32), values_all.astype(jnp.float32)).astype(jnp.bfloat16)
    context = context.reshape(streams * FRAMES, D)
    attended = grouped_sum(context, w_attn_out)
    middle = (flat_in.astype(jnp.float32) + attended).astype(jnp.bfloat16)
    normed_second = layer_norm(middle.astype(jnp.float32), ln2_gain).astype(jnp.bfloat16)
    glu_value = jnp.dot(normed_second, w_glu_value, preferred_element_type=jnp.float32)
    glu_gate = jnp.dot(normed_second, w_glu_gate, preferred_element_type=jnp.float32)
    gated = (glu_value * jax.nn.sigmoid(glu_gate)).astype(jnp.bfloat16).reshape(streams, FRAMES, D)
    conv_in = jnp.concatenate([conv_old, gated], axis=1)
    depthwise = jnp.zeros((streams, FRAMES, D), jnp.float32)
    for kernel_tap in range(KERNEL):
        depthwise = depthwise + depth_kernel[kernel_tap] * conv_in[:, kernel_tap:kernel_tap + FRAMES].astype(jnp.float32)
    shaped = depthwise * norm_scale + norm_shift
    activated = (shaped * jax.nn.sigmoid(shaped)).astype(jnp.bfloat16).reshape(streams * FRAMES, D)
    conv_term = grouped_sum(activated, w_conv_out)
    frame_ok = (jnp.arange(FRAMES, dtype=jnp.int32)[None, :] < valid_new[:, None]).astype(jnp.float32)
    encoded = ((middle.astype(jnp.float32) + conv_term).reshape(streams, FRAMES, D) * frame_ok[:, :, None]).astype(jnp.bfloat16)
    key_out = trim_rows(keys_all.reshape(streams, CACHE + FRAMES, D), valid_new, CACHE)
    value_out = trim_rows(values_all.reshape(streams, CACHE + FRAMES, D), valid_new, CACHE)
    conv_out = trim_rows(conv_in, valid_new, CONV_CACHE)
    return (encoded, key_out, value_out, conv_out)
```

```python
import math

import jax
import jax.numpy as jnp
from jax import lax
from jax.experimental import pallas as pl
from jax.experimental.pallas import tpu as pltpu
from jax.sharding import PartitionSpec as P

MELS = 80
KERNEL = 9
SUB = 8
FRAMES = 7
CACHE = 70
CAP = 2
HEAD = 128
CONV_CACHE = 8
LANES = 128
BLOCK = 16
SPAN = 80
KEEP = 72
SLAB = 8
CHUNK = 10

masked_score = -1e30


def layer_norm(values_in, scale_gain):
    average = jnp.mean(values_in, axis=-1, keepdims=True)
    centered = values_in - average
    spread = jnp.mean(centered * centered, axis=-1, keepdims=True)
    return centered * lax.rsqrt(spread + 1e-05) * scale_gain


def send_slots(new_slot, own_index, peer_count):
    stream_count = new_slot.shape[0]
    target = new_slot // stream_count
    leaving = target != own_index
    order = jnp.arange(stream_count, dtype=jnp.int32)
    earlier = (target[None, :] == target[:, None]) & (order[None, :] < order[:, None])
    position = jnp.sum(earlier.astype(jnp.int32), axis=1)
    return jnp.where(leaving, target * CAP + position, peer_count * CAP)


def arrival_slots(old_slot, own_index):
    stream_count = old_slot.shape[0]
    source = old_slot // stream_count
    staying = source == own_index
    earlier = (source[None, :] == source[:, None]) & (old_slot[None, :] < old_slot[:, None])
    position = jnp.sum(earlier.astype(jnp.int32), axis=1)
    return jnp.where(staying, -1, source * CAP + position)


def shift_rows(rows, first, second, third):
    rows = jnp.where(first, rows[1:], rows[:-1])
    rows = jnp.where(second, rows[2:], rows[:-2])
    return jnp.where(third, rows[4:], rows[:-4])


def attend_body(
    valid_s,
    fill_s,
    slot_s,
    query_ref,
    key_new_ref,
    value_new_ref,
    key_ref,
    value_ref,
    valid_ref,
    context_ref,
    key_out_ref,
    value_out_ref,
    send_ref,
    key_f,
    value_f,
    query_f,
    context_f,
):
    base = pl.program_id(0) * BLOCK
    heads = key_f.shape[0]
    slots = send_ref.shape[0]
    shift = valid_ref[...] - 1
    first = ((shift & 1) != 0)[None]
    second = ((shift & 2) != 0)[None]
    third = ((shift & 4) != 0)[None]
    for h in range(heads):
        lanes = slice(h * LANES, (h + 1) * LANES)
        for old_ref, new_ref, dst in (
            (key_ref, key_new_ref, key_f),
            (value_ref, value_new_ref, value_f),
        ):
            for start in range(0, CACHE, CHUNK):
                dst[h, start * BLOCK : (start + CHUNK) * BLOCK, :] = (
                    old_ref[start : start + CHUNK, :, lanes]
                    .astype(jnp.float32)
                    .reshape(CHUNK * BLOCK, LANES)
                )
            dst[h, CACHE * BLOCK : (CACHE + FRAMES) * BLOCK, :] = (
                new_ref[:, :, lanes].astype(jnp.float32).reshape(FRAMES * BLOCK, LANES)
            )
            dst[h, (CACHE + FRAMES) * BLOCK :, :] = jnp.zeros(
                ((SPAN - CACHE - FRAMES) * BLOCK, LANES), jnp.float32
            )
        query_f[h, : FRAMES * BLOCK, :] = (
            query_ref[:, :, lanes].astype(jnp.float32).reshape(FRAMES * BLOCK, LANES)
        )
        query_f[h, FRAMES * BLOCK :, :] = jnp.zeros(((SLAB - FRAMES) * BLOCK, LANES), jnp.float32)
    place = lax.broadcasted_iota(jnp.int32, (SLAB, SPAN), 1)
    for s in range(BLOCK):
        fill = fill_s[base + s]
        valid = valid_s[base + s]
        allowed = (place >= CACHE - fill) & (place < CACHE + valid)
        for h in range(heads):
            keys = key_f[h, pl.ds(s, SPAN, stride=BLOCK), :].astype(jnp.bfloat16)
            query = query_f[h, pl.ds(s, SLAB, stride=BLOCK), :].astype(jnp.bfloat16)
            scores = lax.dot_general(
                query, keys, (((1,), (1,)), ((), ())), preferred_element_type=jnp.float32
            ) * (1.0 / math.sqrt(HEAD))
            scores = jnp.where(allowed, scores, masked_score)
            peak = jnp.max(scores, axis=1, keepdims=True)
            exponent = jnp.where(allowed, jnp.exp(scores - peak), 0.0)
            weights = (exponent / jnp.sum(exponent, axis=1, keepdims=True)).astype(jnp.bfloat16)
            values = value_f[h, pl.ds(s, SPAN, stride=BLOCK), :].astype(jnp.bfloat16)
            context_f[h, pl.ds(s, SLAB, stride=BLOCK), :] = lax.dot_general(
                weights, values, (((1,), (0,)), ((), ())), preferred_element_type=jnp.float32
            )
    for h in range(heads):
        lanes = slice(h * LANES, (h + 1) * LANES)
        context_ref[:, :, lanes] = (
            context_f[h, : FRAMES * BLOCK, :]
            .reshape(FRAMES, BLOCK, LANES)
            .astype(jnp.bfloat16)
        )
        for src, out_ref in ((key_f, key_out_ref), (value_f, value_out_ref)):
            for start in range(0, CACHE, CHUNK):
                rows = src[h, (start + 1) * BLOCK : (start + CHUNK + 8) * BLOCK, :]
                rows = rows.reshape(CHUNK + 7, BLOCK, LANES)
                out_ref[start : start + CHUNK, :, lanes] = shift_rows(
                    rows, first, second, third
                ).astype(jnp.bfloat16)

    def pack(s, carry):
        slot = slot_s[base + s]
        valid = valid_s[base + s]

        @pl.when(slot < slots)
        def _():
            for kind, src in enumerate((key_f, value_f)):
                for h in range(heads):
                    send_ref[slot, kind, :, h * LANES : (h + 1) * LANES] = src[
                        h, pl.ds(valid * BLOCK + s, KEEP, stride=BLOCK), :
                    ].astype(jnp.bfloat16)

        return carry

    lax.fori_loop(0, BLOCK, pack, 0)


def attend(valid_old, fill_old, bucket, queries, key_new, value_new, key_cache, value_cache, slots):
    stream_count = key_cache.shape[1]
    width = key_cache.shape[2]
    heads = width // HEAD
    wide_valid = jnp.broadcast_to(valid_old[:, None], (stream_count, LANES))

    def block(rows):
        return pl.BlockSpec((rows, BLOCK, width), lambda i, *_: (0, i, 0))

    return pl.pallas_call(
        attend_body,
        grid_spec=pltpu.PrefetchScalarGridSpec(
            num_scalar_prefetch=3,
            grid=(stream_count // BLOCK,),
            in_specs=[
                block(FRAMES),
                block(FRAMES),
                block(FRAMES),
                block(CACHE),
                block(CACHE),
                pl.BlockSpec((BLOCK, LANES), lambda i, *_: (i, 0)),
            ],
            out_specs=[
                block(FRAMES),
                block(CACHE),
                block(CACHE),
                pl.BlockSpec((slots, 2, KEEP, width), lambda i, *_: (0, 0, 0, 0)),
            ],
            scratch_shapes=[
                pltpu.VMEM((heads, SPAN * BLOCK, LANES), jnp.float32),
                pltpu.VMEM((heads, SPAN * BLOCK, LANES), jnp.float32),
                pltpu.VMEM((heads, SLAB * BLOCK, LANES), jnp.float32),
                pltpu.VMEM((heads, SLAB * BLOCK, LANES), jnp.float32),
            ],
        ),
        out_shape=[
            jax.ShapeDtypeStruct((FRAMES, stream_count, width), jnp.bfloat16),
            jax.ShapeDtypeStruct((CACHE, stream_count, width), jnp.bfloat16),
            jax.ShapeDtypeStruct((CACHE, stream_count, width), jnp.bfloat16),
            jax.ShapeDtypeStruct((slots, 2, KEEP, width), jnp.bfloat16),
        ],
        name="attend",
    )(
        valid_old,
        fill_old,
        bucket,
        queries,
        key_new,
        value_new,
        key_cache,
        value_cache,
        wide_valid,
    )


def place_body(arrival_s, got_ref, key_ref, value_ref, key_out_ref, value_out_ref, rows_f):
    base = pl.program_id(0) * BLOCK
    heads = rows_f.shape[1]
    for kind, src in enumerate((key_ref, value_ref)):
        for h in range(heads):
            lanes = slice(h * LANES, (h + 1) * LANES)
            for start in range(0, CACHE, CHUNK):
                rows_f[kind, h, start * BLOCK : (start + CHUNK) * BLOCK, :] = (
                    src[start : start + CHUNK, :, lanes]
                    .astype(jnp.float32)
                    .reshape(CHUNK * BLOCK, LANES)
                )

    def fetch(s, carry):
        slot = arrival_s[base + s]

        @pl.when(slot >= 0)
        def _():
            for kind in range(2):
                for h in range(heads):
                    rows_f[kind, h, pl.ds(s, KEEP, stride=BLOCK), :] = got_ref[
                        slot, kind, :, h * LANES : (h + 1) * LANES
                    ].astype(jnp.float32)

        return carry

    lax.fori_loop(0, BLOCK, fetch, 0)
    for kind, dst in enumerate((key_out_ref, value_out_ref)):
        for h in range(heads):
            lanes = slice(h * LANES, (h + 1) * LANES)
            for start in range(0, CACHE, CHUNK):
                dst[start : start + CHUNK, :, lanes] = (
                    rows_f[kind, h, start * BLOCK : (start + CHUNK) * BLOCK, :]
                    .reshape(CHUNK, BLOCK, LANES)
                    .astype(jnp.bfloat16)
                )


def place(arrival, received, key_rows, value_rows):
    stream_count = key_rows.shape[1]
    width = key_rows.shape[2]
    heads = width // HEAD
    slots = received.shape[0]
    block = pl.BlockSpec((CACHE, BLOCK, width), lambda i, *_: (0, i, 0))
    shape = jax.ShapeDtypeStruct((CACHE, stream_count, width), jnp.bfloat16)
    return pl.pallas_call(
        place_body,
        grid_spec=pltpu.PrefetchScalarGridSpec(
            num_scalar_prefetch=1,
            grid=(stream_count // BLOCK,),
            in_specs=[
                pl.BlockSpec((slots, 2, KEEP, width), lambda i, *_: (0, 0, 0, 0)),
                block,
                block,
            ],
            out_specs=[block, block],
            scratch_shapes=[pltpu.VMEM((2, heads, KEEP * BLOCK, LANES), jnp.float32)],
        ),
        out_shape=[shape, shape],
        name="place",
    )(arrival, received, key_rows, value_rows)


def on_device(
    spectra,
    sub_weight,
    sub_bias,
    key_cache,
    value_cache,
    conv_cache,
    new_slot,
    old_slot,
    valid_new,
    cache_fill,
    ln1_gain,
    w_query,
    w_key,
    w_value,
    w_attn_out,
    ln2_gain,
    w_glu_value,
    w_glu_gate,
    depth_kernel,
    norm_scale,
    norm_shift,
    w_conv_out,
):
    peer_count = lax.axis_size("front")
    own_index = lax.axis_index("front")
    member = lax.axis_index("enc")
    stream_count = spectra.shape[0]
    local_width = w_query.shape[1]
    slots = peer_count * CAP
    bucket = send_slots(new_slot, own_index, peer_count)
    arrival = arrival_slots(old_slot, own_index)
    both = lax.all_gather(valid_new * 128 + cache_fill, "front", axis=0, tiled=True)
    both_old = jnp.take(both, new_slot, axis=0)
    valid_old = both_old // 128
    fill_old = both_old % 128

    with_bias = jnp.concatenate(
        [sub_weight, jnp.broadcast_to(sub_bias[None, :], (16, local_width))], axis=0
    )
    with_bias = lax.all_gather(with_bias, "enc", axis=1, tiled=True)
    model_width = with_bias.shape[1]
    taps = SUB * MELS
    stacked = spectra.transpose(1, 2, 0).reshape(FRAMES, taps, stream_count)
    inputs = (
        jnp.einsum("tks,kc->tsc", stacked, with_bias[:taps], preferred_element_type=jnp.float32)
        + with_bias[taps].astype(jnp.float32)
    ).astype(jnp.bfloat16)
    flat_in = inputs.reshape(FRAMES * stream_count, model_width)
    normed = layer_norm(flat_in.astype(jnp.float32), ln1_gain).astype(jnp.bfloat16)

    def project(matrix):
        return (
            jnp.dot(normed, matrix, preferred_element_type=jnp.float32)
            .astype(jnp.bfloat16)
            .reshape(FRAMES, stream_count, local_width)
        )

    context, key_rows, value_rows, leaving_rows = attend(
        valid_old,
        fill_old,
        bucket,
        project(w_query),
        project(w_key),
        project(w_value),
        key_cache.transpose(1, 0, 2),
        value_cache.transpose(1, 0, 2),
        slots,
    )
    received = lax.all_to_all(leaving_rows, "front", split_axis=0, concat_axis=0, tiled=True)
    partial_out = jnp.dot(
        context.reshape(FRAMES * stream_count, local_width),
        w_attn_out,
        preferred_element_type=jnp.float32,
    )
    attended = lax.psum_scatter(
        partial_out.astype(jnp.bfloat16), "enc", scatter_dimension=1, tiled=True
    ).astype(jnp.float32)
    own_inputs = lax.dynamic_slice_in_dim(flat_in, member * local_width, local_width, 1)
    middle_slice = (own_inputs.astype(jnp.float32) + attended).astype(jnp.bfloat16)
    middle = lax.all_gather(middle_slice, "enc", axis=1, tiled=True)
    normed_second = layer_norm(middle.astype(jnp.float32), ln2_gain).astype(jnp.bfloat16)
    glu_value = jnp.dot(normed_second, w_glu_value, preferred_element_type=jnp.float32)
    glu_gate = jnp.dot(normed_second, w_glu_gate, preferred_element_type=jnp.float32)
    gated = (
        (glu_value * jax.nn.sigmoid(glu_gate))
        .astype(jnp.bfloat16)
        .reshape(FRAMES, stream_count, local_width)
    )
    conv_in = jnp.concatenate([conv_cache.transpose(1, 0, 2), gated], axis=0)
    depthwise = jnp.zeros((FRAMES, stream_count, local_width), jnp.float32)
    for kernel_tap in range(KERNEL):
        depthwise = depthwise + depth_kernel[kernel_tap] * conv_in[
            kernel_tap : kernel_tap + FRAMES
        ].astype(jnp.float32)
    shaped = depthwise * norm_scale + norm_shift
    activated = (
        (shaped * jax.nn.sigmoid(shaped))
        .astype(jnp.bfloat16)
        .reshape(FRAMES * stream_count, local_width)
    )
    conv_term = lax.psum_scatter(
        jnp.dot(activated, w_conv_out, preferred_element_type=jnp.float32).astype(jnp.bfloat16),
        "enc",
        scatter_dimension=1,
        tiled=True,
    ).astype(jnp.float32)
    frame_ok = jnp.arange(FRAMES, dtype=jnp.int32)[:, None] < valid_old[None, :]
    encoded = jnp.where(
        frame_ok[:, :, None],
        (middle_slice.astype(jnp.float32) + conv_term).reshape(
            FRAMES, stream_count, local_width
        ),
        0.0,
    ).astype(jnp.bfloat16)
    shift = (valid_old - 1)[None, :, None]
    conv_out = shift_rows(conv_in[1:], (shift & 1) != 0, (shift & 2) != 0, (shift & 4) != 0)
    conv_out = jnp.concatenate(
        [
            conv_out,
            jnp.where(shift == 6, conv_in[14:15], jnp.where(shift == 5, conv_in[13:14],
            jnp.where(shift == 4, conv_in[12:13], jnp.where(shift == 3, conv_in[11:12],
            jnp.where(shift == 2, conv_in[10:11], jnp.where(shift == 1, conv_in[9:10],
            conv_in[8:9]))))))
        ],
        axis=0,
    )
    finished = jnp.concatenate([encoded, conv_out], axis=0)
    picker = (
        bucket[None, :] == jnp.arange(slots, dtype=jnp.int32)[:, None]
    ).astype(jnp.bfloat16)
    leaving_end = jnp.einsum(
        "ls,tsc->ltc", picker, finished, preferred_element_type=jnp.float32
    ).astype(jnp.bfloat16)
    received_end = lax.all_to_all(leaving_end, "front", split_axis=0, concat_axis=0, tiled=True)
    placer = (
        arrival[:, None] == jnp.arange(slots, dtype=jnp.int32)[None, :]
    ).astype(jnp.bfloat16)
    placed = jnp.einsum(
        "sl,ltc->tsc", placer, received_end, preferred_element_type=jnp.float32
    ).astype(jnp.bfloat16)
    finished = jnp.where((arrival < 0)[None, :, None], finished, placed)
    key_done, value_done = place(arrival, received, key_rows, value_rows)
    return (
        finished[:FRAMES].transpose(1, 0, 2),
        key_done.transpose(1, 0, 2),
        value_done.transpose(1, 0, 2),
        finished[FRAMES:].transpose(1, 0, 2),
    )


def solution(mesh):
    in_specs = (
        P("front", None, None),
        P(None, "enc"),
        P("enc"),
        P("front", None, "enc"),
        P("front", None, "enc"),
        P("front", None, "enc"),
        P("front"),
        P("front"),
        P("front"),
        P("front"),
        P(),
        P(None, "enc"),
        P(None, "enc"),
        P(None, "enc"),
        P("enc", None),
        P(),
        P(None, "enc"),
        P(None, "enc"),
        P(None, "enc"),
        P("enc"),
        P("enc"),
        P("enc", None),
    )
    out_specs = (
        P("front", None, "enc"),
        P("front", None, "enc"),
        P("front", None, "enc"),
        P("front", None, "enc"),
    )
    return jax.shard_map(
        on_device, mesh=mesh, in_specs=in_specs, out_specs=out_specs, check_vma=False
    )
```

```python
import math

import jax
import jax.numpy as jnp
from jax import lax
from jax.experimental import pallas as pl
from jax.experimental.pallas import tpu as pltpu
from jax.sharding import PartitionSpec as P


MELS = 80
KERNEL = 9
SUB = 8
FRAMES = 7
CACHE = 70
CAP = 2
HEAD = 128
LANES = 128
BLOCK = 16
SPAN = 80
KEEP = 72
CHUNK = 10

masked_score = -1e30


def layer_norm(values_in, scale_gain):
    average = jnp.mean(values_in, axis=-1, keepdims=True)
    centered = values_in - average
    spread = jnp.mean(centered * centered, axis=-1, keepdims=True)
    return centered * lax.rsqrt(spread + 1e-05) * scale_gain


def send_slots(new_slot, own_index, peer_count):
    stream_count = new_slot.shape[0]
    target = new_slot // stream_count
    leaving = target != own_index
    order = jnp.arange(stream_count, dtype=jnp.int32)
    earlier = (target[None, :] == target[:, None]) & (order[None, :] < order[:, None])
    position = jnp.sum(earlier.astype(jnp.int32), axis=1)
    return jnp.where(leaving, target * CAP + position, peer_count * CAP)


def arrival_slots(old_slot, own_index):
    stream_count = old_slot.shape[0]
    source = old_slot // stream_count
    staying = source == own_index
    earlier = (source[None, :] == source[:, None]) & (old_slot[None, :] < old_slot[:, None])
    position = jnp.sum(earlier.astype(jnp.int32), axis=1)
    return jnp.where(staying, -1, source * CAP + position)


def shift_rows(rows, first, second, third):
    rows = jnp.where(first, rows[1:], rows[:-1])
    rows = jnp.where(second, rows[2:], rows[:-2])
    return jnp.where(third, rows[4:], rows[:-4])


def attend_body(
    slot_s,
    query_ref,
    key_new_ref,
    value_new_ref,
    key_ref,
    value_ref,
    valid_ref,
    fill_ref,
    context_ref,
    key_out_ref,
    value_out_ref,
    send_ref,
    rows_f,
):
    base = pl.program_id(0) * BLOCK
    width = query_ref.shape[2]
    heads = width // LANES
    slots = send_ref.shape[0]
    span = SPAN * BLOCK
    valid = valid_ref[...]
    low = (CACHE - fill_ref[:, :1]) * BLOCK
    high = (CACHE + valid[:, :1]) * BLOCK
    offset = lax.broadcasted_iota(jnp.int32, (BLOCK, span), 1) - lax.broadcasted_iota(
        jnp.int32, (BLOCK, span), 0
    )
    allowed = ((offset & (BLOCK - 1)) == 0) & (offset >= low) & (offset < high)
    bias = jnp.where(allowed, 0.0, masked_score)[None]
    padding = jnp.zeros(((SPAN - CACHE - FRAMES) * BLOCK, LANES), jnp.bfloat16)

    def joined(old_ref, new_ref, lanes):
        return jnp.concatenate(
            [
                old_ref[:, :, lanes].reshape(CACHE * BLOCK, LANES),
                new_ref[:, :, lanes].reshape(FRAMES * BLOCK, LANES),
                padding,
            ],
            axis=0,
        )

    for h in range(heads):
        lanes = slice(h * LANES, (h + 1) * LANES)
        scores = lax.dot_general(
            query_ref[:, :, lanes].reshape(FRAMES * BLOCK, LANES),
            joined(key_ref, key_new_ref, lanes),
            (((1,), (1,)), ((), ())),
            preferred_element_type=jnp.float32,
        )
        scores = scores.reshape(FRAMES, BLOCK, span) * (1.0 / math.sqrt(HEAD)) + bias
        exponent = jnp.exp(scores - jnp.max(scores, axis=2, keepdims=True))
        weights = exponent * (1.0 / jnp.sum(exponent, axis=2, keepdims=True))
        context = lax.dot_general(
            weights.astype(jnp.bfloat16).reshape(FRAMES * BLOCK, span),
            joined(value_ref, value_new_ref, lanes),
            (((1,), (0,)), ((), ())),
            preferred_element_type=jnp.float32,
        )
        context_ref[:, :, lanes] = context.reshape(FRAMES, BLOCK, LANES).astype(jnp.bfloat16)

    shift = valid - 1
    first = ((shift & 1) != 0)[None]
    second = ((shift & 2) != 0)[None]
    third = ((shift & 4) != 0)[None]
    for kind, (old_ref, new_ref, out_ref) in enumerate(
        ((key_ref, key_new_ref, key_out_ref), (value_ref, value_new_ref, value_out_ref))
    ):
        for h in range(heads):
            lanes = slice(h * LANES, (h + 1) * LANES)
            for start in range(0, CACHE, CHUNK):
                stop = start + CHUNK + 8
                rows = old_ref[start + 1 : min(stop, CACHE), :, lanes].astype(jnp.float32)
                if stop > CACHE:
                    extra = new_ref[:, :, lanes].astype(jnp.float32)
                    rows = jnp.concatenate([rows, extra, extra[:1]], axis=0)[: CHUNK + 7]
                rows = shift_rows(rows, first, second, third)
                out_ref[start : start + CHUNK, :, lanes] = rows.astype(jnp.bfloat16)
                rows_f[kind, h, start * BLOCK : (start + CHUNK) * BLOCK, :] = rows.reshape(
                    CHUNK * BLOCK, LANES
                )

    def pack(s, carry):
        slot = slot_s[base + s]

        @pl.when(slot < slots)
        def _():
            for kind in range(2):
                for h in range(heads):
                    send_ref[slot, kind, :, h * LANES : (h + 1) * LANES] = rows_f[
                        kind, h, pl.ds(s, KEEP, stride=BLOCK), :
                    ].astype(jnp.bfloat16)

        return carry

    lax.fori_loop(0, BLOCK, pack, 0)


def attend(valid_old, fill_old, bucket, queries, key_new, value_new, key_cache, value_cache, slots):
    stream_count = key_cache.shape[1]
    width = key_cache.shape[2]
    heads = width // HEAD

    def wide(column):
        return jnp.broadcast_to(column[:, None], (stream_count, LANES))

    def block(rows):
        return pl.BlockSpec((rows, BLOCK, width), lambda i, *_: (0, i, 0))

    scalar = pl.BlockSpec((BLOCK, LANES), lambda i, *_: (i, 0))
    return pl.pallas_call(
        attend_body,
        grid_spec=pltpu.PrefetchScalarGridSpec(
            num_scalar_prefetch=1,
            grid=(stream_count // BLOCK,),
            in_specs=[
                block(FRAMES),
                block(FRAMES),
                block(FRAMES),
                block(CACHE),
                block(CACHE),
                scalar,
                scalar,
            ],
            out_specs=[
                block(FRAMES),
                block(CACHE),
                block(CACHE),
                pl.BlockSpec((slots, 2, KEEP, width), lambda i, *_: (0, 0, 0, 0)),
            ],
            scratch_shapes=[pltpu.VMEM((2, heads, KEEP * BLOCK, LANES), jnp.float32)],
        ),
        out_shape=[
            jax.ShapeDtypeStruct((FRAMES, stream_count, width), jnp.bfloat16),
            jax.ShapeDtypeStruct((CACHE, stream_count, width), jnp.bfloat16),
            jax.ShapeDtypeStruct((CACHE, stream_count, width), jnp.bfloat16),
            jax.ShapeDtypeStruct((slots, 2, KEEP, width), jnp.bfloat16),
        ],
        name="attend",
    )(
        bucket,
        queries,
        key_new,
        value_new,
        key_cache,
        value_cache,
        wide(valid_old),
        wide(fill_old),
    )


def place_body(arrival_s, got_ref, key_ref, value_ref, key_out_ref, value_out_ref, rows_f):
    base = pl.program_id(0) * BLOCK
    heads = rows_f.shape[1]
    for kind, src in enumerate((key_ref, value_ref)):
        for h in range(heads):
            lanes = slice(h * LANES, (h + 1) * LANES)
            for start in range(0, CACHE, CHUNK):
                rows_f[kind, h, start * BLOCK : (start + CHUNK) * BLOCK, :] = (
                    src[start : start + CHUNK, :, lanes]
                    .astype(jnp.float32)
                    .reshape(CHUNK * BLOCK, LANES)
                )

    def fetch(s, carry):
        slot = arrival_s[base + s]

        @pl.when(slot >= 0)
        def _():
            for kind in range(2):
                for h in range(heads):
                    rows_f[kind, h, pl.ds(s, KEEP, stride=BLOCK), :] = got_ref[
                        slot, kind, :, h * LANES : (h + 1) * LANES
                    ].astype(jnp.float32)

        return carry

    lax.fori_loop(0, BLOCK, fetch, 0)
    for kind, dst in enumerate((key_out_ref, value_out_ref)):
        for h in range(heads):
            lanes = slice(h * LANES, (h + 1) * LANES)
            for start in range(0, CACHE, CHUNK):
                dst[start : start + CHUNK, :, lanes] = (
                    rows_f[kind, h, start * BLOCK : (start + CHUNK) * BLOCK, :]
                    .reshape(CHUNK, BLOCK, LANES)
                    .astype(jnp.bfloat16)
                )


def place(arrival, received, key_rows, value_rows):
    stream_count = key_rows.shape[1]
    width = key_rows.shape[2]
    heads = width // HEAD
    slots = received.shape[0]
    block = pl.BlockSpec((CACHE, BLOCK, width), lambda i, *_: (0, i, 0))
    shape = jax.ShapeDtypeStruct((CACHE, stream_count, width), jnp.bfloat16)
    return pl.pallas_call(
        place_body,
        grid_spec=pltpu.PrefetchScalarGridSpec(
            num_scalar_prefetch=1,
            grid=(stream_count // BLOCK,),
            in_specs=[
                pl.BlockSpec((slots, 2, KEEP, width), lambda i, *_: (0, 0, 0, 0)),
                block,
                block,
            ],
            out_specs=[block, block],
            scratch_shapes=[pltpu.VMEM((2, heads, KEEP * BLOCK, LANES), jnp.float32)],
        ),
        out_shape=[shape, shape],
        name="place",
    )(arrival, received, key_rows, value_rows)


def on_device(
    spectra,
    sub_weight,
    sub_bias,
    key_cache,
    value_cache,
    conv_cache,
    new_slot,
    old_slot,
    valid_new,
    cache_fill,
    ln1_gain,
    w_query,
    w_key,
    w_value,
    w_attn_out,
    ln2_gain,
    w_glu_value,
    w_glu_gate,
    depth_kernel,
    norm_scale,
    norm_shift,
    w_conv_out,
):
    peer_count = lax.axis_size("front")
    own_index = lax.axis_index("front")
    member = lax.axis_index("enc")
    stream_count = spectra.shape[0]
    local_width = w_query.shape[1]
    slots = peer_count * CAP
    bucket = send_slots(new_slot, own_index, peer_count)
    arrival = arrival_slots(old_slot, own_index)
    slot_ids = jnp.arange(slots, dtype=jnp.int32)
    both = valid_new * 128 + cache_fill
    asked = jnp.sum(jnp.where(arrival[None, :] == slot_ids[:, None], both[None, :], 0), axis=1)
    told = lax.all_to_all(
        jnp.broadcast_to(asked[:, None], (slots, LANES)),
        "front",
        split_axis=0,
        concat_axis=0,
        tiled=True,
    )[:, 0]
    told = jnp.sum(jnp.where(bucket[:, None] == slot_ids[None, :], told[None, :], 0), axis=1)
    both_old = jnp.where(bucket < slots, told, both)
    valid_old = both_old // 128
    fill_old = both_old % 128

    with_bias = jnp.concatenate(
        [sub_weight, jnp.broadcast_to(sub_bias[None, :], (16, local_width))], axis=0
    )
    with_bias = lax.all_gather(with_bias, "enc", axis=1, tiled=True)
    model_width = with_bias.shape[1]
    taps = SUB * MELS
    stacked = spectra.transpose(1, 2, 0).reshape(FRAMES, taps, stream_count)
    inputs = (
        jnp.einsum("tks,kc->tsc", stacked, with_bias[:taps], preferred_element_type=jnp.float32)
        + with_bias[taps].astype(jnp.float32)
    ).astype(jnp.bfloat16)
    flat_in = inputs.reshape(FRAMES * stream_count, model_width)
    normed = layer_norm(flat_in.astype(jnp.float32), ln1_gain).astype(jnp.bfloat16)

    def project(matrix):
        return (
            jnp.dot(normed, matrix, preferred_element_type=jnp.float32)
            .astype(jnp.bfloat16)
            .reshape(FRAMES, stream_count, local_width)
        )

    context, key_rows, value_rows, leaving_rows = attend(
        valid_old,
        fill_old,
        bucket,
        project(w_query),
        project(w_key),
        project(w_value),
        key_cache.transpose(1, 0, 2),
        value_cache.transpose(1, 0, 2),
        slots,
    )
    received = lax.all_to_all(leaving_rows, "front", split_axis=0, concat_axis=0, tiled=True)
    partial_out = jnp.dot(
        context.reshape(FRAMES * stream_count, local_width),
        w_attn_out,
        preferred_element_type=jnp.float32,
    )
    attended = lax.psum_scatter(
        partial_out.astype(jnp.bfloat16), "enc", scatter_dimension=1, tiled=True
    ).astype(jnp.float32)
    own_inputs = lax.dynamic_slice_in_dim(flat_in, member * local_width, local_width, 1)
    middle_slice = (own_inputs.astype(jnp.float32) + attended).astype(jnp.bfloat16)
    middle = lax.all_gather(middle_slice, "enc", axis=1, tiled=True)
    normed_second = layer_norm(middle.astype(jnp.float32), ln2_gain).astype(jnp.bfloat16)
    glu_value = jnp.dot(normed_second, w_glu_value, preferred_element_type=jnp.float32)
    glu_gate = jnp.dot(normed_second, w_glu_gate, preferred_element_type=jnp.float32)
    gated = (
        (glu_value * jax.nn.sigmoid(glu_gate))
        .astype(jnp.bfloat16)
        .reshape(FRAMES, stream_count, local_width)
    )
    conv_in = jnp.concatenate([conv_cache.transpose(1, 0, 2), gated], axis=0)
    depthwise = jnp.zeros((FRAMES, stream_count, local_width), jnp.float32)
    for kernel_tap in range(KERNEL):
        depthwise = depthwise + depth_kernel[kernel_tap] * conv_in[
            kernel_tap : kernel_tap + FRAMES
        ].astype(jnp.float32)
    shaped = depthwise * norm_scale + norm_shift
    activated = (
        (shaped * jax.nn.sigmoid(shaped))
        .astype(jnp.bfloat16)
        .reshape(FRAMES * stream_count, local_width)
    )
    conv_term = lax.psum_scatter(
        jnp.dot(activated, w_conv_out, preferred_element_type=jnp.float32).astype(jnp.bfloat16),
        "enc",
        scatter_dimension=1,
        tiled=True,
    ).astype(jnp.float32)
    frame_ok = jnp.arange(FRAMES, dtype=jnp.int32)[:, None] < valid_old[None, :]
    encoded = jnp.where(
        frame_ok[:, :, None],
        (middle_slice.astype(jnp.float32) + conv_term).reshape(
            FRAMES, stream_count, local_width
        ),
        0.0,
    ).astype(jnp.bfloat16)
    shift = (valid_old - 1)[None, :, None]
    conv_out = shift_rows(conv_in[1:], (shift & 1) != 0, (shift & 2) != 0, (shift & 4) != 0)
    conv_out = jnp.concatenate(
        [
            conv_out,
            jnp.where(shift == 6, conv_in[14:15], jnp.where(shift == 5, conv_in[13:14],
            jnp.where(shift == 4, conv_in[12:13], jnp.where(shift == 3, conv_in[11:12],
            jnp.where(shift == 2, conv_in[10:11], jnp.where(shift == 1, conv_in[9:10],
            conv_in[8:9]))))))
        ],
        axis=0,
    )
    finished = jnp.concatenate([encoded, conv_out], axis=0)
    picker = (
        bucket[None, :] == jnp.arange(slots, dtype=jnp.int32)[:, None]
    ).astype(jnp.bfloat16)
    leaving_end = jnp.einsum(
        "ls,tsc->ltc", picker, finished, preferred_element_type=jnp.float32
    ).astype(jnp.bfloat16)
    received_end = lax.all_to_all(leaving_end, "front", split_axis=0, concat_axis=0, tiled=True)
    placer = (
        arrival[:, None] == jnp.arange(slots, dtype=jnp.int32)[None, :]
    ).astype(jnp.bfloat16)
    placed = jnp.einsum(
        "sl,ltc->tsc", placer, received_end, preferred_element_type=jnp.float32
    ).astype(jnp.bfloat16)
    finished = jnp.where((arrival < 0)[None, :, None], finished, placed)
    key_done, value_done = place(arrival, received, key_rows, value_rows)
    return (
        finished[:FRAMES].transpose(1, 0, 2),
        key_done.transpose(1, 0, 2),
        value_done.transpose(1, 0, 2),
        finished[FRAMES:].transpose(1, 0, 2),
    )


def solution(mesh):
    in_specs = (
        P("front", None, None),
        P(None, "enc"),
        P("enc"),
        P("front", None, "enc"),
        P("front", None, "enc"),
        P("front", None, "enc"),
        P("front"),
        P("front"),
        P("front"),
        P("front"),
        P(),
        P(None, "enc"),
        P(None, "enc"),
        P(None, "enc"),
        P("enc", None),
        P(),
        P(None, "enc"),
        P(None, "enc"),
        P(None, "enc"),
        P("enc"),
        P("enc"),
        P("enc", None),
    )
    out_specs = (
        P("front", None, "enc"),
        P("front", None, "enc"),
        P("front", None, "enc"),
        P("front", None, "enc"),
    )

    return jax.shard_map(
        on_device, mesh=mesh, in_specs=in_specs, out_specs=out_specs, check_vma=False
    )
```

```python
import math

import jax
import jax.numpy as jnp
from jax import lax
from jax.experimental import pallas as pl
from jax.experimental.pallas import tpu as pltpu
from jax.sharding import PartitionSpec as P


MELS = 80
KERNEL = 9
SUB = 8
FRAMES = 7
CACHE = 70
CAP = 2
HEAD = 128
CONV_CACHE = 8
LANES = 128
BLOCK = 16
SPAN = 80
KEEP = 72
CHUNK = 10

masked_score = -1e30


def send_slots(new_slot, own_index, peer_count):
    stream_count = new_slot.shape[0]
    target = new_slot // stream_count
    leaving = target != own_index
    order = jnp.arange(stream_count, dtype=jnp.int32)
    earlier = (target[None, :] == target[:, None]) & (order[None, :] < order[:, None])
    position = jnp.sum(earlier.astype(jnp.int32), axis=1)
    return jnp.where(leaving, target * CAP + position, peer_count * CAP)


def arrival_slots(old_slot, own_index):
    stream_count = old_slot.shape[0]
    source = old_slot // stream_count
    staying = source == own_index
    earlier = (source[None, :] == source[:, None]) & (old_slot[None, :] < old_slot[:, None])
    position = jnp.sum(earlier.astype(jnp.int32), axis=1)
    return jnp.where(staying, -1, source * CAP + position)


def shift_rows(rows, first, second, third):
    rows = jnp.where(first, rows[1:], rows[:-1])
    rows = jnp.where(second, rows[2:], rows[:-2])
    return jnp.where(third, rows[4:], rows[:-4])


def attend_body(
    slot_s,
    query_ref,
    key_new_ref,
    value_new_ref,
    key_ref,
    value_ref,
    valid_ref,
    fill_ref,
    context_ref,
    key_out_ref,
    value_out_ref,
    send_ref,
    rows_f,
):
    base = pl.program_id(0) * BLOCK
    width = query_ref.shape[2]
    heads = width // LANES
    slots = send_ref.shape[0]
    span = SPAN * BLOCK
    valid = valid_ref[...]
    low = (CACHE - fill_ref[:, :1]) * BLOCK
    high = (CACHE + valid[:, :1]) * BLOCK
    offset = lax.broadcasted_iota(jnp.int32, (BLOCK, span), 1) - lax.broadcasted_iota(
        jnp.int32, (BLOCK, span), 0
    )
    allowed = ((offset & (BLOCK - 1)) == 0) & (offset >= low) & (offset < high)
    bias = jnp.where(allowed, 0.0, masked_score)[None]
    padding = jnp.zeros(((SPAN - CACHE - FRAMES) * BLOCK, LANES), jnp.bfloat16)

    def joined(old_ref, new_ref, lanes):
        return jnp.concatenate(
            [
                old_ref[:, :, lanes].reshape(CACHE * BLOCK, LANES),
                new_ref[:, :, lanes].reshape(FRAMES * BLOCK, LANES),
                padding,
            ],
            axis=0,
        )

    for h in range(heads):
        lanes = slice(h * LANES, (h + 1) * LANES)
        scores = lax.dot_general(
            query_ref[:, :, lanes].reshape(FRAMES * BLOCK, LANES),
            joined(key_ref, key_new_ref, lanes),
            (((1,), (1,)), ((), ())),
            preferred_element_type=jnp.float32,
        )
        scores = scores.reshape(FRAMES, BLOCK, span) * (1.0 / math.sqrt(HEAD)) + bias
        exponent = jnp.exp(scores - jnp.max(scores, axis=2, keepdims=True))
        weights = exponent * (1.0 / jnp.sum(exponent, axis=2, keepdims=True))
        context = lax.dot_general(
            weights.astype(jnp.bfloat16).reshape(FRAMES * BLOCK, span),
            joined(value_ref, value_new_ref, lanes),
            (((1,), (0,)), ((), ())),
            preferred_element_type=jnp.float32,
        )
        context_ref[0, :, :, lanes] = context.reshape(FRAMES, BLOCK, LANES).astype(jnp.bfloat16)

    shift = valid - 1
    first = ((shift & 1) != 0)[None]
    second = ((shift & 2) != 0)[None]
    third = ((shift & 4) != 0)[None]
    for kind, (old_ref, new_ref, out_ref) in enumerate(
        ((key_ref, key_new_ref, key_out_ref), (value_ref, value_new_ref, value_out_ref))
    ):
        for h in range(heads):
            lanes = slice(h * LANES, (h + 1) * LANES)
            for start in range(0, CACHE, CHUNK):
                stop = start + CHUNK + 8
                rows = old_ref[start + 1 : min(stop, CACHE), :, lanes].astype(jnp.float32)
                if stop > CACHE:
                    extra = new_ref[:, :, lanes].astype(jnp.float32)
                    rows = jnp.concatenate([rows, extra, extra[:1]], axis=0)[: CHUNK + 7]
                rows = shift_rows(rows, first, second, third)
                out_ref[start : start + CHUNK, :, lanes] = rows.astype(jnp.bfloat16)
                rows_f[kind, h, start * BLOCK : (start + CHUNK) * BLOCK, :] = rows.reshape(
                    CHUNK * BLOCK, LANES
                )

    def pack(s, carry):
        slot = slot_s[base + s]

        @pl.when(slot < slots)
        def _():
            for kind in range(2):
                for h in range(heads):
                    send_ref[slot, kind, :, h * LANES : (h + 1) * LANES] = rows_f[
                        kind, h, pl.ds(s, KEEP, stride=BLOCK), :
                    ].astype(jnp.bfloat16)

        return carry

    lax.fori_loop(0, BLOCK, pack, 0)


def attend(
    valid_old, fill_old, bucket, queries, key_new, value_new, key_cache, value_cache, slots, groups
):
    stream_count = key_cache.shape[1]
    width = key_cache.shape[2]
    heads = width // HEAD

    def wide(column):
        return jnp.broadcast_to(column[:, None], (stream_count, LANES))

    def block(rows):
        return pl.BlockSpec((rows, BLOCK, width), lambda i, *_: (0, i, 0))

    per_group = stream_count // groups // BLOCK
    scalar = pl.BlockSpec((BLOCK, LANES), lambda i, *_: (i, 0))
    return pl.pallas_call(
        attend_body,
        grid_spec=pltpu.PrefetchScalarGridSpec(
            num_scalar_prefetch=1,
            grid=(stream_count // BLOCK,),
            in_specs=[
                block(FRAMES),
                block(FRAMES),
                block(FRAMES),
                block(CACHE),
                block(CACHE),
                scalar,
                scalar,
            ],
            out_specs=[
                pl.BlockSpec(
                    (1, FRAMES, BLOCK, width), lambda i, *_: (i // per_group, 0, i % per_group, 0)
                ),
                block(CACHE),
                block(CACHE),
                pl.BlockSpec((slots, 2, KEEP, width), lambda i, *_: (0, 0, 0, 0)),
            ],
            scratch_shapes=[pltpu.VMEM((2, heads, KEEP * BLOCK, LANES), jnp.float32)],
        ),
        out_shape=[
            jax.ShapeDtypeStruct((groups, FRAMES, stream_count // groups, width), jnp.bfloat16),
            jax.ShapeDtypeStruct((CACHE, stream_count, width), jnp.bfloat16),
            jax.ShapeDtypeStruct((CACHE, stream_count, width), jnp.bfloat16),
            jax.ShapeDtypeStruct((slots, 2, KEEP, width), jnp.bfloat16),
        ],
        name="attend",
    )(
        bucket,
        queries,
        key_new,
        value_new,
        key_cache,
        value_cache,
        wide(valid_old),
        wide(fill_old),
    )


def place_body(arrival_s, got_ref, key_ref, value_ref, key_out_ref, value_out_ref, rows_f):
    base = pl.program_id(0) * BLOCK
    heads = rows_f.shape[1]
    for kind, src in enumerate((key_ref, value_ref)):
        for h in range(heads):
            lanes = slice(h * LANES, (h + 1) * LANES)
            for start in range(0, CACHE, CHUNK):
                rows_f[kind, h, start * BLOCK : (start + CHUNK) * BLOCK, :] = (
                    src[start : start + CHUNK, :, lanes]
                    .astype(jnp.float32)
                    .reshape(CHUNK * BLOCK, LANES)
                )

    def fetch(s, carry):
        slot = arrival_s[base + s]

        @pl.when(slot >= 0)
        def _():
            for kind in range(2):
                for h in range(heads):
                    rows_f[kind, h, pl.ds(s, KEEP, stride=BLOCK), :] = got_ref[
                        slot, kind, :, h * LANES : (h + 1) * LANES
                    ].astype(jnp.float32)

        return carry

    lax.fori_loop(0, BLOCK, fetch, 0)
    for kind, dst in enumerate((key_out_ref, value_out_ref)):
        for h in range(heads):
            lanes = slice(h * LANES, (h + 1) * LANES)
            for start in range(0, CACHE, CHUNK):
                dst[start : start + CHUNK, :, lanes] = (
                    rows_f[kind, h, start * BLOCK : (start + CHUNK) * BLOCK, :]
                    .reshape(CHUNK, BLOCK, LANES)
                    .astype(jnp.bfloat16)
                )


def place(arrival, received, key_rows, value_rows):
    stream_count = key_rows.shape[1]
    width = key_rows.shape[2]
    heads = width // HEAD
    slots = received.shape[0]
    block = pl.BlockSpec((CACHE, BLOCK, width), lambda i, *_: (0, i, 0))
    shape = jax.ShapeDtypeStruct((CACHE, stream_count, width), jnp.bfloat16)
    return pl.pallas_call(
        place_body,
        grid_spec=pltpu.PrefetchScalarGridSpec(
            num_scalar_prefetch=1,
            grid=(stream_count // BLOCK,),
            in_specs=[
                pl.BlockSpec((slots, 2, KEEP, width), lambda i, *_: (0, 0, 0, 0)),
                block,
                block,
            ],
            out_specs=[block, block],
            scratch_shapes=[pltpu.VMEM((2, heads, KEEP * BLOCK, LANES), jnp.float32)],
        ),
        out_shape=[shape, shape],
        name="place",
    )(arrival, received, key_rows, value_rows)


def head_body(
    place_s, frames_ref, own_ref, near_ref, far_ref, next_ref, gain_ref, *rest
):
    weights, outs, inputs_ref, raw = rest[:3], rest[3:6], rest[6], rest[7]
    member = place_s[0]
    groups = raw.shape[0]
    taps = frames_ref.shape[2]
    width = raw.shape[2]
    frames = frames_ref[0]
    for offset, piece in enumerate((own_ref, near_ref, far_ref, next_ref)):
        total = jnp.dot(frames, piece[:taps, :], preferred_element_type=jnp.float32)
        total = total + piece[taps : taps + 16, :].astype(jnp.float32)[:1]
        raw[(member + groups - offset) % groups] = total.astype(jnp.bfloat16)
    values = [raw[g].astype(jnp.float32) for g in range(groups)]
    model_width = groups * width
    average = sum(jnp.sum(v, axis=1, keepdims=True) for v in values) * (1.0 / model_width)
    values = [v - average for v in values]
    spread = sum(jnp.sum(v * v, axis=1, keepdims=True) for v in values) * (1.0 / model_width)
    scale = lax.rsqrt(spread + 1e-05)
    normed = [
        (v * scale * gain_ref[:, g * width : (g + 1) * width]).astype(jnp.bfloat16)
        for g, v in enumerate(values)
    ]
    normed = jnp.concatenate(normed, axis=1)
    for matrix, out in zip(weights, outs):
        out[0] = jnp.dot(normed, matrix[...], preferred_element_type=jnp.float32).astype(
            jnp.bfloat16
        )
    share = inputs_ref.shape[1]
    for g in range(groups):
        inputs_ref[0, :, g * width : (g + 1) * width] = raw[
            g, pl.ds(pl.multiple_of(member * share, share), share), :
        ]


def head(member, frames, pieces, gain, matrices):
    count, streams, taps = frames.shape
    width = matrices[0].shape[1]
    groups = len(pieces)

    def whole(array):
        return pl.BlockSpec(array.shape, lambda i, *_: (0, 0))

    per_frame = pl.BlockSpec((1, streams, width), lambda i, *_: (i, 0, 0))
    shape = jax.ShapeDtypeStruct((count, streams, width), jnp.bfloat16)
    gain = gain[None, :]
    return pl.pallas_call(
        head_body,
        grid_spec=pltpu.PrefetchScalarGridSpec(
            num_scalar_prefetch=1,
            grid=(count,),
            in_specs=[pl.BlockSpec((1, streams, taps), lambda i, *_: (i, 0, 0))]
            + [whole(p) for p in pieces]
            + [whole(gain)]
            + [whole(w) for w in matrices],
            out_specs=[per_frame, per_frame, per_frame]
            + [pl.BlockSpec((1, streams // groups, groups * width), lambda i, *_: (i, 0, 0))],
            scratch_shapes=[pltpu.VMEM((groups, streams, width), jnp.bfloat16)],
        ),
        out_shape=[shape, shape, shape]
        + [jax.ShapeDtypeStruct((count, streams // groups, groups * width), jnp.bfloat16)],
        name="head",
    )(member[None], frames, *pieces, gain, *matrices)


def tail_body(place_s, *refs):
    contexts, caches, rest = refs[:4], refs[4:8], refs[8:]
    inputs_ref, gain_ref, valid_ref, own_ref, near_ref, far_low, far_high, next_ref = rest[:8]
    smalls, out_ref = rest[8:12], rest[12]
    member = place_s[0]
    groups = len(contexts)
    _, share, width = contexts[0].shape
    rows = FRAMES * share
    size = groups * width
    half = 2 * size
    sources = tuple(
        zip(
            contexts,
            caches,
            (own_ref, near_ref, far_low, next_ref),
            (own_ref, near_ref, far_high, next_ref),
            (half, half, 0, half),
            smalls,
        )
    )

    def grouped(operand, low_ref, start, sums):
        for n in range(groups):
            block = low_ref[start + n * width : start + (n + 1) * width, :]
            part = jnp.dot(operand, block, preferred_element_type=jnp.float32)
            part = part.astype(jnp.bfloat16).astype(jnp.float32)
            sums[n] = part if sums[n] is None else sums[n] + part

    attended = [None] * groups
    for context_ref, _, low_ref, _, _, _ in sources:
        grouped(context_ref[...].reshape(rows, width), low_ref, 0, attended)
    middle = []
    for n in range(groups):
        inputs = inputs_ref[:, :, n * width : (n + 1) * width].reshape(rows, width)
        middle.append((inputs.astype(jnp.float32) + attended[n]).astype(jnp.bfloat16))
    values = [m.astype(jnp.float32) for m in middle]
    average = sum(jnp.sum(v, axis=1, keepdims=True) for v in values) * (1.0 / size)
    values = [v - average for v in values]
    spread = sum(jnp.sum(v * v, axis=1, keepdims=True) for v in values) * (1.0 / size)
    scale = lax.rsqrt(spread + 1e-05)
    normed = jnp.concatenate(
        [
            (v * scale * gain_ref[:, n * width : (n + 1) * width]).astype(jnp.bfloat16)
            for n, v in enumerate(values)
        ],
        axis=1,
    )
    valid = valid_ref[...]
    shift = valid - 1
    first = ((shift & 1) != 0)[None]
    second = ((shift & 2) != 0)[None]
    third = ((shift & 4) != 0)[None]
    conv_term = [None] * groups
    for step, (_, cache_ref, low_ref, high_ref, start, small_ref) in enumerate(sources):
        group = (member + groups - step) % groups
        glu_value = jnp.dot(
            normed, high_ref[start : start + size, :], preferred_element_type=jnp.float32
        )
        glu_gate = jnp.dot(
            normed, high_ref[start + size : start + 2 * size, :], preferred_element_type=jnp.float32
        )
        gated = (glu_value * jax.nn.sigmoid(glu_gate)).astype(jnp.bfloat16)
        conv_in = jnp.concatenate(
            [
                cache_ref[...].astype(jnp.float32),
                gated.astype(jnp.float32).reshape(FRAMES, share, width),
            ],
            axis=0,
        )
        depthwise = jnp.zeros((FRAMES, share, width), jnp.float32)
        for tap in range(KERNEL):
            depthwise = depthwise + small_ref[tap : tap + 1, :][None] * conv_in[tap : tap + FRAMES]
        shaped = depthwise * small_ref[KERNEL : KERNEL + 1, :][None]
        shaped = shaped + small_ref[KERNEL + 1 : KERNEL + 2, :][None]
        activated = (shaped * jax.nn.sigmoid(shaped)).astype(jnp.bfloat16)
        grouped(activated.reshape(rows, width), low_ref, size, conv_term)
        moved = shift_rows(
            jnp.concatenate([conv_in[1:], conv_in[-1:]], axis=0), first, second, third
        )
        out_ref[group, FRAMES:, :, :] = moved.astype(jnp.bfloat16)
    frame = lax.broadcasted_iota(jnp.int32, (FRAMES, share, width), 0)
    for n in range(groups):
        total = (middle[n].astype(jnp.float32) + conv_term[n]).reshape(FRAMES, share, width)
        out_ref[n, :FRAMES, :, :] = jnp.where(frame < valid[None], total, 0.0).astype(jnp.bfloat16)


def tail(member, groups, *arrays):
    _, share, width = arrays[0].shape
    return pl.pallas_call(
        tail_body,
        in_specs=[pl.BlockSpec(memory_space=pltpu.SMEM)]
        + [pl.BlockSpec(memory_space=pltpu.VMEM)] * len(arrays),
        out_specs=pl.BlockSpec(memory_space=pltpu.VMEM),
        out_shape=jax.ShapeDtypeStruct((groups, FRAMES + CONV_CACHE, share, width), jnp.bfloat16),
        name="tail",
    )(member[None], *arrays)


def swap(chunks, member, count):
    pieces = [lax.dynamic_index_in_dim(chunks, member, 0, False)]
    for step in range(1, count):
        chunk = lax.dynamic_index_in_dim(chunks, (member + step) % count, 0, False)
        pieces.append(toward(chunk, step, count))
    return pieces


def toward(array, steps, count):
    return lax.ppermute(array, "enc", [(i, (i + steps) % count) for i in range(count)])


def on_device(
    spectra,
    sub_weight,
    sub_bias,
    key_cache,
    value_cache,
    conv_cache,
    new_slot,
    old_slot,
    valid_new,
    cache_fill,
    ln1_gain,
    w_query,
    w_key,
    w_value,
    w_attn_out,
    ln2_gain,
    w_glu_value,
    w_glu_gate,
    depth_kernel,
    norm_scale,
    norm_shift,
    w_conv_out,
):
    peer_count = lax.axis_size("front")
    own_index = lax.axis_index("front")
    member = lax.axis_index("enc")
    stream_count = spectra.shape[0]
    local_width = w_query.shape[1]
    slots = peer_count * CAP
    bucket = send_slots(new_slot, own_index, peer_count)
    arrival = arrival_slots(old_slot, own_index)
    slot_ids = jnp.arange(slots, dtype=jnp.int32)
    both = valid_new * 128 + cache_fill
    asked = jnp.sum(jnp.where(arrival[None, :] == slot_ids[:, None], both[None, :], 0), axis=1)
    told = lax.all_to_all(
        jnp.broadcast_to(asked[:, None], (slots, LANES)),
        "front",
        split_axis=0,
        concat_axis=0,
        tiled=True,
    )[:, 0]
    told = jnp.sum(jnp.where(bucket[:, None] == slot_ids[None, :], told[None, :], 0), axis=1)
    both_old = jnp.where(bucket < slots, told, both)
    valid_old = both_old // 128
    fill_old = both_old % 128

    groups = lax.axis_size("enc")
    taps = SUB * MELS
    with_bias = jnp.concatenate(
        [sub_weight, jnp.broadcast_to(sub_bias[None, :], (16, local_width))], axis=0
    )
    sub_pieces = [with_bias] + [toward(with_bias, k, groups) for k in range(1, groups)]

    def blocks(matrix):
        return (
            matrix.reshape(local_width, groups, local_width)
            .transpose(1, 0, 2)
            .reshape(groups * local_width, local_width)
        )

    stack = jnp.concatenate([blocks(w_attn_out), blocks(w_conv_out), w_glu_value, w_glu_gate], axis=0)
    half = stack.shape[0] // 2
    near = toward(stack, 1, groups)
    after = toward(stack, -1, groups)
    far_low = toward(near[:half], 1, groups)
    far_high = toward(after[half:], -1, groups)
    small = jnp.concatenate(
        [depth_kernel, norm_scale[None], norm_shift[None], jnp.zeros((5, local_width), jnp.float32)],
        axis=0,
    )
    small_near, small_far, small_next = [toward(small, k, groups) for k in range(1, groups)]
    share = stream_count // groups
    cache_share = swap(
        conv_cache.reshape(groups, share, CONV_CACHE, local_width).transpose(0, 2, 1, 3),
        member,
        groups,
    )

    frames = spectra.transpose(1, 2, 0).reshape(FRAMES, taps, stream_count).transpose(0, 2, 1)
    queries, key_new, value_new, inputs = head(
        member, frames, sub_pieces, ln1_gain, (w_query, w_key, w_value)
    )
    context, key_rows, value_rows, leaving_rows = attend(
        valid_old,
        fill_old,
        bucket,
        queries,
        key_new,
        value_new,
        key_cache.transpose(1, 0, 2),
        value_cache.transpose(1, 0, 2),
        slots,
        groups,
    )
    received = lax.all_to_all(leaving_rows, "front", split_axis=0, concat_axis=0, tiled=True)
    context = swap(context, member, groups)
    valid_share = lax.dynamic_slice_in_dim(valid_old, member * share, share, 0)
    ended = tail(
        member,
        groups,
        *context,
        *cache_share,
        inputs,
        ln2_gain[None, :],
        jnp.broadcast_to(valid_share[:, None], (share, local_width)),
        stack,
        near,
        far_low,
        far_high,
        after,
        small,
        small_near,
        small_far,
        small_next,
    )
    ended = swap(ended, member, groups)
    ended = jnp.concatenate((ended[::-1] + ended[::-1])[:-1], axis=1)
    finished = lax.dynamic_slice_in_dim(ended, (groups - 1 - member) * share, stream_count, 1)
    picker = (
        bucket[None, :] == jnp.arange(slots, dtype=jnp.int32)[:, None]
    ).astype(jnp.bfloat16)
    leaving_end = jnp.einsum(
        "ls,tsc->ltc", picker, finished, preferred_element_type=jnp.float32
    ).astype(jnp.bfloat16)
    received_end = lax.all_to_all(leaving_end, "front", split_axis=0, concat_axis=0, tiled=True)
    placer = (
        arrival[:, None] == jnp.arange(slots, dtype=jnp.int32)[None, :]
    ).astype(jnp.bfloat16)
    placed = jnp.einsum(
        "sl,ltc->tsc", placer, received_end, preferred_element_type=jnp.float32
    ).astype(jnp.bfloat16)
    finished = jnp.where((arrival < 0)[None, :, None], finished, placed)
    key_done, value_done = place(arrival, received, key_rows, value_rows)
    return (
        finished[:FRAMES].transpose(1, 0, 2),
        key_done.transpose(1, 0, 2),
        value_done.transpose(1, 0, 2),
        finished[FRAMES:].transpose(1, 0, 2),
    )


def solution(mesh):
    in_specs = (
        P("front", None, None),
        P(None, "enc"),
        P("enc"),
        P("front", None, "enc"),
        P("front", None, "enc"),
        P("front", None, "enc"),
        P("front"),
        P("front"),
        P("front"),
        P("front"),
        P(),
        P(None, "enc"),
        P(None, "enc"),
        P(None, "enc"),
        P("enc", None),
        P(),
        P(None, "enc"),
        P(None, "enc"),
        P(None, "enc"),
        P("enc"),
        P("enc"),
        P("enc", None),
    )
    out_specs = (
        P("front", None, "enc"),
        P("front", None, "enc"),
        P("front", None, "enc"),
        P("front", None, "enc"),
    )

    return jax.shard_map(
        on_device, mesh=mesh, in_specs=in_specs, out_specs=out_specs, check_vma=False
    )
```

```python
import math

import jax
import jax.numpy as jnp
from jax import lax
from jax.experimental import pallas as pl
from jax.experimental.pallas import tpu as pltpu
from jax.sharding import PartitionSpec as P


MELS = 80
KERNEL = 9
SUB = 8
FRAMES = 7
CACHE = 70
CAP = 2
HEAD = 128
CONV_CACHE = 8
LANES = 128
BLOCK = 16
SPAN = 80
KEEP = 72
CHUNK = 10

masked_score = -1e30


def send_slots(new_slot, own_index, peer_count):
    stream_count = new_slot.shape[0]
    target = new_slot // stream_count
    leaving = target != own_index
    order = jnp.arange(stream_count, dtype=jnp.int32)
    earlier = (target[None, :] == target[:, None]) & (order[None, :] < order[:, None])
    position = jnp.sum(earlier.astype(jnp.int32), axis=1)
    return jnp.where(leaving, target * CAP + position, peer_count * CAP)


def arrival_slots(old_slot, own_index):
    stream_count = old_slot.shape[0]
    source = old_slot // stream_count
    staying = source == own_index
    earlier = (source[None, :] == source[:, None]) & (old_slot[None, :] < old_slot[:, None])
    position = jnp.sum(earlier.astype(jnp.int32), axis=1)
    return jnp.where(staying, -1, source * CAP + position)


def shift_rows(rows, first, second, third):
    rows = jnp.where(first, rows[1:], rows[:-1])
    rows = jnp.where(second, rows[2:], rows[:-2])
    return jnp.where(third, rows[4:], rows[:-4])


def attend_body(
    query_ref,
    key_new_ref,
    value_new_ref,
    key_ref,
    value_ref,
    valid_ref,
    fill_ref,
    context_ref,
    key_out_ref,
    value_out_ref,
):
    width = query_ref.shape[2]
    heads = width // LANES
    span = SPAN * BLOCK
    valid = valid_ref[...]
    low = (CACHE - fill_ref[:, :1]) * BLOCK
    high = (CACHE + valid[:, :1]) * BLOCK
    offset = lax.broadcasted_iota(jnp.int32, (BLOCK, span), 1) - lax.broadcasted_iota(
        jnp.int32, (BLOCK, span), 0
    )
    allowed = ((offset & (BLOCK - 1)) == 0) & (offset >= low) & (offset < high)
    bias = jnp.where(allowed, 0.0, masked_score)[None]
    padding = jnp.zeros(((SPAN - CACHE - FRAMES) * BLOCK, LANES), jnp.bfloat16)

    def joined(old_ref, new_ref, lanes):
        return jnp.concatenate(
            [
                old_ref[:, :, lanes].reshape(CACHE * BLOCK, LANES),
                new_ref[:, :, lanes].reshape(FRAMES * BLOCK, LANES),
                padding,
            ],
            axis=0,
        )

    for h in range(heads):
        lanes = slice(h * LANES, (h + 1) * LANES)
        scores = lax.dot_general(
            query_ref[:, :, lanes].reshape(FRAMES * BLOCK, LANES),
            joined(key_ref, key_new_ref, lanes),
            (((1,), (1,)), ((), ())),
            preferred_element_type=jnp.float32,
        )
        scores = scores.reshape(FRAMES, BLOCK, span) * (1.0 / math.sqrt(HEAD)) + bias
        exponent = jnp.exp(scores - jnp.max(scores, axis=2, keepdims=True))
        weights = exponent * (1.0 / jnp.sum(exponent, axis=2, keepdims=True))
        context = lax.dot_general(
            weights.astype(jnp.bfloat16).reshape(FRAMES * BLOCK, span),
            joined(value_ref, value_new_ref, lanes),
            (((1,), (0,)), ((), ())),
            preferred_element_type=jnp.float32,
        )
        context_ref[0, :, :, lanes] = context.reshape(FRAMES, BLOCK, LANES).astype(jnp.bfloat16)

    shift = valid - 1
    first = ((shift & 1) != 0)[None]
    second = ((shift & 2) != 0)[None]
    third = ((shift & 4) != 0)[None]
    edge = CACHE - FRAMES
    for old_ref, new_ref, out_ref in (
        (key_ref, key_new_ref, key_out_ref),
        (value_ref, value_new_ref, value_out_ref),
    ):
        for h in range(heads):
            lanes = slice(h * LANES, (h + 1) * LANES)
            old = old_ref[edge + 1 :, :, lanes].astype(jnp.float32)
            new = new_ref[:, :, lanes].astype(jnp.float32)
            rows = jnp.concatenate([old, new, new[:1]], axis=0)
            out_ref[:, :, lanes] = shift_rows(rows, first, second, third).astype(jnp.bfloat16)


def attend(valid_old, fill_old, queries, key_new, value_new, key_cache, value_cache, groups):
    stream_count = key_cache.shape[1]
    width = key_cache.shape[2]

    def wide(column):
        return jnp.broadcast_to(column[:, None], (stream_count, LANES))

    def block(rows):
        return pl.BlockSpec((rows, BLOCK, width), lambda i: (0, i, 0))

    per_group = stream_count // groups // BLOCK
    scalar = pl.BlockSpec((BLOCK, LANES), lambda i: (i, 0))
    context = pl.BlockSpec(
        (1, FRAMES, BLOCK, width), lambda i: (i // per_group, 0, i % per_group, 0)
    )
    slab = jax.ShapeDtypeStruct((FRAMES, stream_count, width), jnp.bfloat16)
    return pl.pallas_call(
        attend_body,
        grid=(stream_count // BLOCK,),
        in_specs=[block(FRAMES)] * 3 + [block(CACHE)] * 2 + [scalar] * 2,
        out_specs=[context, block(FRAMES), block(FRAMES)],
        out_shape=[
            jax.ShapeDtypeStruct((groups, FRAMES, stream_count // groups, width), jnp.bfloat16),
            slab,
            slab,
        ],
        name="attend",
    )(queries, key_new, value_new, key_cache, value_cache, wide(valid_old), wide(fill_old))


def pack_body(slot_s, key_ref, value_ref, send_ref, rows_f):
    base = pl.program_id(0) * BLOCK
    heads = rows_f.shape[1]
    slots = send_ref.shape[0]
    for kind, src in enumerate((key_ref, value_ref)):
        for h in range(heads):
            rows_f[kind, h, : CACHE * BLOCK, :] = (
                src[:, :, h * LANES : (h + 1) * LANES]
                .astype(jnp.float32)
                .reshape(CACHE * BLOCK, LANES)
            )

    def pack(s, carry):
        slot = slot_s[base + s]

        @pl.when(slot < slots)
        def _():
            for kind in range(2):
                for h in range(heads):
                    send_ref[slot, kind, :, h * LANES : (h + 1) * LANES] = rows_f[
                        kind, h, pl.ds(s, KEEP, stride=BLOCK), :
                    ].astype(jnp.bfloat16)

        return carry

    lax.fori_loop(0, BLOCK, pack, 0)


def pack_rows(bucket, key_cache, value_cache, slots):
    stream_count = key_cache.shape[1]
    width = key_cache.shape[2]
    block = pl.BlockSpec((CACHE, BLOCK, width), lambda i, *_: (0, i, 0))
    return pl.pallas_call(
        pack_body,
        grid_spec=pltpu.PrefetchScalarGridSpec(
            num_scalar_prefetch=1,
            grid=(stream_count // BLOCK,),
            in_specs=[block, block],
            out_specs=pl.BlockSpec((slots, 2, KEEP, width), lambda i, *_: (0, 0, 0, 0)),
            scratch_shapes=[
                pltpu.VMEM((2, width // HEAD, KEEP * BLOCK, LANES), jnp.float32)
            ],
        ),
        out_shape=jax.ShapeDtypeStruct((slots, 2, KEEP, width), jnp.bfloat16),
        name="pack",
    )(bucket, key_cache, value_cache)


def place_body(
    arrival_s, got_ref, valid_ref, key_ref, value_ref, key_out_ref, value_out_ref, rows_f
):
    base = pl.program_id(0) * BLOCK
    heads = rows_f.shape[1]
    for kind, src in enumerate((key_ref, value_ref)):
        for h in range(heads):
            lanes = slice(h * LANES, (h + 1) * LANES)
            for start in range(0, CACHE, CHUNK):
                rows_f[kind, h, start * BLOCK : (start + CHUNK) * BLOCK, :] = (
                    src[start : start + CHUNK, :, lanes]
                    .astype(jnp.float32)
                    .reshape(CHUNK * BLOCK, LANES)
                )

    def fetch(s, carry):
        slot = arrival_s[base + s]

        @pl.when(slot >= 0)
        def _():
            for kind in range(2):
                for h in range(heads):
                    rows_f[kind, h, pl.ds(s, KEEP, stride=BLOCK), :] = got_ref[
                        slot, kind, :, h * LANES : (h + 1) * LANES
                    ].astype(jnp.float32)

        return carry

    lax.fori_loop(0, BLOCK, fetch, 0)
    shift = valid_ref[...] - 1
    first = ((shift & 1) != 0)[None]
    second = ((shift & 2) != 0)[None]
    third = ((shift & 4) != 0)[None]
    edge = CACHE - FRAMES
    for kind, dst in enumerate((key_out_ref, value_out_ref)):
        for h in range(heads):
            lanes = slice(h * LANES, (h + 1) * LANES)
            for start in range(0, edge, 9):
                rows = rows_f[kind, h, (start + 1) * BLOCK : (start + 17) * BLOCK, :]
                rows = shift_rows(rows.reshape(16, BLOCK, LANES), first, second, third)
                dst[start : start + 9, :, lanes] = rows.astype(jnp.bfloat16)
            dst[edge:, :, lanes] = jnp.zeros((FRAMES, BLOCK, LANES), jnp.bfloat16)


def place(arrival, valid_new, received, key_rows, value_rows):
    stream_count = key_rows.shape[1]
    width = key_rows.shape[2]
    heads = width // HEAD
    slots = received.shape[0]
    block = pl.BlockSpec((CACHE, BLOCK, width), lambda i, *_: (0, i, 0))
    shape = jax.ShapeDtypeStruct((CACHE, stream_count, width), jnp.bfloat16)
    return pl.pallas_call(
        place_body,
        grid_spec=pltpu.PrefetchScalarGridSpec(
            num_scalar_prefetch=1,
            grid=(stream_count // BLOCK,),
            in_specs=[
                pl.BlockSpec((slots, 2, KEEP, width), lambda i, *_: (0, 0, 0, 0)),
                pl.BlockSpec((BLOCK, LANES), lambda i, *_: (i, 0)),
                block,
                block,
            ],
            out_specs=[block, block],
            scratch_shapes=[pltpu.VMEM((2, heads, KEEP * BLOCK, LANES), jnp.float32)],
        ),
        out_shape=[shape, shape],
        name="place",
    )(
        arrival,
        received,
        jnp.broadcast_to(valid_new[:, None], (stream_count, LANES)),
        key_rows,
        value_rows,
    )


def head_body(
    place_s, frames_ref, own_ref, near_ref, far_ref, next_ref, gain_ref, *rest
):
    weights, outs, inputs_ref, raw = rest[:3], rest[3:6], rest[6], rest[7]
    member = place_s[0]
    groups = raw.shape[0]
    taps = frames_ref.shape[2]
    width = raw.shape[2]
    frames = frames_ref[0]
    for offset, piece in enumerate((own_ref, near_ref, far_ref, next_ref)):
        total = jnp.dot(frames, piece[:taps, :], preferred_element_type=jnp.float32)
        total = total + piece[taps : taps + 16, :].astype(jnp.float32)[:1]
        raw[(member + groups - offset) % groups] = total.astype(jnp.bfloat16)
    values = [raw[g].astype(jnp.float32) for g in range(groups)]
    model_width = groups * width
    average = sum(jnp.sum(v, axis=1, keepdims=True) for v in values) * (1.0 / model_width)
    values = [v - average for v in values]
    spread = sum(jnp.sum(v * v, axis=1, keepdims=True) for v in values) * (1.0 / model_width)
    scale = lax.rsqrt(spread + 1e-05)
    normed = [
        (v * scale * gain_ref[:, g * width : (g + 1) * width]).astype(jnp.bfloat16)
        for g, v in enumerate(values)
    ]
    normed = jnp.concatenate(normed, axis=1)
    for matrix, out in zip(weights, outs):
        out[0] = jnp.dot(normed, matrix[...], preferred_element_type=jnp.float32).astype(
            jnp.bfloat16
        )
    share = inputs_ref.shape[1]
    for g in range(groups):
        inputs_ref[0, :, g * width : (g + 1) * width] = raw[
            g, pl.ds(pl.multiple_of(member * share, share), share), :
        ]


def head(member, frames, pieces, gain, matrices):
    count, streams, taps = frames.shape
    width = matrices[0].shape[1]
    groups = len(pieces)

    def whole(array):
        return pl.BlockSpec(array.shape, lambda i, *_: (0, 0))

    per_frame = pl.BlockSpec((1, streams, width), lambda i, *_: (i, 0, 0))
    shape = jax.ShapeDtypeStruct((count, streams, width), jnp.bfloat16)
    gain = gain[None, :]
    return pl.pallas_call(
        head_body,
        grid_spec=pltpu.PrefetchScalarGridSpec(
            num_scalar_prefetch=1,
            grid=(count,),
            in_specs=[pl.BlockSpec((1, streams, taps), lambda i, *_: (i, 0, 0))]
            + [whole(p) for p in pieces]
            + [whole(gain)]
            + [whole(w) for w in matrices],
            out_specs=[per_frame, per_frame, per_frame]
            + [pl.BlockSpec((1, streams // groups, groups * width), lambda i, *_: (i, 0, 0))],
            scratch_shapes=[pltpu.VMEM((groups, streams, width), jnp.bfloat16)],
        ),
        out_shape=[shape, shape, shape]
        + [jax.ShapeDtypeStruct((count, streams // groups, groups * width), jnp.bfloat16)],
        name="head",
    )(member[None], frames, *pieces, gain, *matrices)


def tail_body(place_s, *refs):
    contexts, caches, smalls, rest = refs[:4], refs[4:8], refs[8:12], refs[12:]
    inputs_ref, gain_ref, valid_ref = rest[:3]
    attn_ref, conv_ref, value_ref, gate_ref = rest[3:7]
    low_refs, high_refs, out_ref = rest[7:13], rest[13:19], rest[19]
    member = place_s[0]
    front_half = place_s[1] == 0
    groups = len(contexts)
    _, share, width = contexts[0].shape
    rows = FRAMES * share
    size = groups * width
    half = width // 2

    def ordered(operand):
        middle_lane = operand.shape[1] // 2
        low, high = operand[:, :middle_lane], operand[:, middle_lane:]
        return jnp.where(front_half, low, high), jnp.where(front_half, high, low)

    def dot(left, right):
        return jnp.dot(left, right, preferred_element_type=jnp.float32)

    def grouped(step, operand, own_ref, start, sums):
        sides = ordered(operand)
        for n in range(groups):
            if step == 0:
                part = dot(operand, own_ref[:, n * width : (n + 1) * width])
            else:
                at = start + n * half
                part = sum(
                    dot(side, low_refs[2 * (step - 1) + i][at : at + half, :])
                    for i, side in enumerate(sides)
                )
            part = part.astype(jnp.bfloat16).astype(jnp.float32)
            sums[n] = part if sums[n] is None else sums[n] + part

    def wide(step, own_ref, order):
        if step == 0:
            return dot(normed, own_ref[...])
        at = high_starts[step - 1] + order * (size // 2)
        return sum(
            dot(side, high_refs[2 * (step - 1) + i][at : at + size // 2, :])
            for i, side in enumerate(normed_sides)
        )

    high_starts = (size, 0, size)
    attended = [None] * groups
    for step in range(groups):
        grouped(step, contexts[step][...].reshape(rows, width), attn_ref, 0, attended)
    middle = []
    for n in range(groups):
        inputs = inputs_ref[:, :, n * width : (n + 1) * width].reshape(rows, width)
        middle.append((inputs.astype(jnp.float32) + attended[n]).astype(jnp.bfloat16))
    values = [m.astype(jnp.float32) for m in middle]
    average = sum(jnp.sum(v, axis=1, keepdims=True) for v in values) * (1.0 / size)
    values = [v - average for v in values]
    spread = sum(jnp.sum(v * v, axis=1, keepdims=True) for v in values) * (1.0 / size)
    scale = lax.rsqrt(spread + 1e-05)
    normed = jnp.concatenate(
        [
            (v * scale * gain_ref[:, n * width : (n + 1) * width]).astype(jnp.bfloat16)
            for n, v in enumerate(values)
        ],
        axis=1,
    )
    normed_sides = ordered(normed)
    valid = valid_ref[...]
    shift = valid - 1
    first = ((shift & 1) != 0)[None]
    second = ((shift & 2) != 0)[None]
    third = ((shift & 4) != 0)[None]
    conv_term = [None] * groups
    for step in range(groups):
        group = (member + groups - step) % groups
        cache_ref, small_ref = caches[step], smalls[step]
        glu_value = wide(step, value_ref, 0)
        glu_gate = wide(step, gate_ref, 1)
        gated = (glu_value * jax.nn.sigmoid(glu_gate)).astype(jnp.bfloat16)
        conv_in = jnp.concatenate(
            [
                cache_ref[...].astype(jnp.float32),
                gated.astype(jnp.float32).reshape(FRAMES, share, width),
            ],
            axis=0,
        )
        depthwise = jnp.zeros((FRAMES, share, width), jnp.float32)
        for tap in range(KERNEL):
            depthwise = depthwise + small_ref[tap : tap + 1, :][None] * conv_in[tap : tap + FRAMES]
        shaped = depthwise * small_ref[KERNEL : KERNEL + 1, :][None]
        shaped = shaped + small_ref[KERNEL + 1 : KERNEL + 2, :][None]
        activated = (shaped * jax.nn.sigmoid(shaped)).astype(jnp.bfloat16)
        grouped(step, activated.reshape(rows, width), conv_ref, size // 2, conv_term)
        moved = shift_rows(
            jnp.concatenate([conv_in[1:], conv_in[-1:]], axis=0), first, second, third
        )
        out_ref[group, FRAMES:, :, :] = moved.astype(jnp.bfloat16)
    frame = lax.broadcasted_iota(jnp.int32, (FRAMES, share, width), 0)
    for n in range(groups):
        total = (middle[n].astype(jnp.float32) + conv_term[n]).reshape(FRAMES, share, width)
        out_ref[n, :FRAMES, :, :] = jnp.where(frame < valid[None], total, 0.0).astype(jnp.bfloat16)


def tail(where, groups, *arrays):
    _, share, width = arrays[0].shape
    return pl.pallas_call(
        tail_body,
        in_specs=[pl.BlockSpec(memory_space=pltpu.SMEM)]
        + [pl.BlockSpec(memory_space=pltpu.VMEM)] * len(arrays),
        out_specs=pl.BlockSpec(memory_space=pltpu.VMEM),
        out_shape=jax.ShapeDtypeStruct((groups, FRAMES + CONV_CACHE, share, width), jnp.bfloat16),
        name="tail",
    )(where, *arrays)


def swap(chunks, member, count):
    pieces = [lax.dynamic_index_in_dim(chunks, member, 0, False)]
    for step in range(1, count):
        chunk = lax.dynamic_index_in_dim(chunks, (member + step) % count, 0, False)
        pieces.append(toward(chunk, step, count))
    return pieces


def toward(array, steps, count):
    return lax.ppermute(array, "enc", [(i, (i + steps) % count) for i in range(count)])


def on_device(
    spectra,
    sub_weight,
    sub_bias,
    key_cache,
    value_cache,
    conv_cache,
    new_slot,
    old_slot,
    valid_new,
    cache_fill,
    ln1_gain,
    w_query,
    w_key,
    w_value,
    w_attn_out,
    ln2_gain,
    w_glu_value,
    w_glu_gate,
    depth_kernel,
    norm_scale,
    norm_shift,
    w_conv_out,
):
    peer_count = lax.axis_size("front")
    own_index = lax.axis_index("front")
    member = lax.axis_index("enc")
    stream_count = spectra.shape[0]
    local_width = w_query.shape[1]
    slots = peer_count * CAP
    bucket = send_slots(new_slot, own_index, peer_count)
    arrival = arrival_slots(old_slot, own_index)
    slot_ids = jnp.arange(slots, dtype=jnp.int32)
    both = valid_new * 128 + cache_fill
    asked = jnp.sum(jnp.where(arrival[None, :] == slot_ids[:, None], both[None, :], 0), axis=1)
    told = lax.all_to_all(
        jnp.broadcast_to(asked[:, None], (slots, LANES)),
        "front",
        split_axis=0,
        concat_axis=0,
        tiled=True,
    )[:, 0]
    told = jnp.sum(jnp.where(bucket[:, None] == slot_ids[None, :], told[None, :], 0), axis=1)
    both_old = jnp.where(bucket < slots, told, both)
    valid_old = both_old // 128
    fill_old = both_old % 128

    key_rows = key_cache.transpose(1, 0, 2)
    value_rows = value_cache.transpose(1, 0, 2)
    leaving_rows = pack_rows(bucket, key_rows, value_rows, slots)
    received = lax.all_to_all(leaving_rows, "front", split_axis=0, concat_axis=0, tiled=True)
    groups = lax.axis_size("enc")
    taps = SUB * MELS
    with_bias = jnp.concatenate(
        [sub_weight, jnp.broadcast_to(sub_bias[None, :], (16, local_width))], axis=0
    )
    sub_pieces = [with_bias] + [toward(with_bias, k, groups) for k in range(1, groups)]

    core = own_index % 2
    half = local_width // 2

    def core_rows(matrix):
        count = matrix.shape[0] // 2
        return lax.dynamic_slice_in_dim(matrix, core * count, count, 0)

    def blocks(matrix):
        return (
            core_rows(matrix)
            .reshape(half, groups, local_width)
            .transpose(1, 0, 2)
            .reshape(groups * half, local_width)
        )

    stack = jnp.concatenate(
        [blocks(w_attn_out), blocks(w_conv_out), core_rows(w_glu_value), core_rows(w_glu_gate)],
        axis=0,
    )
    middle_row = stack.shape[0] // 2

    def other_core(array):
        return lax.ppermute(array, "front", [(i, i ^ 1) for i in range(peer_count)])

    near = toward(stack, 1, groups)
    after = toward(stack, -1, groups)
    far_low = toward(near[:middle_row], 1, groups)
    far_high = toward(after[middle_row:], -1, groups)
    near_other = other_core(near)
    after_other = other_core(after)
    far_low_other = other_core(far_low)
    far_high_other = other_core(far_high)
    small = jnp.concatenate(
        [depth_kernel, norm_scale[None], norm_shift[None], jnp.zeros((5, local_width), jnp.float32)],
        axis=0,
    )
    small_near, small_far, small_next = [toward(small, k, groups) for k in range(1, groups)]
    share = stream_count // groups
    cache_share = swap(
        conv_cache.reshape(groups, share, CONV_CACHE, local_width).transpose(0, 2, 1, 3),
        member,
        groups,
    )

    frames = spectra.transpose(1, 2, 0).reshape(FRAMES, taps, stream_count).transpose(0, 2, 1)
    queries, key_new, value_new, inputs = head(
        member, frames, sub_pieces, ln1_gain, (w_query, w_key, w_value)
    )
    context, key_slab, value_slab = attend(
        valid_old, fill_old, queries, key_new, value_new, key_rows, value_rows, groups
    )
    context = swap(context, member, groups)
    valid_share = lax.dynamic_slice_in_dim(valid_old, member * share, share, 0)
    ended = tail(
        jnp.stack([member, core]),
        groups,
        *context,
        *cache_share,
        small,
        small_near,
        small_far,
        small_next,
        inputs,
        ln2_gain[None, :],
        jnp.broadcast_to(valid_share[:, None], (share, local_width)),
        w_attn_out,
        w_conv_out,
        w_glu_value,
        w_glu_gate,
        near,
        near_other,
        far_low,
        far_low_other,
        after,
        after_other,
        near,
        near_other,
        far_high,
        far_high_other,
        after,
        after_other,
    )
    ended = swap(ended, member, groups)
    ended = jnp.concatenate((ended[::-1] + ended[::-1])[:-1], axis=1)
    finished = lax.dynamic_slice_in_dim(ended, (groups - 1 - member) * share, stream_count, 1)
    finished = jnp.concatenate([finished, key_slab, value_slab], axis=0)
    picker = (
        bucket[None, :] == jnp.arange(slots, dtype=jnp.int32)[:, None]
    ).astype(jnp.bfloat16)
    leaving_end = jnp.einsum(
        "ls,tsc->ltc", picker, finished, preferred_element_type=jnp.float32
    ).astype(jnp.bfloat16)
    received_end = lax.all_to_all(leaving_end, "front", split_axis=0, concat_axis=0, tiled=True)
    placer = (
        arrival[:, None] == jnp.arange(slots, dtype=jnp.int32)[None, :]
    ).astype(jnp.bfloat16)
    placed = jnp.einsum(
        "sl,ltc->tsc", placer, received_end, preferred_element_type=jnp.float32
    ).astype(jnp.bfloat16)
    finished = jnp.where((arrival < 0)[None, :, None], finished, placed)
    key_done, value_done = place(arrival, valid_new, received, key_rows, value_rows)
    edge = CACHE - FRAMES
    ends = FRAMES + CONV_CACHE
    key_done = lax.dynamic_update_slice_in_dim(key_done, finished[ends : ends + FRAMES], edge, 0)
    value_done = lax.dynamic_update_slice_in_dim(value_done, finished[ends + FRAMES :], edge, 0)
    return (
        finished[:FRAMES].transpose(1, 0, 2),
        key_done.transpose(1, 0, 2),
        value_done.transpose(1, 0, 2),
        finished[FRAMES:ends].transpose(1, 0, 2),
    )


def solution(mesh):
    in_specs = (
        P("front", None, None),
        P(None, "enc"),
        P("enc"),
        P("front", None, "enc"),
        P("front", None, "enc"),
        P("front", None, "enc"),
        P("front"),
        P("front"),
        P("front"),
        P("front"),
        P(),
        P(None, "enc"),
        P(None, "enc"),
        P(None, "enc"),
        P("enc", None),
        P(),
        P(None, "enc"),
        P(None, "enc"),
        P(None, "enc"),
        P("enc"),
        P("enc"),
        P("enc", None),
    )
    out_specs = (
        P("front", None, "enc"),
        P("front", None, "enc"),
        P("front", None, "enc"),
        P("front", None, "enc"),
    )

    return jax.shard_map(
        on_device, mesh=mesh, in_specs=in_specs, out_specs=out_specs, check_vma=False
    )
```

```python
import math

import jax
import jax.numpy as jnp
from jax import lax
from jax.experimental import pallas as pl
from jax.experimental.pallas import tpu as pltpu
from jax.sharding import PartitionSpec as P


MELS = 80
KERNEL = 9
SUB = 8
FRAMES = 7
CACHE = 70
CAP = 2
HEAD = 128
CONV_CACHE = 8
LANES = 128
BLOCK = 16
SPAN = 80
KEEP = 72
CHUNK = 10
FIELD = 7

masked_score = -1e30


def route_body(own_s, new_ref, old_ref, both_ref, bucket_ref, arrival_ref, asked_ref):
    own = own_s[0]
    slots, count = asked_ref.shape
    bits = count.bit_length() - 1

    def column(row):
        return jnp.transpose(jnp.broadcast_to(row, (count, count)))

    def ranked(group_column, group_row, before):
        same = jnp.where((group_column == group_row) & before, 1.0, 0.0)
        return jnp.sum(same, axis=0, keepdims=True).astype(jnp.int32)

    target = new_ref[...] >> bits
    first = lax.broadcasted_iota(jnp.int32, (count, count), 0)
    second = lax.broadcasted_iota(jnp.int32, (count, count), 1)
    position = ranked(column(target), target, first < second)
    bucket_ref[...] = jnp.where(target != own, target * CAP + position, slots)
    old_row = old_ref[...]
    old_column = column(old_row)
    source = old_row >> bits
    position = ranked(old_column >> bits, source, old_column < old_row)
    arrival = jnp.where(source == own, -1, source * CAP + position)
    arrival_ref[...] = arrival
    slot = lax.broadcasted_iota(jnp.int32, (slots, count), 0)
    hit = jnp.where(arrival == slot, both_ref[...].astype(jnp.float32), 0.0)
    asked = jnp.sum(hit, axis=1, keepdims=True).astype(jnp.int32)
    asked_ref[...] = jnp.broadcast_to(asked, (slots, count))


def route(own_index, new_slot, old_slot, both, slots):
    count = new_slot.shape[0]
    row = jax.ShapeDtypeStruct((1, count), jnp.int32)
    bucket, arrival, asked = pl.pallas_call(
        route_body,
        in_specs=[pl.BlockSpec(memory_space=pltpu.SMEM)]
        + [pl.BlockSpec(memory_space=pltpu.VMEM)] * 3,
        out_specs=[pl.BlockSpec(memory_space=pltpu.VMEM)] * 3,
        out_shape=[row, row, jax.ShapeDtypeStruct((slots, count), jnp.int32)],
        name="route",
    )(own_index[None], new_slot[None], old_slot[None], both[None])
    return bucket[0], arrival[0], asked


def shift_rows(rows, first, second, third):
    rows = jnp.where(first, rows[1:], rows[:-1])
    rows = jnp.where(second, rows[2:], rows[:-2])
    return jnp.where(third, rows[4:], rows[:-4])


def attend_body(
    bucket_s,
    both_s,
    told_ref,
    query_ref,
    key_new_ref,
    value_new_ref,
    key_ref,
    value_ref,
    context_ref,
    key_out_ref,
    value_out_ref,
    packed_ref,
):
    base = pl.program_id(0) * BLOCK
    slots = told_ref.shape[0]
    for s in range(BLOCK):
        slot = bucket_s[base + s]
        told = told_ref[pl.ds(jnp.minimum(slot, slots - 1), 1), :]
        packed_ref[s : s + 1, :] = jnp.where(
            slot < slots, told, jnp.full_like(told, both_s[base + s])
        )
    packed = packed_ref[...]
    width = query_ref.shape[2]
    heads = width // LANES
    span = SPAN * BLOCK
    valid = packed >> FIELD
    low = (CACHE - (packed[:, :1] & ((1 << FIELD) - 1))) * BLOCK
    high = (CACHE + valid[:, :1]) * BLOCK
    offset = lax.broadcasted_iota(jnp.int32, (BLOCK, span), 1) - lax.broadcasted_iota(
        jnp.int32, (BLOCK, span), 0
    )
    allowed = ((offset & (BLOCK - 1)) == 0) & (offset >= low) & (offset < high)
    bias = jnp.where(allowed, 0.0, masked_score)[None]
    padding = jnp.zeros(((SPAN - CACHE - FRAMES) * BLOCK, LANES), jnp.bfloat16)

    def joined(old_ref, new_ref, lanes):
        return jnp.concatenate(
            [
                old_ref[:, :, lanes].reshape(CACHE * BLOCK, LANES),
                new_ref[:, :, lanes].reshape(FRAMES * BLOCK, LANES),
                padding,
            ],
            axis=0,
        )

    for h in range(heads):
        lanes = slice(h * LANES, (h + 1) * LANES)
        scores = lax.dot_general(
            query_ref[:, :, lanes].reshape(FRAMES * BLOCK, LANES),
            joined(key_ref, key_new_ref, lanes),
            (((1,), (1,)), ((), ())),
            preferred_element_type=jnp.float32,
        )
        scores = scores.reshape(FRAMES, BLOCK, span) * (1.0 / math.sqrt(HEAD)) + bias
        exponent = jnp.exp(scores - jnp.max(scores, axis=2, keepdims=True))
        weights = exponent * (1.0 / jnp.sum(exponent, axis=2, keepdims=True))
        context = lax.dot_general(
            weights.astype(jnp.bfloat16).reshape(FRAMES * BLOCK, span),
            joined(value_ref, value_new_ref, lanes),
            (((1,), (0,)), ((), ())),
            preferred_element_type=jnp.float32,
        )
        context_ref[0, :, :, lanes] = context.reshape(FRAMES, BLOCK, LANES).astype(jnp.bfloat16)

    shift = valid - 1
    first = ((shift & 1) != 0)[None]
    second = ((shift & 2) != 0)[None]
    third = ((shift & 4) != 0)[None]
    edge = CACHE - FRAMES
    for old_ref, new_ref, out_ref in (
        (key_ref, key_new_ref, key_out_ref),
        (value_ref, value_new_ref, value_out_ref),
    ):
        for h in range(heads):
            lanes = slice(h * LANES, (h + 1) * LANES)
            old = old_ref[edge + 1 :, :, lanes].astype(jnp.float32)
            new = new_ref[:, :, lanes].astype(jnp.float32)
            rows = jnp.concatenate([old, new, new[:1]], axis=0)
            out_ref[:, :, lanes] = shift_rows(rows, first, second, third).astype(jnp.bfloat16)


def attend(bucket, both, told, queries, key_new, value_new, key_cache, value_cache, groups):
    stream_count = key_cache.shape[1]
    width = key_cache.shape[2]

    def block(rows):
        return pl.BlockSpec((rows, BLOCK, width), lambda i, *_: (0, i, 0))

    per_group = stream_count // groups // BLOCK
    context = pl.BlockSpec(
        (1, FRAMES, BLOCK, width), lambda i, *_: (i // per_group, 0, i % per_group, 0)
    )
    slab = jax.ShapeDtypeStruct((FRAMES, stream_count, width), jnp.bfloat16)
    return pl.pallas_call(
        attend_body,
        grid_spec=pltpu.PrefetchScalarGridSpec(
            num_scalar_prefetch=2,
            grid=(stream_count // BLOCK,),
            in_specs=[pl.BlockSpec(told.shape, lambda i, *_: (0, 0))]
            + [block(FRAMES)] * 3
            + [block(CACHE)] * 2,
            out_specs=[
                context,
                block(FRAMES),
                block(FRAMES),
                pl.BlockSpec((BLOCK, LANES), lambda i, *_: (i, 0)),
            ],
        ),
        out_shape=[
            jax.ShapeDtypeStruct((groups, FRAMES, stream_count // groups, width), jnp.bfloat16),
            slab,
            slab,
            jax.ShapeDtypeStruct((stream_count, LANES), jnp.int32),
        ],
        name="attend",
    )(bucket, both, told, queries, key_new, value_new, key_cache, value_cache)


def pack_body(slot_s, key_ref, value_ref, send_ref, rows_f):
    base = pl.program_id(0) * BLOCK
    heads = rows_f.shape[1]
    slots = send_ref.shape[0]
    for kind, src in enumerate((key_ref, value_ref)):
        for h in range(heads):
            rows_f[kind, h, : CACHE * BLOCK, :] = (
                src[:, :, h * LANES : (h + 1) * LANES]
                .astype(jnp.float32)
                .reshape(CACHE * BLOCK, LANES)
            )

    def pack(s, carry):
        slot = slot_s[base + s]

        @pl.when(slot < slots)
        def _():
            for kind in range(2):
                for h in range(heads):
                    send_ref[slot, kind, :, h * LANES : (h + 1) * LANES] = rows_f[
                        kind, h, pl.ds(s, KEEP, stride=BLOCK), :
                    ].astype(jnp.bfloat16)

        return carry

    lax.fori_loop(0, BLOCK, pack, 0)


def pack_rows(bucket, key_cache, value_cache, slots):
    stream_count = key_cache.shape[1]
    width = key_cache.shape[2]
    block = pl.BlockSpec((CACHE, BLOCK, width), lambda i, *_: (0, i, 0))
    return pl.pallas_call(
        pack_body,
        grid_spec=pltpu.PrefetchScalarGridSpec(
            num_scalar_prefetch=1,
            grid=(stream_count // BLOCK,),
            in_specs=[block, block],
            out_specs=pl.BlockSpec((slots, 2, KEEP, width), lambda i, *_: (0, 0, 0, 0)),
            scratch_shapes=[
                pltpu.VMEM((2, width // HEAD, KEEP * BLOCK, LANES), jnp.float32)
            ],
        ),
        out_shape=jax.ShapeDtypeStruct((slots, 2, KEEP, width), jnp.bfloat16),
        name="pack",
    )(bucket, key_cache, value_cache)


def place_body(
    arrival_s, got_ref, valid_ref, key_ref, value_ref, key_out_ref, value_out_ref, rows_f
):
    base = pl.program_id(0) * BLOCK
    heads = rows_f.shape[1]
    for kind, src in enumerate((key_ref, value_ref)):
        for h in range(heads):
            lanes = slice(h * LANES, (h + 1) * LANES)
            for start in range(0, CACHE, CHUNK):
                rows_f[kind, h, start * BLOCK : (start + CHUNK) * BLOCK, :] = (
                    src[start : start + CHUNK, :, lanes]
                    .astype(jnp.float32)
                    .reshape(CHUNK * BLOCK, LANES)
                )

    def fetch(s, carry):
        slot = arrival_s[base + s]

        @pl.when(slot >= 0)
        def _():
            for kind in range(2):
                for h in range(heads):
                    rows_f[kind, h, pl.ds(s, KEEP, stride=BLOCK), :] = got_ref[
                        slot, kind, :, h * LANES : (h + 1) * LANES
                    ].astype(jnp.float32)

        return carry

    lax.fori_loop(0, BLOCK, fetch, 0)
    shift = valid_ref[...] - 1
    first = ((shift & 1) != 0)[None]
    second = ((shift & 2) != 0)[None]
    third = ((shift & 4) != 0)[None]
    edge = CACHE - FRAMES
    for kind, dst in enumerate((key_out_ref, value_out_ref)):
        for h in range(heads):
            lanes = slice(h * LANES, (h + 1) * LANES)
            for start in range(0, edge, 9):
                rows = rows_f[kind, h, (start + 1) * BLOCK : (start + 17) * BLOCK, :]
                rows = shift_rows(rows.reshape(16, BLOCK, LANES), first, second, third)
                dst[start : start + 9, :, lanes] = rows.astype(jnp.bfloat16)
            dst[edge:, :, lanes] = jnp.zeros((FRAMES, BLOCK, LANES), jnp.bfloat16)


def place(arrival, valid_new, received, key_rows, value_rows):
    stream_count = key_rows.shape[1]
    width = key_rows.shape[2]
    heads = width // HEAD
    slots = received.shape[0]
    block = pl.BlockSpec((CACHE, BLOCK, width), lambda i, *_: (0, i, 0))
    shape = jax.ShapeDtypeStruct((CACHE, stream_count, width), jnp.bfloat16)
    return pl.pallas_call(
        place_body,
        grid_spec=pltpu.PrefetchScalarGridSpec(
            num_scalar_prefetch=1,
            grid=(stream_count // BLOCK,),
            in_specs=[
                pl.BlockSpec((slots, 2, KEEP, width), lambda i, *_: (0, 0, 0, 0)),
                pl.BlockSpec((BLOCK, LANES), lambda i, *_: (i, 0)),
                block,
                block,
            ],
            out_specs=[block, block],
            scratch_shapes=[pltpu.VMEM((2, heads, KEEP * BLOCK, LANES), jnp.float32)],
        ),
        out_shape=[shape, shape],
        name="place",
    )(
        arrival,
        received,
        jnp.broadcast_to(valid_new[:, None], (stream_count, LANES)),
        key_rows,
        value_rows,
    )


def head_body(
    place_s, frames_ref, own_ref, near_ref, far_ref, next_ref, gain_ref, *rest
):
    weights, outs, inputs_ref, raw = rest[:3], rest[3:6], rest[6], rest[7]
    member = place_s[0]
    groups = raw.shape[0]
    taps = frames_ref.shape[1]
    width = raw.shape[2]
    frames = jnp.transpose(frames_ref[0])
    for offset, piece in enumerate((own_ref, near_ref, far_ref, next_ref)):
        total = jnp.dot(frames, piece[:taps, :], preferred_element_type=jnp.float32)
        total = total + piece[taps : taps + 16, :].astype(jnp.float32)[:1]
        raw[(member + groups - offset) % groups] = total.astype(jnp.bfloat16)
    values = [raw[g].astype(jnp.float32) for g in range(groups)]
    model_width = groups * width
    average = sum(jnp.sum(v, axis=1, keepdims=True) for v in values) * (1.0 / model_width)
    values = [v - average for v in values]
    spread = sum(jnp.sum(v * v, axis=1, keepdims=True) for v in values) * (1.0 / model_width)
    scale = lax.rsqrt(spread + 1e-05)
    normed = [
        (v * scale * gain_ref[:, g * width : (g + 1) * width]).astype(jnp.bfloat16)
        for g, v in enumerate(values)
    ]
    normed = jnp.concatenate(normed, axis=1)
    for matrix, out in zip(weights, outs):
        out[0] = jnp.dot(normed, matrix[...], preferred_element_type=jnp.float32).astype(
            jnp.bfloat16
        )
    share = inputs_ref.shape[1]
    for g in range(groups):
        inputs_ref[0, :, g * width : (g + 1) * width] = raw[
            g, pl.ds(pl.multiple_of(member * share, share), share), :
        ]


def head(member, frames, pieces, gain, matrices):
    count, taps, streams = frames.shape
    width = matrices[0].shape[1]
    groups = len(pieces)

    def whole(array):
        return pl.BlockSpec(array.shape, lambda i, *_: (0, 0))

    per_frame = pl.BlockSpec((1, streams, width), lambda i, *_: (i, 0, 0))
    shape = jax.ShapeDtypeStruct((count, streams, width), jnp.bfloat16)
    gain = gain[None, :]
    return pl.pallas_call(
        head_body,
        grid_spec=pltpu.PrefetchScalarGridSpec(
            num_scalar_prefetch=1,
            grid=(count,),
            in_specs=[pl.BlockSpec((1, taps, streams), lambda i, *_: (i, 0, 0))]
            + [pl.BlockSpec((taps + 16, width), lambda i, *_: (0, 0))] * groups
            + [whole(gain)]
            + [whole(w) for w in matrices],
            out_specs=[per_frame, per_frame, per_frame]
            + [pl.BlockSpec((1, streams // groups, groups * width), lambda i, *_: (i, 0, 0))],
            scratch_shapes=[pltpu.VMEM((groups, streams, width), jnp.bfloat16)],
        ),
        out_shape=[shape, shape, shape]
        + [jax.ShapeDtypeStruct((count, streams // groups, groups * width), jnp.bfloat16)],
        name="head",
    )(member[None], frames, *pieces, gain, *matrices)


def tail_body(place_s, *refs):
    contexts, pieces, rest = refs[:4], refs[4:8], refs[8:]
    inputs_ref, gain_ref, packed_ref = rest[:3]
    attn_ref, conv_ref, value_ref, gate_ref = rest[3:7]
    low_refs, high_refs, outs = rest[7:13], rest[13:19], rest[19:23]
    out_ref, cache_f = rest[23:]
    member = place_s[0]
    front_half = place_s[1] == 0
    groups = len(contexts)
    _, share, width = contexts[0].shape
    rows = FRAMES * share
    size = groups * width
    half = width // 2

    def ordered(operand):
        middle_lane = operand.shape[1] // 2
        low, high = operand[:, :middle_lane], operand[:, middle_lane:]
        return jnp.where(front_half, low, high), jnp.where(front_half, high, low)

    def dot(left, right):
        return jnp.dot(left, right, preferred_element_type=jnp.float32)

    def grouped(step, operand, own_ref, start, sums):
        sides = ordered(operand)
        for n in range(groups):
            if step == 0:
                part = dot(operand, own_ref[:, n * width : (n + 1) * width])
            else:
                at = start + n * half
                part = sum(
                    dot(side, low_refs[2 * (step - 1) + i][at : at + half, :])
                    for i, side in enumerate(sides)
                )
            part = part.astype(jnp.bfloat16).astype(jnp.float32)
            sums[n] = part if sums[n] is None else sums[n] + part

    def wide(step, own_ref, order):
        if step == 0:
            return dot(normed, own_ref[...])
        at = high_starts[step - 1] + order * (size // 2)
        return sum(
            dot(side, high_refs[2 * (step - 1) + i][at : at + size // 2, :])
            for i, side in enumerate(normed_sides)
        )

    high_starts = (size, 0, size)
    attended = [None] * groups
    for step in range(groups):
        grouped(step, contexts[step][...].reshape(rows, width), attn_ref, 0, attended)
    middle = []
    for n in range(groups):
        inputs = inputs_ref[:, :, n * width : (n + 1) * width].reshape(rows, width)
        middle.append((inputs.astype(jnp.float32) + attended[n]).astype(jnp.bfloat16))
    values = [m.astype(jnp.float32) for m in middle]
    average = sum(jnp.sum(v, axis=1, keepdims=True) for v in values) * (1.0 / size)
    values = [v - average for v in values]
    spread = sum(jnp.sum(v * v, axis=1, keepdims=True) for v in values) * (1.0 / size)
    scale = lax.rsqrt(spread + 1e-05)
    normed = jnp.concatenate(
        [
            (v * scale * gain_ref[:, n * width : (n + 1) * width]).astype(jnp.bfloat16)
            for n, v in enumerate(values)
        ],
        axis=1,
    )
    normed_sides = ordered(normed)
    valid = packed_ref[pl.ds(pl.multiple_of(member * share, share), share), :] >> FIELD
    valid = jnp.concatenate([valid] * (width // LANES), axis=1)
    shift = valid - 1
    first = ((shift & 1) != 0)[None]
    second = ((shift & 2) != 0)[None]
    third = ((shift & 4) != 0)[None]
    conv_term = [None] * groups
    extra = SUB * MELS + 16
    tail_rows = extra + 3 * 16
    for step in range(groups):
        group = (member + groups - step) % groups
        piece = pieces[step]
        small = sum(
            piece[extra + 16 * i : extra + 16 * (i + 1), :].astype(jnp.float32) for i in range(3)
        )
        for h in range(width // LANES):
            cache_f[h] = piece[tail_rows:, h * LANES : (h + 1) * LANES].astype(jnp.float32)
        cached = jnp.concatenate(
            [
                jnp.stack(
                    [cache_f[h, pl.ds(t, share, stride=CONV_CACHE), :] for t in range(CONV_CACHE)]
                )
                for h in range(width // LANES)
            ],
            axis=2,
        )
        glu_value = wide(step, value_ref, 0)
        glu_gate = wide(step, gate_ref, 1)
        gated = (glu_value * jax.nn.sigmoid(glu_gate)).astype(jnp.bfloat16)
        conv_in = jnp.concatenate(
            [
                cached,
                gated.astype(jnp.float32).reshape(FRAMES, share, width),
            ],
            axis=0,
        )
        depthwise = jnp.zeros((FRAMES, share, width), jnp.float32)
        for tap in range(KERNEL):
            depthwise = depthwise + small[tap : tap + 1, :][None] * conv_in[tap : tap + FRAMES]
        shaped = depthwise * small[KERNEL : KERNEL + 1, :][None]
        shaped = shaped + small[KERNEL + 1 : KERNEL + 2, :][None]
        activated = (shaped * jax.nn.sigmoid(shaped)).astype(jnp.bfloat16)
        grouped(step, activated.reshape(rows, width), conv_ref, size // 2, conv_term)
        moved = shift_rows(
            jnp.concatenate([conv_in[1:], conv_in[-1:]], axis=0), first, second, third
        )
        out_ref[group, FRAMES:, :, :] = moved.astype(jnp.bfloat16)
    frame = lax.broadcasted_iota(jnp.int32, (FRAMES, share, width), 0)
    for n in range(groups):
        total = (middle[n].astype(jnp.float32) + conv_term[n]).reshape(FRAMES, share, width)
        out_ref[n, :FRAMES, :, :] = jnp.where(frame < valid[None], total, 0.0).astype(jnp.bfloat16)


    for step, out in enumerate(outs):
        out[...] = out_ref[(member + step) % groups]


def tail(where, groups, *arrays):
    _, share, width = arrays[0].shape
    shape = (FRAMES + CONV_CACHE, share, width)
    vmem = pl.BlockSpec(memory_space=pltpu.VMEM)
    return pl.pallas_call(
        tail_body,
        in_specs=[pl.BlockSpec(memory_space=pltpu.SMEM)] + [vmem] * len(arrays),
        out_specs=[vmem] * groups,
        out_shape=[jax.ShapeDtypeStruct(shape, jnp.bfloat16)] * groups,
        scratch_shapes=[
            pltpu.VMEM((groups,) + shape, jnp.bfloat16),
            pltpu.VMEM((width // LANES, CONV_CACHE * share, LANES), jnp.float32),
        ],
        name="tail",
    )(where, *arrays)


def collect_body(bucket_s, place_s, *refs):
    pieces, slabs, (all_ref, send_ref, rows_f) = refs[:4], refs[4:6], refs[6:]
    member = place_s[0]
    groups = len(pieces)
    frames, share, _ = pieces[0].shape
    heads, _, _ = rows_f.shape
    slots, keep, _ = send_ref.shape
    count = groups * share
    for step, piece in enumerate(pieces):
        start = pl.multiple_of(((member + groups - step) % groups) * share, share)
        all_ref[:frames, pl.ds(start, share), :] = piece[...]
        for h in range(heads):
            for t in range(frames):
                rows_f[h, pl.ds(pl.multiple_of(t * count + start, share), share), :] = piece[
                    t, :, h * LANES : (h + 1) * LANES
                ].astype(jnp.float32)
    for slab in slabs:
        all_ref[frames : frames + FRAMES] = slab[...]
        for h in range(heads):
            rows_f[h, frames * count : (frames + FRAMES) * count, :] = (
                slab[:, :, h * LANES : (h + 1) * LANES]
                .astype(jnp.float32)
                .reshape(FRAMES * count, LANES)
            )
        frames += FRAMES

    def pack(s, carry):
        slot = bucket_s[s]

        @pl.when(slot < slots)
        def _():
            for h in range(heads):
                send_ref[slot, :, h * LANES : (h + 1) * LANES] = rows_f[
                    h, pl.ds(s, keep, stride=count), :
                ].astype(jnp.bfloat16)

        return carry

    lax.fori_loop(0, count, pack, 0)


def collect(bucket, member, pieces, slabs, slots):
    frames = FRAMES + CONV_CACHE + 2 * FRAMES
    keep = -(-frames // 16) * 16
    _, count, width = slabs[0].shape
    smem = pl.BlockSpec(memory_space=pltpu.SMEM)
    vmem = pl.BlockSpec(memory_space=pltpu.VMEM)
    return pl.pallas_call(
        collect_body,
        in_specs=[smem, smem] + [vmem] * 6,
        out_specs=[vmem, vmem],
        out_shape=[
            jax.ShapeDtypeStruct((frames, count, width), jnp.bfloat16),
            jax.ShapeDtypeStruct((slots, keep, width), jnp.bfloat16),
        ],
        scratch_shapes=[pltpu.VMEM((width // LANES, keep * count, LANES), jnp.float32)],
        name="collect",
    )(bucket, member[None], *pieces, *slabs)


def finish_body(
    arrival_s, all_ref, got_ref, _, __, encoded_ref, conv_ref, key_ref, value_ref, rows_f, conv_f
):
    heads = rows_f.shape[0]
    frames, count, _ = all_ref.shape
    keep = got_ref.shape[1]
    for h in range(heads):
        rows_f[h, : frames * count, :] = (
            all_ref[:, :, h * LANES : (h + 1) * LANES]
            .astype(jnp.float32)
            .reshape(frames * count, LANES)
        )

    def fetch(s, carry):
        slot = arrival_s[s]

        @pl.when(slot >= 0)
        def _():
            for h in range(heads):
                rows_f[h, pl.ds(s, keep, stride=count), :] = got_ref[
                    slot, :, h * LANES : (h + 1) * LANES
                ].astype(jnp.float32)

        return carry

    lax.fori_loop(0, count, fetch, 0)
    ends = FRAMES + CONV_CACHE
    for h in range(heads):
        lanes = slice(h * LANES, (h + 1) * LANES)
        for start, out in ((0, encoded_ref), (ends, key_ref), (ends + FRAMES, value_ref)):
            rows = rows_f[h, start * count : (start + FRAMES) * count, :]
            out[:, :, lanes] = rows.reshape(FRAMES, count, LANES).astype(jnp.bfloat16)
        for t in range(CONV_CACHE):
            at = (FRAMES + t) * count
            conv_f[pl.ds(t, count, stride=CONV_CACHE), :] = rows_f[h, at : at + count, :]
        conv_ref[:, :, lanes] = (
            conv_f[...].reshape(count, CONV_CACHE, LANES).astype(jnp.bfloat16)
        )


def finish(arrival, everything, received, key_done, value_done):
    _, count, width = everything.shape
    keep = received.shape[1]
    smem = pl.BlockSpec(memory_space=pltpu.SMEM)
    vmem = pl.BlockSpec(memory_space=pltpu.VMEM)
    kept = pl.BlockSpec(memory_space=pl.ANY)
    slab = pl.BlockSpec((FRAMES, count, width), lambda i: (CACHE // FRAMES - 1, 0, 0))
    return pl.pallas_call(
        finish_body,
        grid=(1,),
        in_specs=[smem, vmem, vmem, kept, kept],
        out_specs=[vmem, vmem, slab, slab],
        out_shape=[
            jax.ShapeDtypeStruct((FRAMES, count, width), jnp.bfloat16),
            jax.ShapeDtypeStruct((count, CONV_CACHE, width), jnp.bfloat16),
            jax.ShapeDtypeStruct(key_done.shape, jnp.bfloat16),
            jax.ShapeDtypeStruct(value_done.shape, jnp.bfloat16),
        ],
        scratch_shapes=[
            pltpu.VMEM((width // LANES, keep * count, LANES), jnp.float32),
            pltpu.VMEM((CONV_CACHE * count, LANES), jnp.float32),
        ],
        input_output_aliases={3: 2, 4: 3},
        name="finish",
    )(arrival, everything, received, key_done, value_done)


def swap(chunks, member, count):
    pieces = [lax.dynamic_index_in_dim(chunks, member, 0, False)]
    for step in range(1, count):
        chunk = lax.dynamic_index_in_dim(chunks, (member + step) % count, 0, False)
        pieces.append(toward(chunk, step, count))
    return pieces


def toward(array, steps, count):
    return lax.ppermute(array, "enc", [(i, (i + steps) % count) for i in range(count)])


def on_device(
    spectra,
    sub_weight,
    sub_bias,
    key_cache,
    value_cache,
    conv_cache,
    new_slot,
    old_slot,
    valid_new,
    cache_fill,
    ln1_gain,
    w_query,
    w_key,
    w_value,
    w_attn_out,
    ln2_gain,
    w_glu_value,
    w_glu_gate,
    depth_kernel,
    norm_scale,
    norm_shift,
    w_conv_out,
):
    peer_count = lax.axis_size("front")
    own_index = lax.axis_index("front")
    member = lax.axis_index("enc")
    stream_count = spectra.shape[0]
    local_width = w_query.shape[1]
    slots = peer_count * CAP
    both = valid_new * (1 << FIELD) + cache_fill
    bucket, arrival, asked = route(own_index, new_slot, old_slot, both, slots)
    told = lax.all_to_all(asked, "front", split_axis=0, concat_axis=0, tiled=True)
    key_rows = key_cache.transpose(1, 0, 2)
    value_rows = value_cache.transpose(1, 0, 2)
    leaving_rows = pack_rows(bucket, key_rows, value_rows, slots)
    received = lax.all_to_all(leaving_rows, "front", split_axis=0, concat_axis=0, tiled=True)
    groups = lax.axis_size("enc")
    taps = SUB * MELS
    share = stream_count // groups
    small = jnp.concatenate(
        [depth_kernel, norm_scale[None], norm_shift[None], jnp.zeros((5, local_width), jnp.float32)],
        axis=0,
    )
    small_high = lax.reduce_precision(small, 8, 7)
    small_rest = small - small_high
    small_mid = lax.reduce_precision(small_rest, 8, 7)
    common = [sub_weight, jnp.broadcast_to(sub_bias[None, :], (16, local_width))] + [
        part.astype(jnp.bfloat16) for part in (small_high, small_mid, small_rest - small_mid)
    ]
    chunks = conv_cache.reshape(groups, share * CONV_CACHE, local_width)

    def payload(step):
        chunk = lax.dynamic_index_in_dim(chunks, (member + step) % groups, 0, False)
        return jnp.concatenate(common + [chunk], axis=0)

    pieces = [payload(0)] + [toward(payload(k), k, groups) for k in range(1, groups)]

    core = own_index % 2
    half = local_width // 2

    def core_rows(matrix):
        count = matrix.shape[0] // 2
        return lax.dynamic_slice_in_dim(matrix, core * count, count, 0)

    def blocks(matrix):
        return (
            core_rows(matrix)
            .reshape(half, groups, local_width)
            .transpose(1, 0, 2)
            .reshape(groups * half, local_width)
        )

    stack = jnp.concatenate(
        [blocks(w_attn_out), blocks(w_conv_out), core_rows(w_glu_value), core_rows(w_glu_gate)],
        axis=0,
    )
    middle_row = stack.shape[0] // 2

    def other_core(array):
        return lax.ppermute(array, "front", [(i, i ^ 1) for i in range(peer_count)])

    near = toward(stack, 1, groups)
    after = toward(stack, -1, groups)
    far_low = toward(near[:middle_row], 1, groups)
    far_high = toward(after[middle_row:], -1, groups)
    near_other = other_core(near)
    after_other = other_core(after)
    far_low_other = other_core(far_low)
    far_high_other = other_core(far_high)
    frames = spectra.transpose(1, 2, 0).reshape(FRAMES, taps, stream_count)
    queries, key_new, value_new, inputs = head(
        member, frames, pieces, ln1_gain, (w_query, w_key, w_value)
    )
    context, key_slab, value_slab, packed = attend(
        bucket, both, told, queries, key_new, value_new, key_rows, value_rows, groups
    )
    context = swap(context, member, groups)
    ended = tail(
        jnp.stack([member, core]),
        groups,
        *context,
        *pieces,
        inputs,
        ln2_gain[None, :],
        packed,
        w_attn_out,
        w_conv_out,
        w_glu_value,
        w_glu_gate,
        near,
        near_other,
        far_low,
        far_low_other,
        after,
        after_other,
        near,
        near_other,
        far_high,
        far_high_other,
        after,
        after_other,
    )
    ended = [ended[0]] + [toward(ended[k], k, groups) for k in range(1, groups)]
    everything, leaving_end = collect(bucket, member, ended, (key_slab, value_slab), slots)
    received_end = lax.all_to_all(leaving_end, "front", split_axis=0, concat_axis=0, tiled=True)
    key_done, value_done = place(arrival, valid_new, received, key_rows, value_rows)
    encoded, conv_out, key_done, value_done = finish(
        arrival, everything, received_end, key_done, value_done
    )
    return (
        encoded.transpose(1, 0, 2),
        key_done.transpose(1, 0, 2),
        value_done.transpose(1, 0, 2),
        conv_out,
    )


def solution(mesh):
    in_specs = (
        P("front", None, None),
        P(None, "enc"),
        P("enc"),
        P("front", None, "enc"),
        P("front", None, "enc"),
        P("front", None, "enc"),
        P("front"),
        P("front"),
        P("front"),
        P("front"),
        P(),
        P(None, "enc"),
        P(None, "enc"),
        P(None, "enc"),
        P("enc", None),
        P(),
        P(None, "enc"),
        P(None, "enc"),
        P(None, "enc"),
        P("enc"),
        P("enc"),
        P("enc", None),
    )
    out_specs = (
        P("front", None, "enc"),
        P("front", None, "enc"),
        P("front", None, "enc"),
        P("front", None, "enc"),
    )

    return jax.shard_map(
        on_device, mesh=mesh, in_specs=in_specs, out_specs=out_specs, check_vma=False
    )
```

```python
import math

import jax
import jax.numpy as jnp
from jax import lax
from jax.experimental import pallas as pl
from jax.experimental.pallas import tpu as pltpu
from jax.sharding import PartitionSpec as P


MELS = 80
KERNEL = 9
SUB = 8
FRAMES = 7
CACHE = 70
CAP = 2
HEAD = 128
CONV_CACHE = 8
LANES = 128
BLOCK = 16
SPAN = 80
KEEP = 72
CHUNK = 10
FIELD = 7

masked_score = -1e30


def prepare_body(
    place_s,
    new_ref,
    old_ref,
    both_ref,
    weight_ref,
    bias_ref,
    kernel_ref,
    scale_ref,
    shift_ref,
    cache_ref,
    attn_ref,
    conv_ref,
    value_ref,
    gate_ref,
    *refs,
):
    payloads, (bucket_ref, arrival_ref, out_ref, in_ref, asked_ref, stack_ref, small) = (
        refs[:4],
        refs[4:],
    )
    member, own = place_s[0], place_s[2]
    groups = len(payloads)
    taps, width = weight_ref.shape
    slots, count = asked_ref.shape
    bits = count.bit_length() - 1

    small[:KERNEL, :] = kernel_ref[...]
    small[KERNEL : KERNEL + 1, :] = scale_ref[...]
    small[KERNEL + 1 : KERNEL + 2, :] = shift_ref[...]
    small[KERNEL + 2 :, :] = jnp.zeros((16 - KERNEL - 2, width), jnp.float32)
    rest = small[...]
    bias = jnp.broadcast_to(bias_ref[...].astype(jnp.float32), (16, width)).astype(jnp.bfloat16)
    parts = []
    for _ in range(3):
        part = rest.astype(jnp.bfloat16)
        parts.append(part)
        rest = rest - part.astype(jnp.float32)
    for step, payload in enumerate(payloads):
        payload[:taps, :] = weight_ref[...]
        payload[taps : taps + 16, :] = bias
        for i, part in enumerate(parts):
            payload[taps + 16 * (i + 1) : taps + 16 * (i + 2), :] = part
        payload[taps + 64 :, :] = cache_ref[(member + step) % groups]

    half = attn_ref.shape[0]
    for start, source in ((0, attn_ref), (groups * half, conv_ref)):
        for n in range(groups):
            at = start + n * half
            stack_ref[at : at + half, :] = source[:, n * width : (n + 1) * width]
    at = 2 * groups * half
    stack_ref[at : at + value_ref.shape[0], :] = value_ref[...]
    stack_ref[at + value_ref.shape[0] :, :] = gate_ref[...]

    def column(row):
        return jnp.transpose(jnp.broadcast_to(row, (count, count)))

    def ranked(group_column, group_row, before):
        same = jnp.where((group_column == group_row) & before, 1.0, 0.0)
        return jnp.sum(same, axis=0, keepdims=True).astype(jnp.int32)

    first = lax.broadcasted_iota(jnp.int32, (count, count), 0)
    second = lax.broadcasted_iota(jnp.int32, (count, count), 1)

    def inverse(row):
        hit = jnp.where(column(row) == second, (first + 1).astype(jnp.float32), 0.0)
        return jnp.sum(hit, axis=0, keepdims=True).astype(jnp.int32) - 1

    target = new_ref[...] >> bits
    position = ranked(column(target), target, first < second)
    bucket = jnp.where(target != own, target * CAP + position, slots)
    bucket_ref[...] = bucket
    out_ref[...] = inverse(bucket)
    old_row = old_ref[...]
    old_column = column(old_row)
    source = old_row >> bits
    position = ranked(old_column >> bits, source, old_column < old_row)
    arrival = jnp.where(source == own, -1, source * CAP + position)
    arrival_ref[...] = arrival
    in_ref[...] = inverse(arrival)
    slot = lax.broadcasted_iota(jnp.int32, (slots, count), 0)
    hit = jnp.where(arrival == slot, both_ref[...].astype(jnp.float32), 0.0)
    asked = jnp.sum(hit, axis=1, keepdims=True).astype(jnp.int32)
    asked_ref[...] = jnp.broadcast_to(asked, (slots, count))


def prepare(where, rows, sub, conv, chunks, columns, tall, slots):
    count = rows[0].shape[0]
    groups, chunk_rows, width = chunks.shape
    taps = sub[0].shape[0]
    whole = [r[None] for r in rows] + [sub[0], sub[1][None], conv[0], conv[1][None], conv[2][None]]

    def full(array):
        zeros = (0,) * array.ndim
        return pl.BlockSpec(array.shape, lambda i, place_s: zeros)

    def my_half(array):
        return pl.BlockSpec(
            (array.shape[0] // 2, array.shape[1]), lambda i, place_s: (place_s[1], 0)
        )

    row = jax.ShapeDtypeStruct((1, count), jnp.int32)
    payload = jax.ShapeDtypeStruct((taps + 64 + chunk_rows, width), jnp.bfloat16)
    shapes = [payload] * groups + [row] * 4
    shapes.append(jax.ShapeDtypeStruct((slots, count), jnp.int32))
    shapes.append(jax.ShapeDtypeStruct((2 * groups * width, width), jnp.bfloat16))
    outs = pl.pallas_call(
        prepare_body,
        grid_spec=pltpu.PrefetchScalarGridSpec(
            num_scalar_prefetch=1,
            grid=(1,),
            in_specs=[full(a) for a in whole]
            + [full(chunks)]
            + [my_half(a) for a in columns + tall],
            out_specs=[full(a) for a in shapes],
            scratch_shapes=[pltpu.VMEM((16, width), jnp.float32)],
        ),
        out_shape=shapes,
        name="prepare",
    )(where, *whole, chunks, *columns, *tall)
    return outs[:groups], [r[0] for r in outs[groups : groups + 4]], outs[-2], outs[-1]


def shift_rows(rows, first, second, third):
    rows = jnp.where(first, rows[1:], rows[:-1])
    rows = jnp.where(second, rows[2:], rows[:-2])
    return jnp.where(third, rows[4:], rows[:-4])


def attend_body(
    bucket_s,
    both_s,
    told_ref,
    query_ref,
    key_new_ref,
    value_new_ref,
    key_ref,
    value_ref,
    context_ref,
    key_out_ref,
    value_out_ref,
    packed_ref,
):
    base = pl.program_id(0) * BLOCK
    slots = told_ref.shape[0]
    for s in range(BLOCK):
        slot = bucket_s[base + s]
        told = told_ref[pl.ds(jnp.minimum(slot, slots - 1), 1), :]
        packed_ref[s : s + 1, :] = jnp.where(
            slot < slots, told, jnp.full_like(told, both_s[base + s])
        )
    packed = packed_ref[...]
    width = query_ref.shape[2]
    heads = width // LANES
    span = SPAN * BLOCK
    valid = packed >> FIELD
    low = (CACHE - (packed[:, :1] & ((1 << FIELD) - 1))) * BLOCK
    high = (CACHE + valid[:, :1]) * BLOCK
    offset = lax.broadcasted_iota(jnp.int32, (BLOCK, span), 1) - lax.broadcasted_iota(
        jnp.int32, (BLOCK, span), 0
    )
    allowed = ((offset & (BLOCK - 1)) == 0) & (offset >= low) & (offset < high)
    bias = jnp.where(allowed, 0.0, masked_score)[None]
    padding = jnp.zeros(((SPAN - CACHE - FRAMES) * BLOCK, LANES), jnp.bfloat16)

    def joined(old_ref, new_ref, lanes):
        return jnp.concatenate(
            [
                old_ref[:, :, lanes].reshape(CACHE * BLOCK, LANES),
                new_ref[:, :, lanes].reshape(FRAMES * BLOCK, LANES),
                padding,
            ],
            axis=0,
        )

    for h in range(heads):
        lanes = slice(h * LANES, (h + 1) * LANES)
        scores = lax.dot_general(
            query_ref[:, :, lanes].reshape(FRAMES * BLOCK, LANES),
            joined(key_ref, key_new_ref, lanes),
            (((1,), (1,)), ((), ())),
            preferred_element_type=jnp.float32,
        )
        scores = scores.reshape(FRAMES, BLOCK, span) * (1.0 / math.sqrt(HEAD)) + bias
        exponent = jnp.exp(scores - jnp.max(scores, axis=2, keepdims=True))
        weights = exponent * (1.0 / jnp.sum(exponent, axis=2, keepdims=True))
        context = lax.dot_general(
            weights.astype(jnp.bfloat16).reshape(FRAMES * BLOCK, span),
            joined(value_ref, value_new_ref, lanes),
            (((1,), (0,)), ((), ())),
            preferred_element_type=jnp.float32,
        )
        context_ref[0, :, :, lanes] = context.reshape(FRAMES, BLOCK, LANES).astype(jnp.bfloat16)

    shift = valid - 1
    first = ((shift & 1) != 0)[None]
    second = ((shift & 2) != 0)[None]
    third = ((shift & 4) != 0)[None]
    edge = CACHE - FRAMES
    for old_ref, new_ref, out_ref in (
        (key_ref, key_new_ref, key_out_ref),
        (value_ref, value_new_ref, value_out_ref),
    ):
        for h in range(heads):
            lanes = slice(h * LANES, (h + 1) * LANES)
            old = old_ref[edge + 1 :, :, lanes].astype(jnp.float32)
            new = new_ref[:, :, lanes].astype(jnp.float32)
            rows = jnp.concatenate([old, new, new[:1]], axis=0)
            out_ref[:, :, lanes] = shift_rows(rows, first, second, third).astype(jnp.bfloat16)


def attend(bucket, both, told, queries, key_new, value_new, key_cache, value_cache, groups):
    stream_count = key_cache.shape[1]
    width = key_cache.shape[2]

    def block(rows):
        return pl.BlockSpec((rows, BLOCK, width), lambda i, *_: (0, i, 0))

    per_group = stream_count // groups // BLOCK
    context = pl.BlockSpec(
        (1, FRAMES, BLOCK, width), lambda i, *_: (i // per_group, 0, i % per_group, 0)
    )
    slab = jax.ShapeDtypeStruct((FRAMES, stream_count, width), jnp.bfloat16)
    return pl.pallas_call(
        attend_body,
        grid_spec=pltpu.PrefetchScalarGridSpec(
            num_scalar_prefetch=2,
            grid=(stream_count // BLOCK,),
            in_specs=[pl.BlockSpec(told.shape, lambda i, *_: (0, 0))]
            + [block(FRAMES)] * 3
            + [block(CACHE)] * 2,
            out_specs=[
                context,
                block(FRAMES),
                block(FRAMES),
                pl.BlockSpec((BLOCK, LANES), lambda i, *_: (i, 0)),
            ],
        ),
        out_shape=[
            jax.ShapeDtypeStruct((groups, FRAMES, stream_count // groups, width), jnp.bfloat16),
            slab,
            slab,
            jax.ShapeDtypeStruct((stream_count, LANES), jnp.int32),
        ],
        name="attend",
    )(bucket, both, told, queries, key_new, value_new, key_cache, value_cache)


def pack_body(slot_s, key_ref, value_ref, send_ref, rows_f):
    base = pl.program_id(0) * BLOCK
    heads = rows_f.shape[1]
    slots = send_ref.shape[0]
    for kind, src in enumerate((key_ref, value_ref)):
        for h in range(heads):
            rows_f[kind, h, : CACHE * BLOCK, :] = (
                src[:, :, h * LANES : (h + 1) * LANES]
                .astype(jnp.float32)
                .reshape(CACHE * BLOCK, LANES)
            )

    def pack(s, carry):
        slot = slot_s[base + s]

        @pl.when(slot < slots)
        def _():
            for kind in range(2):
                for h in range(heads):
                    send_ref[slot, kind, :, h * LANES : (h + 1) * LANES] = rows_f[
                        kind, h, pl.ds(s, KEEP, stride=BLOCK), :
                    ].astype(jnp.bfloat16)

        return carry

    lax.fori_loop(0, BLOCK, pack, 0)


def pack_rows(bucket, key_cache, value_cache, slots):
    stream_count = key_cache.shape[1]
    width = key_cache.shape[2]
    block = pl.BlockSpec((CACHE, BLOCK, width), lambda i, *_: (0, i, 0))
    return pl.pallas_call(
        pack_body,
        grid_spec=pltpu.PrefetchScalarGridSpec(
            num_scalar_prefetch=1,
            grid=(stream_count // BLOCK,),
            in_specs=[block, block],
            out_specs=pl.BlockSpec((slots, 2, KEEP, width), lambda i, *_: (0, 0, 0, 0)),
            scratch_shapes=[
                pltpu.VMEM((2, width // HEAD, KEEP * BLOCK, LANES), jnp.float32)
            ],
        ),
        out_shape=jax.ShapeDtypeStruct((slots, 2, KEEP, width), jnp.bfloat16),
        name="pack",
    )(bucket, key_cache, value_cache)


def place_body(
    arrival_s, got_ref, valid_ref, key_ref, value_ref, key_out_ref, value_out_ref, rows_f
):
    base = pl.program_id(0) * BLOCK
    heads = rows_f.shape[1]
    for kind, src in enumerate((key_ref, value_ref)):
        for h in range(heads):
            lanes = slice(h * LANES, (h + 1) * LANES)
            for start in range(0, CACHE, CHUNK):
                rows_f[kind, h, start * BLOCK : (start + CHUNK) * BLOCK, :] = (
                    src[start : start + CHUNK, :, lanes]
                    .astype(jnp.float32)
                    .reshape(CHUNK * BLOCK, LANES)
                )

    def fetch(s, carry):
        slot = arrival_s[base + s]

        @pl.when(slot >= 0)
        def _():
            for kind in range(2):
                for h in range(heads):
                    rows_f[kind, h, pl.ds(s, KEEP, stride=BLOCK), :] = got_ref[
                        slot, kind, :, h * LANES : (h + 1) * LANES
                    ].astype(jnp.float32)

        return carry

    lax.fori_loop(0, BLOCK, fetch, 0)
    shift = valid_ref[...] - 1
    first = ((shift & 1) != 0)[None]
    second = ((shift & 2) != 0)[None]
    third = ((shift & 4) != 0)[None]
    edge = CACHE - FRAMES
    for kind, dst in enumerate((key_out_ref, value_out_ref)):
        for h in range(heads):
            lanes = slice(h * LANES, (h + 1) * LANES)
            for start in range(0, edge, 9):
                rows = rows_f[kind, h, (start + 1) * BLOCK : (start + 17) * BLOCK, :]
                rows = shift_rows(rows.reshape(16, BLOCK, LANES), first, second, third)
                dst[start : start + 9, :, lanes] = rows.astype(jnp.bfloat16)
            dst[edge:, :, lanes] = jnp.zeros((FRAMES, BLOCK, LANES), jnp.bfloat16)


def place(arrival, valid_new, received, key_rows, value_rows):
    stream_count = key_rows.shape[1]
    width = key_rows.shape[2]
    heads = width // HEAD
    slots = received.shape[0]
    block = pl.BlockSpec((CACHE, BLOCK, width), lambda i, *_: (0, i, 0))
    shape = jax.ShapeDtypeStruct((CACHE, stream_count, width), jnp.bfloat16)
    return pl.pallas_call(
        place_body,
        grid_spec=pltpu.PrefetchScalarGridSpec(
            num_scalar_prefetch=1,
            grid=(stream_count // BLOCK,),
            in_specs=[
                pl.BlockSpec((slots, 2, KEEP, width), lambda i, *_: (0, 0, 0, 0)),
                pl.BlockSpec((BLOCK, LANES), lambda i, *_: (i, 0)),
                block,
                block,
            ],
            out_specs=[block, block],
            scratch_shapes=[pltpu.VMEM((2, heads, KEEP * BLOCK, LANES), jnp.float32)],
        ),
        out_shape=[shape, shape],
        name="place",
    )(
        arrival,
        received,
        jnp.broadcast_to(valid_new[:, None], (stream_count, LANES)),
        key_rows,
        value_rows,
    )


def head_body(
    place_s, frames_ref, own_ref, near_ref, far_ref, next_ref, gain_ref, *rest
):
    weights, outs, inputs_ref, flat, raw, normed = rest[:3], rest[3:6], *rest[6:]
    member = place_s[0]
    groups = raw.shape[0]
    width = raw.shape[2]
    count, taps, streams = frames_ref.shape
    for t in range(count):
        flat[t * streams : (t + 1) * streams, :] = jnp.transpose(frames_ref[t])
    for offset, piece in enumerate((own_ref, near_ref, far_ref, next_ref)):
        total = jnp.dot(flat[...], piece[:taps, :], preferred_element_type=jnp.float32)
        total = total + piece[taps : taps + 16, :].astype(jnp.float32)[:1]
        raw[(member + groups - offset) % groups] = total.astype(jnp.bfloat16)
    model_width = groups * width
    share = inputs_ref.shape[1]
    for t in range(count):
        lines = slice(t * streams, (t + 1) * streams)
        values = [raw[g, lines, :].astype(jnp.float32) for g in range(groups)]
        average = sum(jnp.sum(v, axis=1, keepdims=True) for v in values) * (1.0 / model_width)
        values = [v - average for v in values]
        spread = sum(jnp.sum(v * v, axis=1, keepdims=True) for v in values) * (1.0 / model_width)
        scale = lax.rsqrt(spread + 1e-05)
        for g, v in enumerate(values):
            columns = slice(g * width, (g + 1) * width)
            normed[lines, columns] = (v * scale * gain_ref[:, columns]).astype(jnp.bfloat16)
            start = pl.multiple_of(t * streams + member * share, share)
            inputs_ref[t, :, columns] = raw[g, pl.ds(start, share), :]
    for matrix, out in zip(weights, outs):
        product = jnp.dot(normed[...], matrix[...], preferred_element_type=jnp.float32)
        out[...] = product.astype(jnp.bfloat16).reshape(count, streams, width)


def head(where, frames, pieces, gain, matrices):
    count, taps, streams = frames.shape
    width = matrices[0].shape[1]
    groups = len(pieces)

    def whole(array):
        zeros = (0,) * array.ndim
        return pl.BlockSpec(array.shape, lambda i, *_: zeros)

    gain = gain[None, :]
    shapes = [jax.ShapeDtypeStruct((count, streams, width), jnp.bfloat16)] * 3
    shapes.append(
        jax.ShapeDtypeStruct((count, streams // groups, groups * width), jnp.bfloat16)
    )
    return pl.pallas_call(
        head_body,
        grid_spec=pltpu.PrefetchScalarGridSpec(
            num_scalar_prefetch=1,
            grid=(1,),
            in_specs=[whole(frames)]
            + [pl.BlockSpec((taps + 16, width), lambda i, *_: (0, 0))] * groups
            + [whole(gain)]
            + [whole(w) for w in matrices],
            out_specs=[whole(a) for a in shapes],
            scratch_shapes=[
                pltpu.VMEM((count * streams, taps), jnp.bfloat16),
                pltpu.VMEM((groups, count * streams, width), jnp.bfloat16),
                pltpu.VMEM((count * streams, groups * width), jnp.bfloat16),
            ],
        ),
        out_shape=shapes,
        name="head",
    )(where, frames, *pieces, gain, *matrices)


def tail_body(place_s, *refs):
    contexts, pieces, rest = refs[:4], refs[4:8], refs[8:]
    inputs_ref, gain_ref, packed_ref = rest[:3]
    attn_ref, conv_ref, value_ref, gate_ref = rest[3:7]
    low_refs, high_refs, outs = rest[7:13], rest[13:19], rest[19:23]
    out_ref, cache_f = rest[23:]
    member = place_s[0]
    front_half = place_s[1] == 0
    groups = len(contexts)
    _, share, width = contexts[0].shape
    rows = FRAMES * share
    size = groups * width
    half = width // 2

    def ordered(operand):
        middle_lane = operand.shape[1] // 2
        low, high = operand[:, :middle_lane], operand[:, middle_lane:]
        return jnp.where(front_half, low, high), jnp.where(front_half, high, low)

    def dot(left, right):
        return jnp.dot(left, right, preferred_element_type=jnp.float32)

    def grouped(step, operand, own_ref, start, sums):
        sides = ordered(operand)
        for n in range(groups):
            if step == 0:
                part = dot(operand, own_ref[:, n * width : (n + 1) * width])
            else:
                at = start + n * half
                part = sum(
                    dot(side, low_refs[2 * (step - 1) + i][at : at + half, :])
                    for i, side in enumerate(sides)
                )
            part = part.astype(jnp.bfloat16).astype(jnp.float32)
            sums[n] = part if sums[n] is None else sums[n] + part

    def wide(step, own_ref, order):
        if step == 0:
            return dot(normed, own_ref[...])
        at = high_starts[step - 1] + order * (size // 2)
        return sum(
            dot(side, high_refs[2 * (step - 1) + i][at : at + size // 2, :])
            for i, side in enumerate(normed_sides)
        )

    high_starts = (size, 0, size)
    attended = [None] * groups
    for step in range(groups):
        grouped(step, contexts[step][...].reshape(rows, width), attn_ref, 0, attended)
    middle = []
    for n in range(groups):
        inputs = inputs_ref[:, :, n * width : (n + 1) * width].reshape(rows, width)
        middle.append((inputs.astype(jnp.float32) + attended[n]).astype(jnp.bfloat16))
    values = [m.astype(jnp.float32) for m in middle]
    average = sum(jnp.sum(v, axis=1, keepdims=True) for v in values) * (1.0 / size)
    values = [v - average for v in values]
    spread = sum(jnp.sum(v * v, axis=1, keepdims=True) for v in values) * (1.0 / size)
    scale = lax.rsqrt(spread + 1e-05)
    normed = jnp.concatenate(
        [
            (v * scale * gain_ref[:, n * width : (n + 1) * width]).astype(jnp.bfloat16)
            for n, v in enumerate(values)
        ],
        axis=1,
    )
    normed_sides = ordered(normed)
    valid = packed_ref[pl.ds(pl.multiple_of(member * share, share), share), :] >> FIELD
    valid = jnp.concatenate([valid] * (width // LANES), axis=1)
    shift = valid - 1
    first = ((shift & 1) != 0)[None]
    second = ((shift & 2) != 0)[None]
    third = ((shift & 4) != 0)[None]
    conv_term = [None] * groups
    extra = SUB * MELS + 16
    tail_rows = extra + 3 * 16
    for step in range(groups):
        group = (member + groups - step) % groups
        piece = pieces[step]
        small = sum(
            piece[extra + 16 * i : extra + 16 * (i + 1), :].astype(jnp.float32) for i in range(3)
        )
        for h in range(width // LANES):
            cache_f[h] = piece[tail_rows:, h * LANES : (h + 1) * LANES].astype(jnp.float32)
        cached = jnp.concatenate(
            [
                jnp.stack(
                    [cache_f[h, pl.ds(t, share, stride=CONV_CACHE), :] for t in range(CONV_CACHE)]
                )
                for h in range(width // LANES)
            ],
            axis=2,
        )
        glu_value = wide(step, value_ref, 0)
        glu_gate = wide(step, gate_ref, 1)
        gated = (glu_value * jax.nn.sigmoid(glu_gate)).astype(jnp.bfloat16)
        conv_in = jnp.concatenate(
            [
                cached,
                gated.astype(jnp.float32).reshape(FRAMES, share, width),
            ],
            axis=0,
        )
        depthwise = jnp.zeros((FRAMES, share, width), jnp.float32)
        for tap in range(KERNEL):
            depthwise = depthwise + small[tap : tap + 1, :][None] * conv_in[tap : tap + FRAMES]
        shaped = depthwise * small[KERNEL : KERNEL + 1, :][None]
        shaped = shaped + small[KERNEL + 1 : KERNEL + 2, :][None]
        activated = (shaped * jax.nn.sigmoid(shaped)).astype(jnp.bfloat16)
        grouped(step, activated.reshape(rows, width), conv_ref, size // 2, conv_term)
        moved = shift_rows(
            jnp.concatenate([conv_in[1:], conv_in[-1:]], axis=0), first, second, third
        )
        out_ref[group, FRAMES:, :, :] = moved.astype(jnp.bfloat16)
    frame = lax.broadcasted_iota(jnp.int32, (FRAMES, share, width), 0)
    for n in range(groups):
        total = (middle[n].astype(jnp.float32) + conv_term[n]).reshape(FRAMES, share, width)
        out_ref[n, :FRAMES, :, :] = jnp.where(frame < valid[None], total, 0.0).astype(jnp.bfloat16)


    for step, out in enumerate(outs):
        out[...] = out_ref[(member + step) % groups]


def tail(where, groups, *arrays):
    _, share, width = arrays[0].shape
    shape = (FRAMES + CONV_CACHE, share, width)
    vmem = pl.BlockSpec(memory_space=pltpu.VMEM)
    return pl.pallas_call(
        tail_body,
        in_specs=[pl.BlockSpec(memory_space=pltpu.SMEM)] + [vmem] * len(arrays),
        out_specs=[vmem] * groups,
        out_shape=[jax.ShapeDtypeStruct(shape, jnp.bfloat16)] * groups,
        scratch_shapes=[
            pltpu.VMEM((groups,) + shape, jnp.bfloat16),
            pltpu.VMEM((width // LANES, CONV_CACHE * share, LANES), jnp.float32),
        ],
        name="tail",
    )(where, *arrays)


def collect_body(leaving_s, place_s, *refs):
    pieces, slabs, (all_ref, send_ref, rows_f) = refs[:4], refs[4:6], refs[6:]
    member = place_s[0]
    groups = len(pieces)
    frames, share, _ = pieces[0].shape
    heads, _, _ = rows_f.shape
    slots, keep, _ = send_ref.shape
    count = groups * share
    for step, piece in enumerate(pieces):
        start = pl.multiple_of(((member + groups - step) % groups) * share, share)
        all_ref[:frames, pl.ds(start, share), :] = piece[...]
        for h in range(heads):
            for t in range(frames):
                rows_f[h, pl.ds(pl.multiple_of(t * count + start, share), share), :] = piece[
                    t, :, h * LANES : (h + 1) * LANES
                ].astype(jnp.float32)
    for slab in slabs:
        all_ref[frames : frames + FRAMES] = slab[...]
        for h in range(heads):
            rows_f[h, frames * count : (frames + FRAMES) * count, :] = (
                slab[:, :, h * LANES : (h + 1) * LANES]
                .astype(jnp.float32)
                .reshape(FRAMES * count, LANES)
            )
        frames += FRAMES

    def pack(slot, carry):
        s = leaving_s[slot]

        @pl.when(s >= 0)
        def _():
            for h in range(heads):
                send_ref[slot, :, h * LANES : (h + 1) * LANES] = rows_f[
                    h, pl.ds(s, keep, stride=count), :
                ].astype(jnp.bfloat16)

        return carry

    lax.fori_loop(0, slots, pack, 0)


def collect(leaving, where, pieces, slabs, slots):
    frames = FRAMES + CONV_CACHE + 2 * FRAMES
    keep = -(-frames // 16) * 16
    _, count, width = slabs[0].shape
    smem = pl.BlockSpec(memory_space=pltpu.SMEM)
    vmem = pl.BlockSpec(memory_space=pltpu.VMEM)
    return pl.pallas_call(
        collect_body,
        in_specs=[smem, smem] + [vmem] * 6,
        out_specs=[vmem, vmem],
        out_shape=[
            jax.ShapeDtypeStruct((frames, count, width), jnp.bfloat16),
            jax.ShapeDtypeStruct((slots, keep, width), jnp.bfloat16),
        ],
        scratch_shapes=[pltpu.VMEM((width // LANES, keep * count, LANES), jnp.float32)],
        name="collect",
    )(leaving, where, *pieces, *slabs)


def finish_body(
    coming_s, all_ref, got_ref, _, __, encoded_ref, conv_ref, key_ref, value_ref, rows_f, conv_f
):
    heads = rows_f.shape[0]
    frames, count, _ = all_ref.shape
    keep = got_ref.shape[1]
    for h in range(heads):
        rows_f[h, : frames * count, :] = (
            all_ref[:, :, h * LANES : (h + 1) * LANES]
            .astype(jnp.float32)
            .reshape(frames * count, LANES)
        )

    def fetch(slot, carry):
        s = coming_s[slot]

        @pl.when(s >= 0)
        def _():
            for h in range(heads):
                rows_f[h, pl.ds(s, keep, stride=count), :] = got_ref[
                    slot, :, h * LANES : (h + 1) * LANES
                ].astype(jnp.float32)

        return carry

    lax.fori_loop(0, got_ref.shape[0], fetch, 0)
    ends = FRAMES + CONV_CACHE
    for h in range(heads):
        lanes = slice(h * LANES, (h + 1) * LANES)
        for start, out in ((0, encoded_ref), (ends, key_ref), (ends + FRAMES, value_ref)):
            rows = rows_f[h, start * count : (start + FRAMES) * count, :]
            out[:, :, lanes] = rows.reshape(FRAMES, count, LANES).astype(jnp.bfloat16)
        for t in range(CONV_CACHE):
            at = (FRAMES + t) * count
            conv_f[pl.ds(t, count, stride=CONV_CACHE), :] = rows_f[h, at : at + count, :]
        conv_ref[:, :, lanes] = (
            conv_f[...].reshape(count, CONV_CACHE, LANES).astype(jnp.bfloat16)
        )


def finish(coming, everything, received, key_done, value_done):
    _, count, width = everything.shape
    keep = received.shape[1]
    smem = pl.BlockSpec(memory_space=pltpu.SMEM)
    vmem = pl.BlockSpec(memory_space=pltpu.VMEM)
    kept = pl.BlockSpec(memory_space=pl.ANY)
    slab = pl.BlockSpec((FRAMES, count, width), lambda i: (CACHE // FRAMES - 1, 0, 0))
    return pl.pallas_call(
        finish_body,
        grid=(1,),
        in_specs=[smem, vmem, vmem, kept, kept],
        out_specs=[vmem, vmem, slab, slab],
        out_shape=[
            jax.ShapeDtypeStruct((FRAMES, count, width), jnp.bfloat16),
            jax.ShapeDtypeStruct((count, CONV_CACHE, width), jnp.bfloat16),
            jax.ShapeDtypeStruct(key_done.shape, jnp.bfloat16),
            jax.ShapeDtypeStruct(value_done.shape, jnp.bfloat16),
        ],
        scratch_shapes=[
            pltpu.VMEM((width // LANES, keep * count, LANES), jnp.float32),
            pltpu.VMEM((CONV_CACHE * count, LANES), jnp.float32),
        ],
        input_output_aliases={3: 2, 4: 3},
        name="finish",
    )(coming, everything, received, key_done, value_done)


def swap(chunks, member, count):
    pieces = [lax.dynamic_index_in_dim(chunks, member, 0, False)]
    for step in range(1, count):
        chunk = lax.dynamic_index_in_dim(chunks, (member + step) % count, 0, False)
        pieces.append(toward(chunk, step, count))
    return pieces


def toward(array, steps, count):
    return lax.ppermute(array, "enc", [(i, (i + steps) % count) for i in range(count)])


def on_device(
    spectra,
    sub_weight,
    sub_bias,
    key_cache,
    value_cache,
    conv_cache,
    new_slot,
    old_slot,
    valid_new,
    cache_fill,
    ln1_gain,
    w_query,
    w_key,
    w_value,
    w_attn_out,
    ln2_gain,
    w_glu_value,
    w_glu_gate,
    depth_kernel,
    norm_scale,
    norm_shift,
    w_conv_out,
):
    peer_count = lax.axis_size("front")
    own_index = lax.axis_index("front")
    member = lax.axis_index("enc")
    stream_count = spectra.shape[0]
    local_width = w_query.shape[1]
    slots = peer_count * CAP
    groups = lax.axis_size("enc")
    core = own_index % 2
    where = jnp.stack([member, core, own_index])
    both = valid_new * (1 << FIELD) + cache_fill
    share = stream_count // groups
    payloads, maps, asked, stack = prepare(
        where,
        (new_slot, old_slot, both),
        (sub_weight, sub_bias),
        (depth_kernel, norm_scale, norm_shift),
        conv_cache.reshape(groups, share * CONV_CACHE, local_width),
        (w_attn_out, w_conv_out),
        (w_glu_value, w_glu_gate),
        slots,
    )
    bucket, arrival, leaving, coming = maps
    pieces = [payloads[0]] + [toward(payloads[k], k, groups) for k in range(1, groups)]
    told = lax.all_to_all(asked, "front", split_axis=0, concat_axis=0, tiled=True)
    key_rows = key_cache.transpose(1, 0, 2)
    value_rows = value_cache.transpose(1, 0, 2)
    leaving_rows = pack_rows(bucket, key_rows, value_rows, slots)
    received = lax.all_to_all(leaving_rows, "front", split_axis=0, concat_axis=0, tiled=True)
    taps = SUB * MELS
    middle_row = stack.shape[0] // 2

    def other_core(array):
        return lax.ppermute(array, "front", [(i, i ^ 1) for i in range(peer_count)])

    near = toward(stack, 1, groups)
    after = toward(stack, -1, groups)
    far_low = toward(near[:middle_row], 1, groups)
    far_high = toward(after[middle_row:], -1, groups)
    near_other = other_core(near)
    after_other = other_core(after)
    far_low_other = other_core(far_low)
    far_high_other = other_core(far_high)
    frames = spectra.transpose(1, 2, 0).reshape(FRAMES, taps, stream_count)
    queries, key_new, value_new, inputs = head(
        where, frames, pieces, ln1_gain, (w_query, w_key, w_value)
    )
    context, key_slab, value_slab, packed = attend(
        bucket, both, told, queries, key_new, value_new, key_rows, value_rows, groups
    )
    context = swap(context, member, groups)
    ended = tail(
        where,
        groups,
        *context,
        *pieces,
        inputs,
        ln2_gain[None, :],
        packed,
        w_attn_out,
        w_conv_out,
        w_glu_value,
        w_glu_gate,
        near,
        near_other,
        far_low,
        far_low_other,
        after,
        after_other,
        near,
        near_other,
        far_high,
        far_high_other,
        after,
        after_other,
    )
    ended = [ended[0]] + [toward(ended[k], k, groups) for k in range(1, groups)]
    everything, leaving_end = collect(leaving, where, ended, (key_slab, value_slab), slots)
    received_end = lax.all_to_all(leaving_end, "front", split_axis=0, concat_axis=0, tiled=True)
    key_done, value_done = place(arrival, valid_new, received, key_rows, value_rows)
    encoded, conv_out, key_done, value_done = finish(
        coming, everything, received_end, key_done, value_done
    )
    return (
        encoded.transpose(1, 0, 2),
        key_done.transpose(1, 0, 2),
        value_done.transpose(1, 0, 2),
        conv_out,
    )


def solution(mesh):
    in_specs = (
        P("front", None, None),
        P(None, "enc"),
        P("enc"),
        P("front", None, "enc"),
        P("front", None, "enc"),
        P("front", None, "enc"),
        P("front"),
        P("front"),
        P("front"),
        P("front"),
        P(),
        P(None, "enc"),
        P(None, "enc"),
        P(None, "enc"),
        P("enc", None),
        P(),
        P(None, "enc"),
        P(None, "enc"),
        P(None, "enc"),
        P("enc"),
        P("enc"),
        P("enc", None),
    )
    out_specs = (
        P("front", None, "enc"),
        P("front", None, "enc"),
        P("front", None, "enc"),
        P("front", None, "enc"),
    )

    return jax.shard_map(
        on_device, mesh=mesh, in_specs=in_specs, out_specs=out_specs, check_vma=False
    )
```

```python
import functools
import math

import jax
import jax.numpy as jnp
from jax import lax
from jax.experimental import pallas as pl
from jax.experimental.pallas import tpu as pltpu
from jax.sharding import PartitionSpec as P


MELS = 80
KERNEL = 9
SUB = 8
FRAMES = 7
CACHE = 70
CAP = 2
HEAD = 128
CONV_CACHE = 8
LANES = 128
BLOCK = 16
SPAN = 80
KEEP = 72
CHUNK = 10
FIELD = 7

masked_score = -1e30


def prepare_body(
    place_s,
    new_ref,
    old_ref,
    valid_ref,
    fill_ref,
    weight_ref,
    bias_ref,
    kernel_ref,
    scale_ref,
    shift_ref,
    cache_ref,
    attn_ref,
    conv_ref,
    value_ref,
    gate_ref,
    *refs,
):
    payloads, maps, (wide_ref, asked_ref, stack_ref, small) = refs[:4], refs[4:11], refs[11:]
    both_ref, bucket_ref, out_ref, out_rank_ref, arrival_ref, in_ref, in_rank_ref = maps
    member, own = place_s[0], place_s[2]
    groups = len(payloads)
    taps, width = weight_ref.shape
    slots, count = asked_ref.shape
    bits = count.bit_length() - 1

    small[:KERNEL, :] = kernel_ref[...]
    small[KERNEL : KERNEL + 1, :] = scale_ref[...]
    small[KERNEL + 1 : KERNEL + 2, :] = shift_ref[...]
    small[KERNEL + 2 :, :] = jnp.zeros((16 - KERNEL - 2, width), jnp.float32)
    rest = small[...]
    bias = jnp.broadcast_to(bias_ref[...].astype(jnp.float32), (16, width)).astype(jnp.bfloat16)
    parts = []
    for _ in range(3):
        part = rest.astype(jnp.bfloat16)
        parts.append(part)
        rest = rest - part.astype(jnp.float32)
    for step, payload in enumerate(payloads):
        payload[:taps, :] = weight_ref[...]
        payload[taps : taps + 16, :] = bias
        for i, part in enumerate(parts):
            payload[taps + 16 * (i + 1) : taps + 16 * (i + 2), :] = part
        payload[taps + 64 :, :] = cache_ref[(member + step) % groups]

    half = attn_ref.shape[0]
    for start, source in ((0, attn_ref), (groups * half, conv_ref)):
        for n in range(groups):
            at = start + n * half
            stack_ref[at : at + half, :] = source[:, n * width : (n + 1) * width]
    at = 2 * groups * half
    stack_ref[at : at + value_ref.shape[0], :] = value_ref[...]
    stack_ref[at + value_ref.shape[0] :, :] = gate_ref[...]

    def column(row):
        return jnp.transpose(jnp.broadcast_to(row, (count, count)))

    def ranked(group_column, group_row, before):
        same = jnp.where((group_column == group_row) & before, 1.0, 0.0)
        return jnp.sum(same, axis=0, keepdims=True).astype(jnp.int32)

    first = lax.broadcasted_iota(jnp.int32, (count, count), 0)
    second = lax.broadcasted_iota(jnp.int32, (count, count), 1)

    def inverse(row):
        hit = jnp.where(column(row) == second, (first + 1).astype(jnp.float32), 0.0)
        return jnp.sum(hit, axis=0, keepdims=True).astype(jnp.int32) - 1

    def listed(chosen, list_ref, rank_ref):
        marks = column(jnp.where(chosen, 1, 0)).astype(jnp.float32)
        rank = jnp.sum(jnp.where(first <= second, marks, 0.0), axis=0, keepdims=True)
        rank = rank.astype(jnp.int32)
        rank_ref[...] = rank
        list_ref[...] = inverse(jnp.where(chosen, rank - 1, -1))

    valid = valid_ref[...]
    wide_ref[...] = column(valid)
    both = valid * (1 << FIELD) + fill_ref[...]
    both_ref[...] = both
    target = new_ref[...] >> bits
    position = ranked(column(target), target, first < second)
    bucket = jnp.where(target != own, target * CAP + position, slots)
    bucket_ref[...] = bucket
    listed(target != own, out_ref, out_rank_ref)
    old_row = old_ref[...]
    old_column = column(old_row)
    source = old_row >> bits
    position = ranked(old_column >> bits, source, old_column < old_row)
    arrival = jnp.where(source == own, -1, source * CAP + position)
    arrival_ref[...] = arrival
    listed(source != own, in_ref, in_rank_ref)
    slot = lax.broadcasted_iota(jnp.int32, (slots, count), 0)
    hit = jnp.where(arrival == slot, both.astype(jnp.float32), 0.0)
    asked = jnp.sum(hit, axis=1, keepdims=True).astype(jnp.int32)
    asked_ref[...] = jnp.broadcast_to(asked, (slots, count))


def prepare(where, rows, sub, conv, chunks, columns, tall, slots):
    count = rows[0].shape[0]
    groups, chunk_rows, width = chunks.shape
    taps = sub[0].shape[0]
    whole = [r[None] for r in rows] + [sub[0], sub[1][None], conv[0], conv[1][None], conv[2][None]]

    def full(array):
        zeros = (0,) * array.ndim
        return pl.BlockSpec(array.shape, lambda i, place_s: zeros)

    def my_half(array):
        return pl.BlockSpec(
            (array.shape[0] // 2, array.shape[1]), lambda i, place_s: (place_s[1], 0)
        )

    row = jax.ShapeDtypeStruct((1, count), jnp.int32)
    payload = jax.ShapeDtypeStruct((taps + 64 + chunk_rows, width), jnp.bfloat16)
    shapes = [payload] * groups + [row] * 7
    shapes.append(jax.ShapeDtypeStruct((count, count), jnp.int32))
    shapes.append(jax.ShapeDtypeStruct((slots, count), jnp.int32))
    shapes.append(jax.ShapeDtypeStruct((2 * groups * width, width), jnp.bfloat16))
    outs = pl.pallas_call(
        prepare_body,
        grid_spec=pltpu.PrefetchScalarGridSpec(
            num_scalar_prefetch=1,
            grid=(1,),
            in_specs=[full(a) for a in whole]
            + [full(chunks)]
            + [my_half(a) for a in columns + tall],
            out_specs=[full(a) for a in shapes],
            scratch_shapes=[pltpu.VMEM((16, width), jnp.float32)],
        ),
        out_shape=shapes,
        name="prepare",
    )(where, *whole, chunks, *columns, *tall)
    return outs[:groups], [r[0] for r in outs[groups : groups + 7]], *outs[-3:]


def shift_rows(rows, first, second, third):
    rows = jnp.where(first, rows[1:], rows[:-1])
    rows = jnp.where(second, rows[2:], rows[:-2])
    return jnp.where(third, rows[4:], rows[:-4])


def attend_body(
    place_s,
    bucket_s,
    both_s,
    told_ref,
    query_ref,
    key_new_ref,
    value_new_ref,
    key_ref,
    value_ref,
    *rest,
    begin,
    groups,
    per_group,
):
    near_ref, far_ref, key_out_ref, value_out_ref, packed_ref = rest[-5:]
    step = pl.program_id(0)
    base = chosen_block(step, place_s, begin, groups, per_group) * BLOCK
    slots = told_ref.shape[0]
    for s in range(BLOCK):
        slot = bucket_s[base + s]
        told = told_ref[pl.ds(jnp.minimum(slot, slots - 1), 1), :]
        packed_ref[s : s + 1, :] = jnp.where(
            slot < slots, told, jnp.full_like(told, both_s[base + s])
        )
    packed = packed_ref[...]
    width = query_ref.shape[2]
    heads = width // LANES
    span = SPAN * BLOCK
    valid = packed >> FIELD
    low = (CACHE - (packed[:, :1] & ((1 << FIELD) - 1))) * BLOCK
    high = (CACHE + valid[:, :1]) * BLOCK
    offset = lax.broadcasted_iota(jnp.int32, (BLOCK, span), 1) - lax.broadcasted_iota(
        jnp.int32, (BLOCK, span), 0
    )
    allowed = ((offset & (BLOCK - 1)) == 0) & (offset >= low) & (offset < high)
    bias = jnp.where(allowed, 0.0, masked_score)[None]
    padding = jnp.zeros(((SPAN - CACHE - FRAMES) * BLOCK, LANES), jnp.bfloat16)

    def joined(old_ref, new_ref, lanes):
        return jnp.concatenate(
            [
                old_ref[:, :, lanes].reshape(CACHE * BLOCK, LANES),
                new_ref[:, :, lanes].reshape(FRAMES * BLOCK, LANES),
                padding,
            ],
            axis=0,
        )

    for h in range(heads):
        lanes = slice(h * LANES, (h + 1) * LANES)
        scores = lax.dot_general(
            query_ref[:, :, lanes].reshape(FRAMES * BLOCK, LANES),
            joined(key_ref, key_new_ref, lanes),
            (((1,), (1,)), ((), ())),
            preferred_element_type=jnp.float32,
        )
        scores = scores.reshape(FRAMES, BLOCK, span) * (1.0 / math.sqrt(HEAD)) + bias
        exponent = jnp.exp(scores - jnp.max(scores, axis=2, keepdims=True))
        weights = exponent * (1.0 / jnp.sum(exponent, axis=2, keepdims=True))
        context = lax.dot_general(
            weights.astype(jnp.bfloat16).reshape(FRAMES * BLOCK, span),
            joined(value_ref, value_new_ref, lanes),
            (((1,), (0,)), ((), ())),
            preferred_element_type=jnp.float32,
        )
        context = context.reshape(FRAMES, BLOCK, LANES).astype(jnp.bfloat16)

        @pl.when(step < per_group)
        def _():
            near_ref[:, :, lanes] = context

        @pl.when(step >= per_group)
        def _():
            far_ref[:, :, lanes] = context

    shift = valid - 1
    first = ((shift & 1) != 0)[None]
    second = ((shift & 2) != 0)[None]
    third = ((shift & 4) != 0)[None]
    edge = CACHE - FRAMES
    for old_ref, new_ref, out_ref in (
        (key_ref, key_new_ref, key_out_ref),
        (value_ref, value_new_ref, value_out_ref),
    ):
        for h in range(heads):
            lanes = slice(h * LANES, (h + 1) * LANES)
            old = old_ref[edge + 1 :, :, lanes].astype(jnp.float32)
            new = new_ref[:, :, lanes].astype(jnp.float32)
            rows = jnp.concatenate([old, new, new[:1]], axis=0)
            out_ref[:, :, lanes] = shift_rows(rows, first, second, third).astype(jnp.bfloat16)


def chosen_block(i, place_s, begin, groups, per_group):
    return ((place_s[0] + begin + i // per_group) % groups) * per_group + i % per_group


def attend(begin, where, bucket, both, told, new, caches, groups, earlier=()):
    stream_count = caches[0].shape[1]
    width = caches[0].shape[2]
    share = stream_count // groups
    per_group = share // BLOCK

    def at(i, place_s):
        return chosen_block(i, place_s, begin, groups, per_group)

    def block(rows):
        return pl.BlockSpec((rows, BLOCK, width), lambda i, p, *_: (0, at(i, p), 0))

    part = (FRAMES, BLOCK, width)
    context = jax.ShapeDtypeStruct((FRAMES, share, width), jnp.bfloat16)
    slab = jax.ShapeDtypeStruct((FRAMES, stream_count, width), jnp.bfloat16)
    return pl.pallas_call(
        functools.partial(attend_body, begin=begin, groups=groups, per_group=per_group),
        grid_spec=pltpu.PrefetchScalarGridSpec(
            num_scalar_prefetch=3,
            grid=(2 * per_group,),
            in_specs=[pl.BlockSpec(told.shape, lambda i, *_: (0, 0))]
            + [block(FRAMES)] * 3
            + [block(CACHE)] * 2
            + [pl.BlockSpec(memory_space=pl.ANY)] * len(earlier),
            out_specs=[
                pl.BlockSpec(part, lambda i, *_: (0, jnp.minimum(i, per_group - 1), 0)),
                pl.BlockSpec(part, lambda i, *_: (0, jnp.maximum(i - per_group, 0), 0)),
                block(FRAMES),
                block(FRAMES),
                pl.BlockSpec((BLOCK, LANES), lambda i, p, *_: (at(i, p), 0)),
            ],
        ),
        out_shape=[
            context,
            context,
            slab,
            slab,
            jax.ShapeDtypeStruct((stream_count, LANES), jnp.int32),
        ],
        input_output_aliases={9 + k: 2 + k for k in range(len(earlier))},
        name="attend_b" if earlier else "attend_a",
    )(where, bucket, both, told, *new, *caches, *earlier)


def bounds(rank_s, base):
    return jnp.where(base == 0, 0, rank_s[jnp.maximum(base - 1, 0)]), rank_s[base + BLOCK - 1]


def pack_body(slot_s, list_s, rank_s, key_ref, value_ref, send_ref, rows_f):
    base = pl.program_id(0) * BLOCK
    heads = rows_f.shape[1]
    for kind, src in enumerate((key_ref, value_ref)):
        for h in range(heads):
            rows_f[kind, h, : CACHE * BLOCK, :] = (
                src[:, :, h * LANES : (h + 1) * LANES]
                .astype(jnp.float32)
                .reshape(CACHE * BLOCK, LANES)
            )

    def pack(k, carry):
        s = list_s[k] - base
        slot = slot_s[base + s]
        for kind in range(2):
            for h in range(heads):
                send_ref[slot, kind, :, h * LANES : (h + 1) * LANES] = rows_f[
                    kind, h, pl.ds(s, KEEP, stride=BLOCK), :
                ].astype(jnp.bfloat16)
        return carry

    lax.fori_loop(*bounds(rank_s, base), pack, 0)


def pack_rows(leaving, key_cache, value_cache, slots):
    stream_count = key_cache.shape[1]
    width = key_cache.shape[2]
    block = pl.BlockSpec((CACHE, BLOCK, width), lambda i, *_: (0, i, 0))
    return pl.pallas_call(
        pack_body,
        grid_spec=pltpu.PrefetchScalarGridSpec(
            num_scalar_prefetch=3,
            grid=(stream_count // BLOCK,),
            in_specs=[block, block],
            out_specs=pl.BlockSpec((slots, 2, KEEP, width), lambda i, *_: (0, 0, 0, 0)),
            scratch_shapes=[
                pltpu.VMEM((2, width // HEAD, KEEP * BLOCK, LANES), jnp.float32)
            ],
        ),
        out_shape=jax.ShapeDtypeStruct((slots, 2, KEEP, width), jnp.bfloat16),
        name="pack",
    )(*leaving, key_cache, value_cache)


def place_body(
    arrival_s, list_s, rank_s, got_ref, valid_ref, key_ref, value_ref, key_out_ref, value_out_ref, rows_f
):
    base = pl.program_id(0) * BLOCK
    heads = rows_f.shape[1]
    for kind, src in enumerate((key_ref, value_ref)):
        for h in range(heads):
            lanes = slice(h * LANES, (h + 1) * LANES)
            for start in range(0, CACHE, CHUNK):
                rows_f[kind, h, start * BLOCK : (start + CHUNK) * BLOCK, :] = (
                    src[start : start + CHUNK, :, lanes]
                    .astype(jnp.float32)
                    .reshape(CHUNK * BLOCK, LANES)
                )

    def fetch(k, carry):
        s = list_s[k] - base
        slot = arrival_s[base + s]
        for kind in range(2):
            for h in range(heads):
                rows_f[kind, h, pl.ds(s, KEEP, stride=BLOCK), :] = got_ref[
                    slot, kind, :, h * LANES : (h + 1) * LANES
                ].astype(jnp.float32)
        return carry

    lax.fori_loop(*bounds(rank_s, base), fetch, 0)
    shift = valid_ref[...] - 1
    first = ((shift & 1) != 0)[None]
    second = ((shift & 2) != 0)[None]
    third = ((shift & 4) != 0)[None]
    edge = CACHE - FRAMES
    for kind, dst in enumerate((key_out_ref, value_out_ref)):
        for h in range(heads):
            lanes = slice(h * LANES, (h + 1) * LANES)
            for start in range(0, edge, 9):
                rows = rows_f[kind, h, (start + 1) * BLOCK : (start + 17) * BLOCK, :]
                rows = shift_rows(rows.reshape(16, BLOCK, LANES), first, second, third)
                dst[start : start + 9, :, lanes] = rows.astype(jnp.bfloat16)
            dst[edge:, :, lanes] = jnp.zeros((FRAMES, BLOCK, LANES), jnp.bfloat16)


def place(coming, valid_wide, received, key_rows, value_rows):
    stream_count = key_rows.shape[1]
    width = key_rows.shape[2]
    heads = width // HEAD
    slots = received.shape[0]
    block = pl.BlockSpec((CACHE, BLOCK, width), lambda i, *_: (0, i, 0))
    shape = jax.ShapeDtypeStruct((CACHE, stream_count, width), jnp.bfloat16)
    return pl.pallas_call(
        place_body,
        grid_spec=pltpu.PrefetchScalarGridSpec(
            num_scalar_prefetch=3,
            grid=(stream_count // BLOCK,),
            in_specs=[
                pl.BlockSpec((slots, 2, KEEP, width), lambda i, *_: (0, 0, 0, 0)),
                pl.BlockSpec((BLOCK, LANES), lambda i, *_: (i, 0)),
                block,
                block,
            ],
            out_specs=[block, block],
            scratch_shapes=[pltpu.VMEM((2, heads, KEEP * BLOCK, LANES), jnp.float32)],
        ),
        out_shape=[shape, shape],
        name="place",
    )(
        *coming,
        received,
        valid_wide,
        key_rows,
        value_rows,
    )


def head_body(
    place_s, frames_ref, own_ref, near_ref, far_ref, next_ref, gain_ref, *rest
):
    weights, outs, inputs_ref, flat, raw, normed = rest[:3], rest[3:6], *rest[6:]
    member = place_s[0]
    groups = raw.shape[0]
    width = raw.shape[2]
    count, taps, streams = frames_ref.shape
    for t in range(count):
        flat[t * streams : (t + 1) * streams, :] = jnp.transpose(frames_ref[t])
    for offset, piece in enumerate((own_ref, near_ref, far_ref, next_ref)):
        total = jnp.dot(flat[...], piece[:taps, :], preferred_element_type=jnp.float32)
        total = total + piece[taps : taps + 16, :].astype(jnp.float32)[:1]
        raw[(member + groups - offset) % groups] = total.astype(jnp.bfloat16)
    model_width = groups * width
    share = inputs_ref.shape[1]
    for t in range(count):
        lines = slice(t * streams, (t + 1) * streams)
        values = [raw[g, lines, :].astype(jnp.float32) for g in range(groups)]
        average = sum(jnp.sum(v, axis=1, keepdims=True) for v in values) * (1.0 / model_width)
        values = [v - average for v in values]
        spread = sum(jnp.sum(v * v, axis=1, keepdims=True) for v in values) * (1.0 / model_width)
        scale = lax.rsqrt(spread + 1e-05)
        for g, v in enumerate(values):
            columns = slice(g * width, (g + 1) * width)
            normed[lines, columns] = (v * scale * gain_ref[:, columns]).astype(jnp.bfloat16)
            start = pl.multiple_of(t * streams + member * share, share)
            inputs_ref[t, :, columns] = raw[g, pl.ds(start, share), :]
    for matrix, out in zip(weights, outs):
        product = jnp.dot(normed[...], matrix[...], preferred_element_type=jnp.float32)
        out[...] = product.astype(jnp.bfloat16).reshape(count, streams, width)


def head(where, frames, pieces, gain, matrices):
    count, taps, streams = frames.shape
    width = matrices[0].shape[1]
    groups = len(pieces)

    def whole(array):
        zeros = (0,) * array.ndim
        return pl.BlockSpec(array.shape, lambda i, *_: zeros)

    gain = gain[None, :]
    shapes = [jax.ShapeDtypeStruct((count, streams, width), jnp.bfloat16)] * 3
    shapes.append(
        jax.ShapeDtypeStruct((count, streams // groups, groups * width), jnp.bfloat16)
    )
    return pl.pallas_call(
        head_body,
        grid_spec=pltpu.PrefetchScalarGridSpec(
            num_scalar_prefetch=1,
            grid=(1,),
            in_specs=[whole(frames)]
            + [pl.BlockSpec((taps + 16, width), lambda i, *_: (0, 0))] * groups
            + [whole(gain)]
            + [whole(w) for w in matrices],
            out_specs=[whole(a) for a in shapes],
            scratch_shapes=[
                pltpu.VMEM((count * streams, taps), jnp.bfloat16),
                pltpu.VMEM((groups, count * streams, width), jnp.bfloat16),
                pltpu.VMEM((count * streams, groups * width), jnp.bfloat16),
            ],
        ),
        out_shape=shapes,
        name="head",
    )(where, frames, *pieces, gain, *matrices)


def tail_body(place_s, *refs):
    contexts, pieces, rest = refs[:4], refs[4:8], refs[8:]
    inputs_ref, gain_ref, packed_ref = rest[:3]
    attn_ref, conv_ref, value_ref, gate_ref = rest[3:7]
    low_refs, high_refs, outs = rest[7:13], rest[13:19], rest[19:23]
    out_ref, cache_f = rest[23:]
    member = place_s[0]
    front_half = place_s[1] == 0
    groups = len(contexts)
    _, share, width = contexts[0].shape
    rows = FRAMES * share
    size = groups * width
    half = width // 2

    def ordered(operand):
        middle_lane = operand.shape[1] // 2
        low, high = operand[:, :middle_lane], operand[:, middle_lane:]
        return jnp.where(front_half, low, high), jnp.where(front_half, high, low)

    def dot(left, right):
        return jnp.dot(left, right, preferred_element_type=jnp.float32)

    def grouped(step, operand, own_ref, start, sums):
        sides = ordered(operand)
        for n in range(groups):
            if step == 0:
                part = dot(operand, own_ref[:, n * width : (n + 1) * width])
            else:
                at = start + n * half
                part = sum(
                    dot(side, low_refs[2 * (step - 1) + i][at : at + half, :])
                    for i, side in enumerate(sides)
                )
            part = part.astype(jnp.bfloat16).astype(jnp.float32)
            sums[n] = part if sums[n] is None else sums[n] + part

    def wide(step, own_ref, order):
        if step == 0:
            return dot(normed, own_ref[...])
        at = high_starts[step - 1] + order * (size // 2)
        return sum(
            dot(side, high_refs[2 * (step - 1) + i][at : at + size // 2, :])
            for i, side in enumerate(normed_sides)
        )

    high_starts = (size, 0, size)
    attended = [None] * groups
    for step in range(groups):
        grouped(step, contexts[step][...].reshape(rows, width), attn_ref, 0, attended)
    middle = []
    for n in range(groups):
        inputs = inputs_ref[:, :, n * width : (n + 1) * width].reshape(rows, width)
        middle.append((inputs.astype(jnp.float32) + attended[n]).astype(jnp.bfloat16))
    values = [m.astype(jnp.float32) for m in middle]
    average = sum(jnp.sum(v, axis=1, keepdims=True) for v in values) * (1.0 / size)
    values = [v - average for v in values]
    spread = sum(jnp.sum(v * v, axis=1, keepdims=True) for v in values) * (1.0 / size)
    scale = lax.rsqrt(spread + 1e-05)
    normed = jnp.concatenate(
        [
            (v * scale * gain_ref[:, n * width : (n + 1) * width]).astype(jnp.bfloat16)
            for n, v in enumerate(values)
        ],
        axis=1,
    )
    normed_sides = ordered(normed)
    valid = packed_ref[pl.ds(pl.multiple_of(member * share, share), share), :] >> FIELD
    valid = jnp.concatenate([valid] * (width // LANES), axis=1)
    shift = valid - 1
    first = ((shift & 1) != 0)[None]
    second = ((shift & 2) != 0)[None]
    third = ((shift & 4) != 0)[None]
    conv_term = [None] * groups
    extra = SUB * MELS + 16
    tail_rows = extra + 3 * 16
    for step in range(groups):
        group = (member + groups - step) % groups
        piece = pieces[step]
        small = sum(
            piece[extra + 16 * i : extra + 16 * (i + 1), :].astype(jnp.float32) for i in range(3)
        )
        for h in range(width // LANES):
            cache_f[h] = piece[tail_rows:, h * LANES : (h + 1) * LANES].astype(jnp.float32)
        cached = jnp.concatenate(
            [
                jnp.stack(
                    [cache_f[h, pl.ds(t, share, stride=CONV_CACHE), :] for t in range(CONV_CACHE)]
                )
                for h in range(width // LANES)
            ],
            axis=2,
        )
        glu_value = wide(step, value_ref, 0)
        glu_gate = wide(step, gate_ref, 1)
        gated = (glu_value * jax.nn.sigmoid(glu_gate)).astype(jnp.bfloat16)
        conv_in = jnp.concatenate(
            [
                cached,
                gated.astype(jnp.float32).reshape(FRAMES, share, width),
            ],
            axis=0,
        )
        depthwise = jnp.zeros((FRAMES, share, width), jnp.float32)
        for tap in range(KERNEL):
            depthwise = depthwise + small[tap : tap + 1, :][None] * conv_in[tap : tap + FRAMES]
        shaped = depthwise * small[KERNEL : KERNEL + 1, :][None]
        shaped = shaped + small[KERNEL + 1 : KERNEL + 2, :][None]
        activated = (shaped * jax.nn.sigmoid(shaped)).astype(jnp.bfloat16)
        grouped(step, activated.reshape(rows, width), conv_ref, size // 2, conv_term)
        moved = shift_rows(
            jnp.concatenate([conv_in[1:], conv_in[-1:]], axis=0), first, second, third
        )
        out_ref[group, FRAMES:, :, :] = moved.astype(jnp.bfloat16)
    frame = lax.broadcasted_iota(jnp.int32, (FRAMES, share, width), 0)
    for n in range(groups):
        total = (middle[n].astype(jnp.float32) + conv_term[n]).reshape(FRAMES, share, width)
        out_ref[n, :FRAMES, :, :] = jnp.where(frame < valid[None], total, 0.0).astype(jnp.bfloat16)


    for step, out in enumerate(outs):
        out[...] = out_ref[(member + step) % groups]


def tail(where, groups, *arrays):
    _, share, width = arrays[0].shape
    shape = (FRAMES + CONV_CACHE, share, width)
    vmem = pl.BlockSpec(memory_space=pltpu.VMEM)
    return pl.pallas_call(
        tail_body,
        in_specs=[pl.BlockSpec(memory_space=pltpu.SMEM)] + [vmem] * len(arrays),
        out_specs=[vmem] * groups,
        out_shape=[jax.ShapeDtypeStruct(shape, jnp.bfloat16)] * groups,
        scratch_shapes=[
            pltpu.VMEM((groups,) + shape, jnp.bfloat16),
            pltpu.VMEM((width // LANES, CONV_CACHE * share, LANES), jnp.float32),
        ],
        name="tail",
    )(where, *arrays)


def collect_body(slot_s, list_s, rank_s, place_s, *refs):
    pieces, slabs, (all_ref, send_ref, rows_f) = refs[:4], refs[4:6], refs[6:]
    member = place_s[0]
    groups = len(pieces)
    frames, share, _ = pieces[0].shape
    heads, _, _ = rows_f.shape
    _, keep, _ = send_ref.shape
    count = groups * share
    for step, piece in enumerate(pieces):
        start = pl.multiple_of(((member + groups - step) % groups) * share, share)
        all_ref[:frames, pl.ds(start, share), :] = piece[...]
        for h in range(heads):
            for t in range(frames):
                rows_f[h, pl.ds(pl.multiple_of(t * count + start, share), share), :] = piece[
                    t, :, h * LANES : (h + 1) * LANES
                ].astype(jnp.float32)
    for slab in slabs:
        all_ref[frames : frames + FRAMES] = slab[...]
        for h in range(heads):
            rows_f[h, frames * count : (frames + FRAMES) * count, :] = (
                slab[:, :, h * LANES : (h + 1) * LANES]
                .astype(jnp.float32)
                .reshape(FRAMES * count, LANES)
            )
        frames += FRAMES

    def pack(k, carry):
        s = list_s[k]
        slot = slot_s[s]
        for h in range(heads):
            send_ref[slot, :, h * LANES : (h + 1) * LANES] = rows_f[
                h, pl.ds(s, keep, stride=count), :
            ].astype(jnp.bfloat16)
        return carry

    lax.fori_loop(0, rank_s[count - 1], pack, 0)


def collect(leaving, where, pieces, slabs, slots):
    frames = FRAMES + CONV_CACHE + 2 * FRAMES
    keep = -(-frames // 16) * 16
    _, count, width = slabs[0].shape
    smem = pl.BlockSpec(memory_space=pltpu.SMEM)
    vmem = pl.BlockSpec(memory_space=pltpu.VMEM)
    return pl.pallas_call(
        collect_body,
        in_specs=[smem] * 4 + [vmem] * 6,
        out_specs=[vmem, vmem],
        out_shape=[
            jax.ShapeDtypeStruct((frames, count, width), jnp.bfloat16),
            jax.ShapeDtypeStruct((slots, keep, width), jnp.bfloat16),
        ],
        scratch_shapes=[pltpu.VMEM((width // LANES, keep * count, LANES), jnp.float32)],
        name="collect",
    )(*leaving, where, *pieces, *slabs)


def finish_body(
    slot_s, list_s, rank_s, all_ref, got_ref, _, __, encoded_ref, conv_ref, key_ref, value_ref, rows_f, conv_f
):
    heads = rows_f.shape[0]
    frames, count, _ = all_ref.shape
    keep = got_ref.shape[1]
    for h in range(heads):
        rows_f[h, : frames * count, :] = (
            all_ref[:, :, h * LANES : (h + 1) * LANES]
            .astype(jnp.float32)
            .reshape(frames * count, LANES)
        )

    def fetch(k, carry):
        s = list_s[k]
        slot = slot_s[s]
        for h in range(heads):
            rows_f[h, pl.ds(s, keep, stride=count), :] = got_ref[
                slot, :, h * LANES : (h + 1) * LANES
            ].astype(jnp.float32)
        return carry

    lax.fori_loop(0, rank_s[count - 1], fetch, 0)
    ends = FRAMES + CONV_CACHE
    for h in range(heads):
        lanes = slice(h * LANES, (h + 1) * LANES)
        for start, out in ((0, encoded_ref), (ends, key_ref), (ends + FRAMES, value_ref)):
            rows = rows_f[h, start * count : (start + FRAMES) * count, :]
            out[:, :, lanes] = rows.reshape(FRAMES, count, LANES).astype(jnp.bfloat16)
        for t in range(CONV_CACHE):
            at = (FRAMES + t) * count
            conv_f[pl.ds(t, count, stride=CONV_CACHE), :] = rows_f[h, at : at + count, :]
        conv_ref[:, :, lanes] = (
            conv_f[...].reshape(count, CONV_CACHE, LANES).astype(jnp.bfloat16)
        )


def finish(coming, everything, received, key_done, value_done):
    _, count, width = everything.shape
    keep = received.shape[1]
    smem = pl.BlockSpec(memory_space=pltpu.SMEM)
    vmem = pl.BlockSpec(memory_space=pltpu.VMEM)
    kept = pl.BlockSpec(memory_space=pl.ANY)
    slab = pl.BlockSpec((FRAMES, count, width), lambda i: (CACHE // FRAMES - 1, 0, 0))
    return pl.pallas_call(
        finish_body,
        grid=(1,),
        in_specs=[smem] * 3 + [vmem, vmem, kept, kept],
        out_specs=[vmem, vmem, slab, slab],
        out_shape=[
            jax.ShapeDtypeStruct((FRAMES, count, width), jnp.bfloat16),
            jax.ShapeDtypeStruct((count, CONV_CACHE, width), jnp.bfloat16),
            jax.ShapeDtypeStruct(key_done.shape, jnp.bfloat16),
            jax.ShapeDtypeStruct(value_done.shape, jnp.bfloat16),
        ],
        scratch_shapes=[
            pltpu.VMEM((width // LANES, keep * count, LANES), jnp.float32),
            pltpu.VMEM((CONV_CACHE * count, LANES), jnp.float32),
        ],
        input_output_aliases={5: 2, 6: 3},
        name="finish",
    )(*coming, everything, received, key_done, value_done)


def toward(array, steps, count):
    return lax.ppermute(array, "enc", [(i, (i + steps) % count) for i in range(count)])


def on_device(
    spectra,
    sub_weight,
    sub_bias,
    key_cache,
    value_cache,
    conv_cache,
    new_slot,
    old_slot,
    valid_new,
    cache_fill,
    ln1_gain,
    w_query,
    w_key,
    w_value,
    w_attn_out,
    ln2_gain,
    w_glu_value,
    w_glu_gate,
    depth_kernel,
    norm_scale,
    norm_shift,
    w_conv_out,
):
    peer_count = lax.axis_size("front")
    own_index = lax.axis_index("front")
    member = lax.axis_index("enc")
    stream_count = spectra.shape[0]
    local_width = w_query.shape[1]
    slots = peer_count * CAP
    groups = lax.axis_size("enc")
    core = own_index % 2
    where = jnp.stack([member, core, own_index])
    share = stream_count // groups
    payloads, maps, valid_wide, asked, stack = prepare(
        where,
        (new_slot, old_slot, valid_new, cache_fill),
        (sub_weight, sub_bias),
        (depth_kernel, norm_scale, norm_shift),
        conv_cache.reshape(groups, share * CONV_CACHE, local_width),
        (w_attn_out, w_conv_out),
        (w_glu_value, w_glu_gate),
        slots,
    )
    both, bucket, leaving, coming = maps[0], maps[1], maps[1:4], maps[4:7]
    pieces = [payloads[0]] + [toward(payloads[k], k, groups) for k in range(1, groups)]
    told = lax.all_to_all(asked, "front", split_axis=0, concat_axis=0, tiled=True)
    key_rows = key_cache.transpose(1, 0, 2)
    value_rows = value_cache.transpose(1, 0, 2)
    leaving_rows = pack_rows(leaving, key_rows, value_rows, slots)
    received = lax.all_to_all(leaving_rows, "front", split_axis=0, concat_axis=0, tiled=True)
    taps = SUB * MELS
    middle_row = stack.shape[0] // 2

    def other_core(array):
        return lax.ppermute(array, "front", [(i, i ^ 1) for i in range(peer_count)])

    near = toward(stack, 1, groups)
    after = toward(stack, -1, groups)
    far_low = toward(near[:middle_row], 1, groups)
    far_high = toward(after[middle_row:], -1, groups)
    near_other = other_core(near)
    after_other = other_core(after)
    far_low_other = other_core(far_low)
    far_high_other = other_core(far_high)
    frames = spectra.transpose(1, 2, 0).reshape(FRAMES, taps, stream_count)
    queries, key_new, value_new, inputs = head(
        where, frames, pieces, ln1_gain, (w_query, w_key, w_value)
    )
    new = (queries, key_new, value_new)
    caches = (key_rows, value_rows)
    first, second, *earlier = attend(1, where, bucket, both, told, new, caches, groups)
    context = [toward(first, 1, groups), toward(second, 2, groups)]
    third, own, key_slab, value_slab, packed = attend(
        groups - 1, where, bucket, both, told, new, caches, groups, earlier
    )
    context = [own] + context + [toward(third, groups - 1, groups)]
    ended = tail(
        where,
        groups,
        *context,
        *pieces,
        inputs,
        ln2_gain[None, :],
        packed,
        w_attn_out,
        w_conv_out,
        w_glu_value,
        w_glu_gate,
        near,
        near_other,
        far_low,
        far_low_other,
        after,
        after_other,
        near,
        near_other,
        far_high,
        far_high_other,
        after,
        after_other,
    )
    ended = [ended[0]] + [toward(ended[k], k, groups) for k in range(1, groups)]
    everything, leaving_end = collect(leaving, where, ended, (key_slab, value_slab), slots)
    received_end = lax.all_to_all(leaving_end, "front", split_axis=0, concat_axis=0, tiled=True)
    key_done, value_done = place(coming, valid_wide, received, key_rows, value_rows)
    encoded, conv_out, key_done, value_done = finish(
        coming, everything, received_end, key_done, value_done
    )
    return (
        encoded.transpose(1, 0, 2),
        key_done.transpose(1, 0, 2),
        value_done.transpose(1, 0, 2),
        conv_out,
    )


def solution(mesh):
    in_specs = (
        P("front", None, None),
        P(None, "enc"),
        P("enc"),
        P("front", None, "enc"),
        P("front", None, "enc"),
        P("front", None, "enc"),
        P("front"),
        P("front"),
        P("front"),
        P("front"),
        P(),
        P(None, "enc"),
        P(None, "enc"),
        P(None, "enc"),
        P("enc", None),
        P(),
        P(None, "enc"),
        P(None, "enc"),
        P(None, "enc"),
        P("enc"),
        P("enc"),
        P("enc", None),
    )
    out_specs = (
        P("front", None, "enc"),
        P("front", None, "enc"),
        P("front", None, "enc"),
        P("front", None, "enc"),
    )

    return jax.shard_map(
        on_device, mesh=mesh, in_specs=in_specs, out_specs=out_specs, check_vma=False
    )
```

```python
import functools
import math

import jax
import jax.numpy as jnp
from jax import lax
from jax.experimental import pallas as pl
from jax.experimental.pallas import tpu as pltpu
from jax.sharding import PartitionSpec as P


MELS = 80
KERNEL = 9
SUB = 8
FRAMES = 7
CACHE = 70
CAP = 2
HEAD = 128
CONV_CACHE = 8
LANES = 128
BLOCK = 16
SPAN = 80
KEEP = 72
CHUNK = 10
FIELD = 7

masked_score = -1e30


def prepare_body(
    place_s,
    new_ref,
    old_ref,
    valid_ref,
    fill_ref,
    weight_ref,
    bias_ref,
    kernel_ref,
    scale_ref,
    shift_ref,
    cache_ref,
    attn_ref,
    conv_ref,
    value_ref,
    gate_ref,
    *refs,
):
    payloads, maps, (wide_ref, asked_ref, stack_ref, small) = refs[:4], refs[4:11], refs[11:]
    both_ref, bucket_ref, out_ref, out_rank_ref, arrival_ref, in_ref, in_rank_ref = maps
    member, own = place_s[0], place_s[2]
    groups = len(payloads)
    taps, width = weight_ref.shape
    slots, count = asked_ref.shape
    bits = count.bit_length() - 1

    small[:KERNEL, :] = kernel_ref[...]
    small[KERNEL : KERNEL + 1, :] = scale_ref[...]
    small[KERNEL + 1 : KERNEL + 2, :] = shift_ref[...]
    small[KERNEL + 2 :, :] = jnp.zeros((16 - KERNEL - 2, width), jnp.float32)
    rest = small[...]
    bias = bias_ref[...].astype(jnp.float32).reshape(1, width)
    bias = jnp.broadcast_to(bias, (16, width)).astype(jnp.bfloat16)
    parts = []
    for _ in range(3):
        part = rest.astype(jnp.bfloat16)
        parts.append(part)
        rest = rest - part.astype(jnp.float32)
    for step, payload in enumerate(payloads):
        payload[:taps, :] = weight_ref[...]
        payload[taps : taps + 16, :] = bias
        for i, part in enumerate(parts):
            payload[taps + 16 * (i + 1) : taps + 16 * (i + 2), :] = part
        payload[taps + 64 :, :] = cache_ref[(member + step) % groups]

    half = attn_ref.shape[0]
    for start, source in ((0, attn_ref), (groups * half, conv_ref)):
        for n in range(groups):
            at = start + n * half
            stack_ref[at : at + half, :] = source[:, n * width : (n + 1) * width]
    at = 2 * groups * half
    stack_ref[at : at + value_ref.shape[0], :] = value_ref[...]
    stack_ref[at + value_ref.shape[0] :, :] = gate_ref[...]

    def column(row):
        return jnp.transpose(jnp.broadcast_to(row, (count, count)))

    def ranked(group_column, group_row, before):
        same = jnp.where((group_column == group_row) & before, 1.0, 0.0)
        return jnp.sum(same, axis=0, keepdims=True).astype(jnp.int32)

    first = lax.broadcasted_iota(jnp.int32, (count, count), 0)
    second = lax.broadcasted_iota(jnp.int32, (count, count), 1)

    def inverse(row):
        hit = jnp.where(column(row) == second, (first + 1).astype(jnp.float32), 0.0)
        return jnp.sum(hit, axis=0, keepdims=True).astype(jnp.int32) - 1

    def listed(chosen, list_ref, rank_ref):
        marks = column(jnp.where(chosen, 1, 0)).astype(jnp.float32)
        rank = jnp.sum(jnp.where(first <= second, marks, 0.0), axis=0, keepdims=True)
        rank = rank.astype(jnp.int32)
        rank_ref[...] = rank
        list_ref[...] = inverse(jnp.where(chosen, rank - 1, -1))

    valid = valid_ref[...]
    wide_ref[...] = column(valid)
    both = valid * (1 << FIELD) + fill_ref[...]
    both_ref[...] = both
    target = new_ref[...] >> bits
    position = ranked(column(target), target, first < second)
    bucket = jnp.where(target != own, target * CAP + position, slots)
    bucket_ref[...] = bucket
    listed(target != own, out_ref, out_rank_ref)
    old_row = old_ref[...]
    old_column = column(old_row)
    source = old_row >> bits
    position = ranked(old_column >> bits, source, old_column < old_row)
    arrival = jnp.where(source == own, -1, source * CAP + position)
    arrival_ref[...] = arrival
    listed(source != own, in_ref, in_rank_ref)
    slot = lax.broadcasted_iota(jnp.int32, (slots, count), 0)
    hit = jnp.where(arrival == slot, both.astype(jnp.float32), 0.0)
    asked = jnp.sum(hit, axis=1, keepdims=True).astype(jnp.int32)
    asked_ref[...] = jnp.broadcast_to(asked, (slots, count))


def prepare(where, rows, sub, conv, chunks, columns, tall, slots):
    count = rows[0].shape[0]
    groups, chunk_rows, width = chunks.shape
    taps = sub[0].shape[0]
    whole = [r[None] for r in rows] + [sub[0], sub[1], conv[0], conv[1][None], conv[2][None]]

    def full(array):
        zeros = (0,) * array.ndim
        return pl.BlockSpec(array.shape, lambda i, place_s: zeros)

    def my_half(array):
        return pl.BlockSpec(
            (array.shape[0] // 2, array.shape[1]), lambda i, place_s: (place_s[1], 0)
        )

    row = jax.ShapeDtypeStruct((1, count), jnp.int32)
    payload = jax.ShapeDtypeStruct((taps + 64 + chunk_rows, width), jnp.bfloat16)
    shapes = [payload] * groups + [row] * 7
    shapes.append(jax.ShapeDtypeStruct((count, count), jnp.int32))
    shapes.append(jax.ShapeDtypeStruct((slots, count), jnp.int32))
    shapes.append(jax.ShapeDtypeStruct((2 * groups * width, width), jnp.bfloat16))
    outs = pl.pallas_call(
        prepare_body,
        grid_spec=pltpu.PrefetchScalarGridSpec(
            num_scalar_prefetch=1,
            grid=(1,),
            in_specs=[full(a) for a in whole]
            + [full(chunks)]
            + [my_half(a) for a in columns + tall],
            out_specs=[full(a) for a in shapes],
            scratch_shapes=[pltpu.VMEM((16, width), jnp.float32)],
        ),
        out_shape=shapes,
        name="prepare",
    )(where, *whole, chunks, *columns, *tall)
    return outs[:groups], [r[0] for r in outs[groups : groups + 7]], *outs[-3:]


def shift_rows(rows, first, second, third):
    rows = jnp.where(first, rows[1:], rows[:-1])
    rows = jnp.where(second, rows[2:], rows[:-2])
    return jnp.where(third, rows[4:], rows[:-4])


def attend_body(
    place_s,
    bucket_s,
    both_s,
    told_ref,
    query_ref,
    key_new_ref,
    value_new_ref,
    key_ref,
    value_ref,
    *rest,
    begin,
    groups,
    per_group,
):
    near_ref, far_ref, key_out_ref, value_out_ref, packed_ref = rest[-5:]
    step = pl.program_id(0)
    base = chosen_block(step, place_s, begin, groups, per_group) * BLOCK
    slots = told_ref.shape[0]
    for s in range(BLOCK):
        slot = bucket_s[base + s]
        told = told_ref[pl.ds(jnp.minimum(slot, slots - 1), 1), :]
        packed_ref[s : s + 1, :] = jnp.where(
            slot < slots, told, jnp.full_like(told, both_s[base + s])
        )
    packed = packed_ref[...]
    width = query_ref.shape[2]
    heads = width // LANES
    span = SPAN * BLOCK
    valid = packed >> FIELD
    low = (CACHE - (packed[:, :1] & ((1 << FIELD) - 1))) * BLOCK
    high = (CACHE + valid[:, :1]) * BLOCK
    offset = lax.broadcasted_iota(jnp.int32, (BLOCK, span), 1) - lax.broadcasted_iota(
        jnp.int32, (BLOCK, span), 0
    )
    allowed = ((offset & (BLOCK - 1)) == 0) & (offset >= low) & (offset < high)
    bias = jnp.where(allowed, 0.0, masked_score)[None]
    padding = jnp.zeros(((SPAN - CACHE - FRAMES) * BLOCK, LANES), jnp.bfloat16)

    def joined(old_ref, new_ref, lanes):
        return jnp.concatenate(
            [
                old_ref[:, :, lanes].reshape(CACHE * BLOCK, LANES),
                new_ref[:, :, lanes].reshape(FRAMES * BLOCK, LANES),
                padding,
            ],
            axis=0,
        )

    contexts = []
    for h in range(heads):
        lanes = slice(h * LANES, (h + 1) * LANES)
        scores = lax.dot_general(
            query_ref[:, :, lanes].reshape(FRAMES * BLOCK, LANES),
            joined(key_ref, key_new_ref, lanes),
            (((1,), (1,)), ((), ())),
            preferred_element_type=jnp.float32,
        )
        scores = scores.reshape(FRAMES, BLOCK, span) * (1.0 / math.sqrt(HEAD)) + bias
        exponent = jnp.exp(scores - jnp.max(scores, axis=2, keepdims=True))
        weights = exponent * (1.0 / jnp.sum(exponent, axis=2, keepdims=True))
        context = lax.dot_general(
            weights.astype(jnp.bfloat16).reshape(FRAMES * BLOCK, span),
            joined(value_ref, value_new_ref, lanes),
            (((1,), (0,)), ((), ())),
            preferred_element_type=jnp.float32,
        )
        contexts.append(context.reshape(FRAMES, BLOCK, LANES).astype(jnp.bfloat16))

    shift = valid - 1
    first = ((shift & 1) != 0)[None]
    second = ((shift & 2) != 0)[None]
    third = ((shift & 4) != 0)[None]
    edge = CACHE - FRAMES
    for old_ref, new_ref, out_ref in (
        (key_ref, key_new_ref, key_out_ref),
        (value_ref, value_new_ref, value_out_ref),
    ):
        for h in range(heads):
            lanes = slice(h * LANES, (h + 1) * LANES)
            old = old_ref[edge + 1 :, :, lanes].astype(jnp.float32)
            new = new_ref[:, :, lanes].astype(jnp.float32)
            rows = jnp.concatenate([old, new, new[:1]], axis=0)
            out_ref[:, :, lanes] = shift_rows(rows, first, second, third).astype(jnp.bfloat16)

    @pl.when(step < per_group)
    def _():
        for h, context in enumerate(contexts):
            near_ref[:, :, h * LANES : (h + 1) * LANES] = context

    @pl.when(step >= per_group)
    def _():
        for h, context in enumerate(contexts):
            far_ref[:, :, h * LANES : (h + 1) * LANES] = context


def chosen_block(i, place_s, begin, groups, per_group):
    return ((place_s[0] + begin + i // per_group) % groups) * per_group + i % per_group


def attend(begin, where, bucket, both, told, new, caches, groups, earlier=()):
    stream_count = caches[0].shape[1]
    width = caches[0].shape[2]
    share = stream_count // groups
    per_group = share // BLOCK

    def at(i, place_s):
        return chosen_block(i, place_s, begin, groups, per_group)

    def block(rows):
        return pl.BlockSpec((rows, BLOCK, width), lambda i, p, *_: (0, at(i, p), 0))

    part = (FRAMES, BLOCK, width)
    context = jax.ShapeDtypeStruct((FRAMES, share, width), jnp.bfloat16)
    slab = jax.ShapeDtypeStruct((FRAMES, stream_count, width), jnp.bfloat16)
    return pl.pallas_call(
        functools.partial(attend_body, begin=begin, groups=groups, per_group=per_group),
        grid_spec=pltpu.PrefetchScalarGridSpec(
            num_scalar_prefetch=3,
            grid=(2 * per_group,),
            in_specs=[pl.BlockSpec(told.shape, lambda i, *_: (0, 0))]
            + [block(FRAMES)] * 3
            + [block(CACHE)] * 2
            + [pl.BlockSpec(memory_space=pl.ANY)] * len(earlier),
            out_specs=[
                pl.BlockSpec(part, lambda i, *_: (0, jnp.minimum(i, per_group - 1), 0)),
                pl.BlockSpec(part, lambda i, *_: (0, jnp.maximum(i - per_group, 0), 0)),
                block(FRAMES),
                block(FRAMES),
                pl.BlockSpec((BLOCK, LANES), lambda i, p, *_: (at(i, p), 0)),
            ],
        ),
        out_shape=[
            context,
            context,
            slab,
            slab,
            jax.ShapeDtypeStruct((stream_count, LANES), jnp.int32),
        ],
        input_output_aliases={9 + k: 2 + k for k in range(len(earlier))},
        name="attend_b" if earlier else "attend_a",
    )(where, bucket, both, told, *new, *caches, *earlier)


def bounds(rank_s, base):
    return jnp.where(base == 0, 0, rank_s[jnp.maximum(base - 1, 0)]), rank_s[base + BLOCK - 1]


def pack_body(slot_s, list_s, rank_s, key_ref, value_ref, send_ref, rows_f):
    base = pl.program_id(0) * BLOCK
    heads = rows_f.shape[1]
    for kind, src in enumerate((key_ref, value_ref)):
        for h in range(heads):
            rows_f[kind, h, : CACHE * BLOCK, :] = (
                src[:, :, h * LANES : (h + 1) * LANES]
                .astype(jnp.float32)
                .reshape(CACHE * BLOCK, LANES)
            )

    def pack(k, carry):
        s = list_s[k] - base
        slot = slot_s[base + s]
        for kind in range(2):
            for h in range(heads):
                send_ref[slot, kind, :, h * LANES : (h + 1) * LANES] = rows_f[
                    kind, h, pl.ds(s, KEEP, stride=BLOCK), :
                ].astype(jnp.bfloat16)
        return carry

    lax.fori_loop(*bounds(rank_s, base), pack, 0)


def pack_rows(leaving, key_cache, value_cache, slots):
    stream_count = key_cache.shape[1]
    width = key_cache.shape[2]
    block = pl.BlockSpec((CACHE, BLOCK, width), lambda i, *_: (0, i, 0))
    return pl.pallas_call(
        pack_body,
        grid_spec=pltpu.PrefetchScalarGridSpec(
            num_scalar_prefetch=3,
            grid=(stream_count // BLOCK,),
            in_specs=[block, block],
            out_specs=pl.BlockSpec((slots, 2, KEEP, width), lambda i, *_: (0, 0, 0, 0)),
            scratch_shapes=[
                pltpu.VMEM((2, width // HEAD, KEEP * BLOCK, LANES), jnp.float32)
            ],
        ),
        out_shape=jax.ShapeDtypeStruct((slots, 2, KEEP, width), jnp.bfloat16),
        name="pack",
    )(*leaving, key_cache, value_cache)


def place_body(
    arrival_s, list_s, rank_s, got_ref, valid_ref, key_ref, value_ref, key_out_ref, value_out_ref, rows_f
):
    base = pl.program_id(0) * BLOCK
    heads = rows_f.shape[1]
    for kind, src in enumerate((key_ref, value_ref)):
        for h in range(heads):
            lanes = slice(h * LANES, (h + 1) * LANES)
            for start in range(0, CACHE, CHUNK):
                rows_f[kind, h, start * BLOCK : (start + CHUNK) * BLOCK, :] = (
                    src[start : start + CHUNK, :, lanes]
                    .astype(jnp.float32)
                    .reshape(CHUNK * BLOCK, LANES)
                )

    def fetch(k, carry):
        s = list_s[k] - base
        slot = arrival_s[base + s]
        for kind in range(2):
            for h in range(heads):
                rows_f[kind, h, pl.ds(s, KEEP, stride=BLOCK), :] = got_ref[
                    slot, kind, :, h * LANES : (h + 1) * LANES
                ].astype(jnp.float32)
        return carry

    lax.fori_loop(*bounds(rank_s, base), fetch, 0)
    shift = valid_ref[...] - 1
    first = ((shift & 1) != 0)[None]
    second = ((shift & 2) != 0)[None]
    third = ((shift & 4) != 0)[None]
    edge = CACHE - FRAMES
    for kind, dst in enumerate((key_out_ref, value_out_ref)):
        for h in range(heads):
            lanes = slice(h * LANES, (h + 1) * LANES)
            for start in range(0, edge, 9):
                rows = rows_f[kind, h, (start + 1) * BLOCK : (start + 17) * BLOCK, :]
                rows = shift_rows(rows.reshape(16, BLOCK, LANES), first, second, third)
                dst[start : start + 9, :, lanes] = rows.astype(jnp.bfloat16)
            dst[edge:, :, lanes] = jnp.zeros((FRAMES, BLOCK, LANES), jnp.bfloat16)


def place(coming, valid_wide, received, key_rows, value_rows):
    stream_count = key_rows.shape[1]
    width = key_rows.shape[2]
    heads = width // HEAD
    slots = received.shape[0]
    block = pl.BlockSpec((CACHE, BLOCK, width), lambda i, *_: (0, i, 0))
    shape = jax.ShapeDtypeStruct((CACHE, stream_count, width), jnp.bfloat16)
    return pl.pallas_call(
        place_body,
        grid_spec=pltpu.PrefetchScalarGridSpec(
            num_scalar_prefetch=3,
            grid=(stream_count // BLOCK,),
            in_specs=[
                pl.BlockSpec((slots, 2, KEEP, width), lambda i, *_: (0, 0, 0, 0)),
                pl.BlockSpec((BLOCK, LANES), lambda i, *_: (i, 0)),
                block,
                block,
            ],
            out_specs=[block, block],
            scratch_shapes=[pltpu.VMEM((2, heads, KEEP * BLOCK, LANES), jnp.float32)],
        ),
        out_shape=[shape, shape],
        name="place",
    )(
        *coming,
        received,
        valid_wide,
        key_rows,
        value_rows,
    )


def head_body(
    place_s, frames_ref, own_ref, near_ref, far_ref, next_ref, gain_ref, *rest
):
    weights, outs, inputs_ref, flat, raw, normed = rest[:3], rest[3:6], *rest[6:]
    member = place_s[0]
    groups = raw.shape[0]
    width = raw.shape[2]
    count, taps, streams = frames_ref.shape
    for t in range(count):
        flat[t * streams : (t + 1) * streams, :] = jnp.transpose(frames_ref[t])
    for offset, piece in enumerate((own_ref, near_ref, far_ref, next_ref)):
        total = jnp.dot(flat[...], piece[:taps, :], preferred_element_type=jnp.float32)
        total = total + piece[taps : taps + 16, :].astype(jnp.float32)[:1]
        raw[(member + groups - offset) % groups] = total.astype(jnp.bfloat16)
    model_width = groups * width
    share = inputs_ref.shape[1]
    for t in range(count):
        lines = slice(t * streams, (t + 1) * streams)
        values = [raw[g, lines, :].astype(jnp.float32) for g in range(groups)]
        average = sum(jnp.sum(v, axis=1, keepdims=True) for v in values) * (1.0 / model_width)
        values = [v - average for v in values]
        spread = sum(jnp.sum(v * v, axis=1, keepdims=True) for v in values) * (1.0 / model_width)
        scale = lax.rsqrt(spread + 1e-05)
        for g, v in enumerate(values):
            columns = slice(g * width, (g + 1) * width)
            normed[lines, columns] = (v * scale * gain_ref[:, columns]).astype(jnp.bfloat16)
            start = pl.multiple_of(t * streams + member * share, share)
            inputs_ref[t, :, columns] = raw[g, pl.ds(start, share), :]
    for matrix, out in zip(weights, outs):
        product = jnp.dot(normed[...], matrix[...], preferred_element_type=jnp.float32)
        out[...] = product.astype(jnp.bfloat16).reshape(count, streams, width)


def head(where, frames, pieces, gain, matrices):
    count, taps, streams = frames.shape
    width = matrices[0].shape[1]
    groups = len(pieces)

    def whole(array):
        zeros = (0,) * array.ndim
        return pl.BlockSpec(array.shape, lambda i, *_: zeros)

    gain = gain[None, :]
    shapes = [jax.ShapeDtypeStruct((count, streams, width), jnp.bfloat16)] * 3
    shapes.append(
        jax.ShapeDtypeStruct((count, streams // groups, groups * width), jnp.bfloat16)
    )
    return pl.pallas_call(
        head_body,
        grid_spec=pltpu.PrefetchScalarGridSpec(
            num_scalar_prefetch=1,
            grid=(1,),
            in_specs=[whole(frames)]
            + [pl.BlockSpec((taps + 16, width), lambda i, *_: (0, 0))] * groups
            + [whole(gain)]
            + [whole(w) for w in matrices],
            out_specs=[whole(a) for a in shapes],
            scratch_shapes=[
                pltpu.VMEM((count * streams, taps), jnp.bfloat16),
                pltpu.VMEM((groups, count * streams, width), jnp.bfloat16),
                pltpu.VMEM((count * streams, groups * width), jnp.bfloat16),
            ],
        ),
        out_shape=shapes,
        name="head",
    )(where, frames, *pieces, gain, *matrices)


def tail_body(place_s, *refs):
    contexts, pieces, rest = refs[:4], refs[4:8], refs[8:]
    inputs_ref, gain_ref, packed_ref = rest[:3]
    attn_ref, conv_ref, value_ref, gate_ref = rest[3:7]
    ring_refs, outs = rest[7:13], rest[13:17]
    out_ref, cache_f = rest[17:]
    member = place_s[0]
    front_half = place_s[1] == 0
    groups = len(contexts)
    _, share, width = contexts[0].shape
    rows = FRAMES * share
    size = groups * width
    half = width // 2

    def ordered(operand):
        middle_lane = operand.shape[1] // 2
        low, high = operand[:, :middle_lane], operand[:, middle_lane:]
        return jnp.where(front_half, low, high), jnp.where(front_half, high, low)

    def dot(left, right):
        return jnp.dot(left, right, preferred_element_type=jnp.float32)

    def grouped(step, operand, own_ref, start, sums):
        sides = ordered(operand)
        for n in range(groups):
            if step == 0:
                part = dot(operand, own_ref[:, n * width : (n + 1) * width])
            else:
                at = start + n * half
                part = sum(
                    dot(side, ring_refs[2 * (step - 1) + i][at : at + half, :])
                    for i, side in enumerate(sides)
                )
            part = part.astype(jnp.bfloat16).astype(jnp.float32)
            sums[n] = part if sums[n] is None else sums[n] + part

    def wide(step, own_ref, order):
        if step == 0:
            return dot(normed, own_ref[...])
        at = size + order * (size // 2)
        return sum(
            dot(side, ring_refs[2 * (step - 1) + i][at : at + size // 2, :])
            for i, side in enumerate(normed_sides)
        )

    attended = [None] * groups
    for step in range(groups):
        grouped(step, contexts[step][...].reshape(rows, width), attn_ref, 0, attended)
    middle = []
    for n in range(groups):
        inputs = inputs_ref[:, :, n * width : (n + 1) * width].reshape(rows, width)
        middle.append((inputs.astype(jnp.float32) + attended[n]).astype(jnp.bfloat16))
    values = [m.astype(jnp.float32) for m in middle]
    average = sum(jnp.sum(v, axis=1, keepdims=True) for v in values) * (1.0 / size)
    values = [v - average for v in values]
    spread = sum(jnp.sum(v * v, axis=1, keepdims=True) for v in values) * (1.0 / size)
    scale = lax.rsqrt(spread + 1e-05)
    normed = jnp.concatenate(
        [
            (v * scale * gain_ref[:, n * width : (n + 1) * width]).astype(jnp.bfloat16)
            for n, v in enumerate(values)
        ],
        axis=1,
    )
    normed_sides = ordered(normed)
    valid = packed_ref[pl.ds(pl.multiple_of(member * share, share), share), :] >> FIELD
    valid = jnp.concatenate([valid] * (width // LANES), axis=1)
    shift = valid - 1
    first = ((shift & 1) != 0)[None]
    second = ((shift & 2) != 0)[None]
    third = ((shift & 4) != 0)[None]
    conv_term = [None] * groups
    extra = SUB * MELS + 16
    tail_rows = extra + 3 * 16
    for step in range(groups):
        group = (member + groups - step) % groups
        piece = pieces[step]
        small = sum(
            piece[extra + 16 * i : extra + 16 * (i + 1), :].astype(jnp.float32) for i in range(3)
        )
        for h in range(width // LANES):
            cache_f[h] = piece[tail_rows:, h * LANES : (h + 1) * LANES].astype(jnp.float32)
        cached = jnp.concatenate(
            [
                jnp.stack(
                    [cache_f[h, pl.ds(t, share, stride=CONV_CACHE), :] for t in range(CONV_CACHE)]
                )
                for h in range(width // LANES)
            ],
            axis=2,
        )
        glu_value = wide(step, value_ref, 0)
        glu_gate = wide(step, gate_ref, 1)
        gated = (glu_value * jax.nn.sigmoid(glu_gate)).astype(jnp.bfloat16)
        conv_in = jnp.concatenate(
            [
                cached,
                gated.astype(jnp.float32).reshape(FRAMES, share, width),
            ],
            axis=0,
        )
        depthwise = jnp.zeros((FRAMES, share, width), jnp.float32)
        for tap in range(KERNEL):
            depthwise = depthwise + small[tap : tap + 1, :][None] * conv_in[tap : tap + FRAMES]
        shaped = depthwise * small[KERNEL : KERNEL + 1, :][None]
        shaped = shaped + small[KERNEL + 1 : KERNEL + 2, :][None]
        activated = (shaped * jax.nn.sigmoid(shaped)).astype(jnp.bfloat16)
        grouped(step, activated.reshape(rows, width), conv_ref, size // 2, conv_term)
        moved = shift_rows(
            jnp.concatenate([conv_in[1:], conv_in[-1:]], axis=0), first, second, third
        )
        out_ref[group, FRAMES:, :, :] = moved.astype(jnp.bfloat16)
    frame = lax.broadcasted_iota(jnp.int32, (FRAMES, share, width), 0)
    for n in range(groups):
        total = (middle[n].astype(jnp.float32) + conv_term[n]).reshape(FRAMES, share, width)
        out_ref[n, :FRAMES, :, :] = jnp.where(frame < valid[None], total, 0.0).astype(jnp.bfloat16)


    for step, out in enumerate(outs):
        out[...] = out_ref[(member + step) % groups]


def tail(where, groups, *arrays):
    _, share, width = arrays[0].shape
    shape = (FRAMES + CONV_CACHE, share, width)
    vmem = pl.BlockSpec(memory_space=pltpu.VMEM)
    return pl.pallas_call(
        tail_body,
        in_specs=[pl.BlockSpec(memory_space=pltpu.SMEM)] + [vmem] * len(arrays),
        out_specs=[vmem] * groups,
        out_shape=[jax.ShapeDtypeStruct(shape, jnp.bfloat16)] * groups,
        scratch_shapes=[
            pltpu.VMEM((groups,) + shape, jnp.bfloat16),
            pltpu.VMEM((width // LANES, CONV_CACHE * share, LANES), jnp.float32),
        ],
        name="tail",
    )(where, *arrays)


def collect_body(slot_s, list_s, rank_s, place_s, *refs):
    pieces, slabs, (all_ref, send_ref, rows_f) = refs[:4], refs[4:6], refs[6:]
    member = place_s[0]
    groups = len(pieces)
    frames, share, _ = pieces[0].shape
    heads, _, _ = rows_f.shape
    _, keep, _ = send_ref.shape
    count = groups * share
    for step, piece in enumerate(pieces):
        start = pl.multiple_of(((member + groups - step) % groups) * share, share)
        all_ref[:frames, pl.ds(start, share), :] = piece[...]
        for h in range(heads):
            for t in range(frames):
                rows_f[h, pl.ds(pl.multiple_of(t * count + start, share), share), :] = piece[
                    t, :, h * LANES : (h + 1) * LANES
                ].astype(jnp.float32)
    for slab in slabs:
        all_ref[frames : frames + FRAMES] = slab[...]
        for h in range(heads):
            rows_f[h, frames * count : (frames + FRAMES) * count, :] = (
                slab[:, :, h * LANES : (h + 1) * LANES]
                .astype(jnp.float32)
                .reshape(FRAMES * count, LANES)
            )
        frames += FRAMES

    def pack(k, carry):
        s = list_s[k]
        slot = slot_s[s]
        for h in range(heads):
            send_ref[slot, :, h * LANES : (h + 1) * LANES] = rows_f[
                h, pl.ds(s, keep, stride=count), :
            ].astype(jnp.bfloat16)
        return carry

    lax.fori_loop(0, rank_s[count - 1], pack, 0)


def collect(leaving, where, pieces, slabs, slots):
    frames = FRAMES + CONV_CACHE + 2 * FRAMES
    keep = -(-frames // 16) * 16
    _, count, width = slabs[0].shape
    smem = pl.BlockSpec(memory_space=pltpu.SMEM)
    vmem = pl.BlockSpec(memory_space=pltpu.VMEM)
    return pl.pallas_call(
        collect_body,
        in_specs=[smem] * 4 + [vmem] * 6,
        out_specs=[vmem, vmem],
        out_shape=[
            jax.ShapeDtypeStruct((frames, count, width), jnp.bfloat16),
            jax.ShapeDtypeStruct((slots, keep, width), jnp.bfloat16),
        ],
        scratch_shapes=[pltpu.VMEM((width // LANES, keep * count, LANES), jnp.float32)],
        name="collect",
    )(*leaving, where, *pieces, *slabs)


def finish_body(
    slot_s, list_s, rank_s, all_ref, got_ref, _, __, encoded_ref, conv_ref, key_ref, value_ref, rows_f, conv_f
):
    heads = rows_f.shape[0]
    frames, count, _ = all_ref.shape
    keep = got_ref.shape[1]
    for h in range(heads):
        rows_f[h, : frames * count, :] = (
            all_ref[:, :, h * LANES : (h + 1) * LANES]
            .astype(jnp.float32)
            .reshape(frames * count, LANES)
        )

    def fetch(k, carry):
        s = list_s[k]
        slot = slot_s[s]
        for h in range(heads):
            rows_f[h, pl.ds(s, keep, stride=count), :] = got_ref[
                slot, :, h * LANES : (h + 1) * LANES
            ].astype(jnp.float32)
        return carry

    lax.fori_loop(0, rank_s[count - 1], fetch, 0)
    ends = FRAMES + CONV_CACHE
    for h in range(heads):
        lanes = slice(h * LANES, (h + 1) * LANES)
        for start, out in ((0, encoded_ref), (ends, key_ref), (ends + FRAMES, value_ref)):
            rows = rows_f[h, start * count : (start + FRAMES) * count, :]
            out[:, :, lanes] = rows.reshape(FRAMES, count, LANES).astype(jnp.bfloat16)
        for t in range(CONV_CACHE):
            at = (FRAMES + t) * count
            conv_f[pl.ds(t, count, stride=CONV_CACHE), :] = rows_f[h, at : at + count, :]
        conv_ref[:, :, lanes] = (
            conv_f[...].reshape(count, CONV_CACHE, LANES).astype(jnp.bfloat16)
        )


def finish(coming, everything, received, key_done, value_done):
    _, count, width = everything.shape
    keep = received.shape[1]
    smem = pl.BlockSpec(memory_space=pltpu.SMEM)
    vmem = pl.BlockSpec(memory_space=pltpu.VMEM)
    kept = pl.BlockSpec(memory_space=pl.ANY)
    slab = pl.BlockSpec((FRAMES, count, width), lambda i: (CACHE // FRAMES - 1, 0, 0))
    return pl.pallas_call(
        finish_body,
        grid=(1,),
        in_specs=[smem] * 3 + [vmem, vmem, kept, kept],
        out_specs=[vmem, vmem, slab, slab],
        out_shape=[
            jax.ShapeDtypeStruct((FRAMES, count, width), jnp.bfloat16),
            jax.ShapeDtypeStruct((count, CONV_CACHE, width), jnp.bfloat16),
            jax.ShapeDtypeStruct(key_done.shape, jnp.bfloat16),
            jax.ShapeDtypeStruct(value_done.shape, jnp.bfloat16),
        ],
        scratch_shapes=[
            pltpu.VMEM((width // LANES, keep * count, LANES), jnp.float32),
            pltpu.VMEM((CONV_CACHE * count, LANES), jnp.float32),
        ],
        input_output_aliases={5: 2, 6: 3},
        name="finish",
    )(*coming, everything, received, key_done, value_done)


def toward(array, steps, count):
    return lax.ppermute(array, "enc", [(i, (i + steps) % count) for i in range(count)])


def on_device(
    spectra,
    sub_weight,
    sub_bias,
    key_cache,
    value_cache,
    conv_cache,
    new_slot,
    old_slot,
    valid_new,
    cache_fill,
    ln1_gain,
    w_query,
    w_key,
    w_value,
    w_attn_out,
    ln2_gain,
    w_glu_value,
    w_glu_gate,
    depth_kernel,
    norm_scale,
    norm_shift,
    w_conv_out,
):
    peer_count = lax.axis_size("front")
    own_index = lax.axis_index("front")
    member = lax.axis_index("enc")
    stream_count = spectra.shape[0]
    local_width = w_query.shape[1]
    slots = peer_count * CAP
    groups = lax.axis_size("enc")
    core = own_index % 2
    where = jnp.stack([member, core, own_index])
    share = stream_count // groups
    payloads, maps, valid_wide, asked, stack = prepare(
        where,
        (new_slot, old_slot, valid_new, cache_fill),
        (sub_weight, sub_bias),
        (depth_kernel, norm_scale, norm_shift),
        conv_cache.reshape(groups, share * CONV_CACHE, local_width),
        (w_attn_out, w_conv_out),
        (w_glu_value, w_glu_gate),
        slots,
    )
    both, bucket, leaving, coming = maps[0], maps[1], maps[1:4], maps[4:7]
    pieces = [payloads[0]] + [toward(payloads[k], k, groups) for k in range(1, groups)]
    told = lax.all_to_all(asked, "front", split_axis=0, concat_axis=0, tiled=True)
    key_rows = key_cache.transpose(1, 0, 2)
    value_rows = value_cache.transpose(1, 0, 2)
    leaving_rows = pack_rows(leaving, key_rows, value_rows, slots)
    received = lax.all_to_all(leaving_rows, "front", split_axis=0, concat_axis=0, tiled=True)
    taps = SUB * MELS

    def other_core(array):
        return lax.ppermute(array, "front", [(i, i ^ 1) for i in range(peer_count)])

    near = toward(stack, 1, groups)
    after = toward(stack, -1, groups)
    far = toward(after, -1, groups)
    after_other = other_core(after)
    near_other = other_core(near)
    far_other = other_core(far)
    frames = spectra.transpose(1, 2, 0).reshape(FRAMES, taps, stream_count)
    queries, key_new, value_new, inputs = head(
        where, frames, pieces, ln1_gain, (w_query, w_key, w_value)
    )
    new = (queries, key_new, value_new)
    caches = (key_rows, value_rows)
    first, second, *earlier = attend(1, where, bucket, both, told, new, caches, groups)
    context = [toward(first, 1, groups), toward(second, 2, groups)]
    third, own, key_slab, value_slab, packed = attend(
        groups - 1, where, bucket, both, told, new, caches, groups, earlier
    )
    context = [own] + context + [toward(third, groups - 1, groups)]
    ended = tail(
        where,
        groups,
        *context,
        *pieces,
        inputs,
        ln2_gain[None, :],
        packed,
        w_attn_out,
        w_conv_out,
        w_glu_value,
        w_glu_gate,
        near,
        near_other,
        far,
        far_other,
        after,
        after_other,
    )
    ended = [ended[0]] + [toward(ended[k], k, groups) for k in range(1, groups)]
    everything, leaving_end = collect(leaving, where, ended, (key_slab, value_slab), slots)
    received_end = lax.all_to_all(leaving_end, "front", split_axis=0, concat_axis=0, tiled=True)
    key_done, value_done = place(coming, valid_wide, received, key_rows, value_rows)
    encoded, conv_out, key_done, value_done = finish(
        coming, everything, received_end, key_done, value_done
    )
    return (
        encoded.transpose(1, 0, 2),
        key_done.transpose(1, 0, 2),
        value_done.transpose(1, 0, 2),
        conv_out,
    )


def solution(mesh):
    in_specs = (
        P("front", None, None),
        P(None, "enc"),
        P("enc"),
        P("front", None, "enc"),
        P("front", None, "enc"),
        P("front", None, "enc"),
        P("front"),
        P("front"),
        P("front"),
        P("front"),
        P(),
        P(None, "enc"),
        P(None, "enc"),
        P(None, "enc"),
        P("enc", None),
        P(),
        P(None, "enc"),
        P(None, "enc"),
        P(None, "enc"),
        P("enc"),
        P("enc"),
        P("enc", None),
    )
    out_specs = (
        P("front", None, "enc"),
        P("front", None, "enc"),
        P("front", None, "enc"),
        P("front", None, "enc"),
    )

    return jax.shard_map(
        on_device, mesh=mesh, in_specs=in_specs, out_specs=out_specs, check_vma=False
    )
```

```python
import functools
import math

import jax
import jax.numpy as jnp
from jax import lax
from jax.experimental import pallas as pl
from jax.experimental.pallas import tpu as pltpu
from jax.sharding import PartitionSpec as P


MELS = 80
KERNEL = 9
SUB = 8
FRAMES = 7
CACHE = 70
CAP = 2
HEAD = 128
CONV_CACHE = 8
LANES = 128
BLOCK = 16
SPAN = 80
KEEP = 72
CHUNK = 10
FIELD = 7

masked_score = -1e30


def prepare_body(
    place_s,
    new_ref,
    old_ref,
    valid_ref,
    fill_ref,
    weight_ref,
    bias_ref,
    kernel_ref,
    scale_ref,
    shift_ref,
    cache_ref,
    attn_ref,
    conv_ref,
    value_ref,
    gate_ref,
    *refs,
):
    payloads, maps, (wide_ref, asked_ref, stack_ref, small) = refs[:4], refs[4:11], refs[11:]
    both_ref, bucket_ref, out_ref, out_rank_ref, arrival_ref, in_ref, in_rank_ref = maps
    member, own = place_s[0], place_s[2]
    groups = len(payloads)
    taps, width = weight_ref.shape
    slots, count = asked_ref.shape
    bits = count.bit_length() - 1

    small[:KERNEL, :] = kernel_ref[...]
    small[KERNEL : KERNEL + 1, :] = scale_ref[...]
    small[KERNEL + 1 : KERNEL + 2, :] = shift_ref[...]
    small[KERNEL + 2 :, :] = jnp.zeros((16 - KERNEL - 2, width), jnp.float32)
    rest = small[...]
    bias = bias_ref[...].astype(jnp.float32).reshape(1, width)
    bias = jnp.broadcast_to(bias, (16, width)).astype(jnp.bfloat16)
    parts = []
    for _ in range(3):
        part = rest.astype(jnp.bfloat16)
        parts.append(part)
        rest = rest - part.astype(jnp.float32)
    for step, payload in enumerate(payloads):
        payload[:taps, :] = weight_ref[...]
        payload[taps : taps + 16, :] = bias
        for i, part in enumerate(parts):
            payload[taps + 16 * (i + 1) : taps + 16 * (i + 2), :] = part
        payload[taps + 64 :, :] = cache_ref[(member + step) % groups]

    half = attn_ref.shape[0]
    for start, source in ((0, attn_ref), (groups * half, conv_ref)):
        for n in range(groups):
            at = start + n * half
            stack_ref[at : at + half, :] = source[:, n * width : (n + 1) * width]
    at = 2 * groups * half
    stack_ref[at : at + value_ref.shape[0], :] = value_ref[...]
    stack_ref[at + value_ref.shape[0] :, :] = gate_ref[...]

    def column(row):
        return jnp.transpose(jnp.broadcast_to(row, (count, count)))

    def ranked(group_column, group_row, before):
        same = jnp.where((group_column == group_row) & before, 1.0, 0.0)
        return jnp.sum(same, axis=0, keepdims=True).astype(jnp.int32)

    first = lax.broadcasted_iota(jnp.int32, (count, count), 0)
    second = lax.broadcasted_iota(jnp.int32, (count, count), 1)

    def inverse(row):
        hit = jnp.where(column(row) == second, (first + 1).astype(jnp.float32), 0.0)
        return jnp.sum(hit, axis=0, keepdims=True).astype(jnp.int32) - 1

    def listed(chosen, list_ref, rank_ref):
        marks = column(jnp.where(chosen, 1, 0)).astype(jnp.float32)
        rank = jnp.sum(jnp.where(first <= second, marks, 0.0), axis=0, keepdims=True)
        rank = rank.astype(jnp.int32)
        rank_ref[...] = rank
        list_ref[...] = inverse(jnp.where(chosen, rank - 1, -1))

    valid = valid_ref[...]
    wide_ref[...] = column(valid)
    both = valid * (1 << FIELD) + fill_ref[...]
    both_ref[...] = both
    target = new_ref[...] >> bits
    position = ranked(column(target), target, first < second)
    bucket = jnp.where(target != own, target * CAP + position, slots)
    bucket_ref[...] = bucket
    listed(target != own, out_ref, out_rank_ref)
    old_row = old_ref[...]
    old_column = column(old_row)
    source = old_row >> bits
    position = ranked(old_column >> bits, source, old_column < old_row)
    arrival = jnp.where(source == own, -1, source * CAP + position)
    arrival_ref[...] = arrival
    listed(source != own, in_ref, in_rank_ref)
    slot = lax.broadcasted_iota(jnp.int32, (slots, count), 0)
    hit = jnp.where(arrival == slot, both.astype(jnp.float32), 0.0)
    asked = jnp.sum(hit, axis=1, keepdims=True).astype(jnp.int32)
    asked_ref[...] = jnp.broadcast_to(asked, (slots, count))


def prepare(where, rows, sub, conv, chunks, columns, tall, slots):
    count = rows[0].shape[0]
    groups, chunk_rows, width = chunks.shape
    taps = sub[0].shape[0]
    whole = [r[None] for r in rows] + [sub[0], sub[1], conv[0], conv[1][None], conv[2][None]]

    def full(array):
        zeros = (0,) * array.ndim
        return pl.BlockSpec(array.shape, lambda i, place_s: zeros)

    def my_half(array):
        return pl.BlockSpec(
            (array.shape[0] // 2, array.shape[1]), lambda i, place_s: (place_s[1], 0)
        )

    row = jax.ShapeDtypeStruct((1, count), jnp.int32)
    payload = jax.ShapeDtypeStruct((taps + 64 + chunk_rows, width), jnp.bfloat16)
    shapes = [payload] * groups + [row] * 7
    shapes.append(jax.ShapeDtypeStruct((count, count), jnp.int32))
    shapes.append(jax.ShapeDtypeStruct((slots, count), jnp.int32))
    shapes.append(jax.ShapeDtypeStruct((2 * groups * width, width), jnp.bfloat16))
    outs = pl.pallas_call(
        prepare_body,
        grid_spec=pltpu.PrefetchScalarGridSpec(
            num_scalar_prefetch=1,
            grid=(1,),
            in_specs=[full(a) for a in whole]
            + [full(chunks)]
            + [my_half(a) for a in columns + tall],
            out_specs=[full(a) for a in shapes],
            scratch_shapes=[pltpu.VMEM((16, width), jnp.float32)],
        ),
        out_shape=shapes,
        name="prepare",
    )(where, *whole, chunks, *columns, *tall)
    return outs[:groups], [r[0] for r in outs[groups : groups + 7]], *outs[-3:]


def shift_rows(rows, first, second, third):
    rows = jnp.where(first, rows[1:], rows[:-1])
    rows = jnp.where(second, rows[2:], rows[:-2])
    return jnp.where(third, rows[4:], rows[:-4])


def attend_body(
    place_s,
    bucket_s,
    both_s,
    told_ref,
    query_ref,
    key_new_ref,
    value_new_ref,
    key_ref,
    value_ref,
    *rest,
    begin,
    groups,
    per_group,
):
    near_ref, far_ref, key_out_ref, value_out_ref, packed_ref = rest[-5:]
    step = pl.program_id(0)
    base = chosen_block(step, place_s, begin, groups, per_group) * BLOCK
    slots = told_ref.shape[0]
    for s in range(BLOCK):
        slot = bucket_s[base + s]
        told = told_ref[pl.ds(jnp.minimum(slot, slots - 1), 1), :]
        packed_ref[s : s + 1, :] = jnp.where(
            slot < slots, told, jnp.full_like(told, both_s[base + s])
        )
    packed = packed_ref[...]
    width = query_ref.shape[2]
    heads = width // LANES
    span = SPAN * BLOCK
    valid = packed >> FIELD
    low = (CACHE - (packed[:, :1] & ((1 << FIELD) - 1))) * BLOCK
    high = (CACHE + valid[:, :1]) * BLOCK
    offset = lax.broadcasted_iota(jnp.int32, (BLOCK, span), 1) - lax.broadcasted_iota(
        jnp.int32, (BLOCK, span), 0
    )
    allowed = ((offset & (BLOCK - 1)) == 0) & (offset >= low) & (offset < high)
    bias = jnp.where(allowed, 0.0, masked_score)[None]
    padding = jnp.zeros(((SPAN - CACHE - FRAMES) * BLOCK, LANES), jnp.bfloat16)

    def joined(old_ref, new_ref, lanes):
        return jnp.concatenate(
            [
                old_ref[:, :, lanes].reshape(CACHE * BLOCK, LANES),
                new_ref[:, :, lanes].reshape(FRAMES * BLOCK, LANES),
                padding,
            ],
            axis=0,
        )

    contexts = []
    for h in range(heads):
        lanes = slice(h * LANES, (h + 1) * LANES)
        scores = lax.dot_general(
            query_ref[:, :, lanes].reshape(FRAMES * BLOCK, LANES),
            joined(key_ref, key_new_ref, lanes),
            (((1,), (1,)), ((), ())),
            preferred_element_type=jnp.float32,
        )
        scores = scores.reshape(FRAMES, BLOCK, span) * (1.0 / math.sqrt(HEAD)) + bias
        exponent = jnp.exp(scores - jnp.max(scores, axis=2, keepdims=True))
        weights = exponent * (1.0 / jnp.sum(exponent, axis=2, keepdims=True))
        context = lax.dot_general(
            weights.astype(jnp.bfloat16).reshape(FRAMES * BLOCK, span),
            joined(value_ref, value_new_ref, lanes),
            (((1,), (0,)), ((), ())),
            preferred_element_type=jnp.float32,
        )
        contexts.append(context.reshape(FRAMES, BLOCK, LANES).astype(jnp.bfloat16))

    shift = valid - 1
    first = ((shift & 1) != 0)[None]
    second = ((shift & 2) != 0)[None]
    third = ((shift & 4) != 0)[None]
    edge = CACHE - FRAMES
    for old_ref, new_ref, out_ref in (
        (key_ref, key_new_ref, key_out_ref),
        (value_ref, value_new_ref, value_out_ref),
    ):
        for h in range(heads):
            lanes = slice(h * LANES, (h + 1) * LANES)
            old = old_ref[edge + 1 :, :, lanes].astype(jnp.float32)
            new = new_ref[:, :, lanes].astype(jnp.float32)
            rows = jnp.concatenate([old, new, new[:1]], axis=0)
            out_ref[:, :, lanes] = shift_rows(rows, first, second, third).astype(jnp.bfloat16)

    @pl.when(step < per_group)
    def _():
        for h, context in enumerate(contexts):
            near_ref[:, :, h * LANES : (h + 1) * LANES] = context

    @pl.when(step >= per_group)
    def _():
        for h, context in enumerate(contexts):
            far_ref[:, :, h * LANES : (h + 1) * LANES] = context


def chosen_block(i, place_s, begin, groups, per_group):
    return ((place_s[0] + begin + i // per_group) % groups) * per_group + i % per_group


def attend(begin, where, bucket, both, told, new, caches, groups, earlier=()):
    stream_count = caches[0].shape[1]
    width = caches[0].shape[2]
    share = stream_count // groups
    per_group = share // BLOCK

    def at(i, place_s):
        return chosen_block(i, place_s, begin, groups, per_group)

    def block(rows):
        return pl.BlockSpec((rows, BLOCK, width), lambda i, p, *_: (0, at(i, p), 0))

    part = (FRAMES, BLOCK, width)
    context = jax.ShapeDtypeStruct((FRAMES, share, width), jnp.bfloat16)
    slab = jax.ShapeDtypeStruct((FRAMES, stream_count, width), jnp.bfloat16)
    return pl.pallas_call(
        functools.partial(attend_body, begin=begin, groups=groups, per_group=per_group),
        grid_spec=pltpu.PrefetchScalarGridSpec(
            num_scalar_prefetch=3,
            grid=(2 * per_group,),
            in_specs=[pl.BlockSpec(told.shape, lambda i, *_: (0, 0))]
            + [block(FRAMES)] * 3
            + [block(CACHE)] * 2
            + [pl.BlockSpec(memory_space=pl.ANY)] * len(earlier),
            out_specs=[
                pl.BlockSpec(part, lambda i, *_: (0, jnp.minimum(i, per_group - 1), 0)),
                pl.BlockSpec(part, lambda i, *_: (0, jnp.maximum(i - per_group, 0), 0)),
                block(FRAMES),
                block(FRAMES),
                pl.BlockSpec((BLOCK, LANES), lambda i, p, *_: (at(i, p), 0)),
            ],
        ),
        out_shape=[
            context,
            context,
            slab,
            slab,
            jax.ShapeDtypeStruct((stream_count, LANES), jnp.int32),
        ],
        input_output_aliases={9 + k: 2 + k for k in range(len(earlier))},
        name="attend_b" if earlier else "attend_a",
    )(where, bucket, both, told, *new, *caches, *earlier)


def bounds(rank_s, base):
    return jnp.where(base == 0, 0, rank_s[jnp.maximum(base - 1, 0)]), rank_s[base + BLOCK - 1]


def pack_body(slot_s, list_s, rank_s, key_ref, value_ref, send_ref, rows_f):
    base = pl.program_id(0) * BLOCK
    heads = rows_f.shape[1]
    for kind, src in enumerate((key_ref, value_ref)):
        for h in range(heads):
            rows_f[kind, h, : CACHE * BLOCK, :] = (
                src[:, :, h * LANES : (h + 1) * LANES]
                .astype(jnp.float32)
                .reshape(CACHE * BLOCK, LANES)
            )

    def pack(k, carry):
        s = list_s[k] - base
        slot = slot_s[base + s]
        for kind in range(2):
            for h in range(heads):
                send_ref[slot, kind, :, h * LANES : (h + 1) * LANES] = rows_f[
                    kind, h, pl.ds(s, KEEP, stride=BLOCK), :
                ].astype(jnp.bfloat16)
        return carry

    lax.fori_loop(*bounds(rank_s, base), pack, 0)


def pack_rows(leaving, key_cache, value_cache, slots):
    stream_count = key_cache.shape[1]
    width = key_cache.shape[2]
    block = pl.BlockSpec((CACHE, BLOCK, width), lambda i, *_: (0, i, 0))
    return pl.pallas_call(
        pack_body,
        grid_spec=pltpu.PrefetchScalarGridSpec(
            num_scalar_prefetch=3,
            grid=(stream_count // BLOCK,),
            in_specs=[block, block],
            out_specs=pl.BlockSpec((slots, 2, KEEP, width), lambda i, *_: (0, 0, 0, 0)),
            scratch_shapes=[
                pltpu.VMEM((2, width // HEAD, KEEP * BLOCK, LANES), jnp.float32)
            ],
        ),
        out_shape=jax.ShapeDtypeStruct((slots, 2, KEEP, width), jnp.bfloat16),
        name="pack",
    )(*leaving, key_cache, value_cache)


def place_body(
    arrival_s, list_s, rank_s, got_ref, valid_ref, key_ref, value_ref, key_out_ref, value_out_ref, rows_f
):
    base = pl.program_id(0) * BLOCK
    heads = rows_f.shape[1]
    for kind, src in enumerate((key_ref, value_ref)):
        for h in range(heads):
            lanes = slice(h * LANES, (h + 1) * LANES)
            for start in range(0, CACHE, CHUNK):
                rows_f[kind, h, start * BLOCK : (start + CHUNK) * BLOCK, :] = (
                    src[start : start + CHUNK, :, lanes]
                    .astype(jnp.float32)
                    .reshape(CHUNK * BLOCK, LANES)
                )

    def fetch(k, carry):
        s = list_s[k] - base
        slot = arrival_s[base + s]
        for kind in range(2):
            for h in range(heads):
                rows_f[kind, h, pl.ds(s, KEEP, stride=BLOCK), :] = got_ref[
                    slot, kind, :, h * LANES : (h + 1) * LANES
                ].astype(jnp.float32)
        return carry

    lax.fori_loop(*bounds(rank_s, base), fetch, 0)
    shift = valid_ref[...] - 1
    first = ((shift & 1) != 0)[None]
    second = ((shift & 2) != 0)[None]
    third = ((shift & 4) != 0)[None]
    edge = CACHE - FRAMES
    for kind, dst in enumerate((key_out_ref, value_out_ref)):
        for h in range(heads):
            lanes = slice(h * LANES, (h + 1) * LANES)
            for start in range(0, edge, 9):
                rows = rows_f[kind, h, (start + 1) * BLOCK : (start + 17) * BLOCK, :]
                rows = shift_rows(rows.reshape(16, BLOCK, LANES), first, second, third)
                dst[start : start + 9, :, lanes] = rows.astype(jnp.bfloat16)
            dst[edge:, :, lanes] = jnp.zeros((FRAMES, BLOCK, LANES), jnp.bfloat16)


def place(coming, valid_wide, received, key_rows, value_rows):
    stream_count = key_rows.shape[1]
    width = key_rows.shape[2]
    heads = width // HEAD
    slots = received.shape[0]
    block = pl.BlockSpec((CACHE, BLOCK, width), lambda i, *_: (0, i, 0))
    shape = jax.ShapeDtypeStruct((CACHE, stream_count, width), jnp.bfloat16)
    return pl.pallas_call(
        place_body,
        grid_spec=pltpu.PrefetchScalarGridSpec(
            num_scalar_prefetch=3,
            grid=(stream_count // BLOCK,),
            in_specs=[
                pl.BlockSpec((slots, 2, KEEP, width), lambda i, *_: (0, 0, 0, 0)),
                pl.BlockSpec((BLOCK, LANES), lambda i, *_: (i, 0)),
                block,
                block,
            ],
            out_specs=[block, block],
            scratch_shapes=[pltpu.VMEM((2, heads, KEEP * BLOCK, LANES), jnp.float32)],
        ),
        out_shape=[shape, shape],
        name="place",
    )(
        *coming,
        received,
        valid_wide,
        key_rows,
        value_rows,
    )


def head_body(
    place_s, frames_ref, own_ref, near_ref, far_ref, next_ref, gain_ref, *rest
):
    weights, outs, inputs_ref, flat, raw, normed = rest[:3], rest[3:6], *rest[6:]
    member = place_s[0]
    groups = raw.shape[0]
    width = raw.shape[2]
    count, taps, streams = frames_ref.shape
    for t in range(count):
        flat[t * streams : (t + 1) * streams, :] = jnp.transpose(frames_ref[t])
    for offset, piece in enumerate((own_ref, near_ref, far_ref, next_ref)):
        total = jnp.dot(flat[...], piece[:taps, :], preferred_element_type=jnp.float32)
        total = total + piece[taps : taps + 16, :].astype(jnp.float32)[:1]
        raw[(member + groups - offset) % groups] = total.astype(jnp.bfloat16)
    model_width = groups * width
    share = inputs_ref.shape[1]
    for t in range(count):
        lines = slice(t * streams, (t + 1) * streams)
        values = [raw[g, lines, :].astype(jnp.float32) for g in range(groups)]
        average = sum(jnp.sum(v, axis=1, keepdims=True) for v in values) * (1.0 / model_width)
        values = [v - average for v in values]
        spread = sum(jnp.sum(v * v, axis=1, keepdims=True) for v in values) * (1.0 / model_width)
        scale = lax.rsqrt(spread + 1e-05)
        for g, v in enumerate(values):
            columns = slice(g * width, (g + 1) * width)
            normed[lines, columns] = (v * scale * gain_ref[:, columns]).astype(jnp.bfloat16)
            start = pl.multiple_of(t * streams + member * share, share)
            inputs_ref[t, :, columns] = raw[g, pl.ds(start, share), :]
    for matrix, out in zip(weights, outs):
        product = jnp.dot(normed[...], matrix[...], preferred_element_type=jnp.float32)
        out[...] = product.astype(jnp.bfloat16).reshape(count, streams, width)


def head(where, frames, pieces, gain, matrices):
    count, taps, streams = frames.shape
    width = matrices[0].shape[1]
    groups = len(pieces)

    def whole(array):
        zeros = (0,) * array.ndim
        return pl.BlockSpec(array.shape, lambda i, *_: zeros)

    gain = gain[None, :]
    shapes = [jax.ShapeDtypeStruct((count, streams, width), jnp.bfloat16)] * 3
    shapes.append(
        jax.ShapeDtypeStruct((count, streams // groups, groups * width), jnp.bfloat16)
    )
    return pl.pallas_call(
        head_body,
        grid_spec=pltpu.PrefetchScalarGridSpec(
            num_scalar_prefetch=1,
            grid=(1,),
            in_specs=[whole(frames)]
            + [pl.BlockSpec((taps + 16, width), lambda i, *_: (0, 0))] * groups
            + [whole(gain)]
            + [whole(w) for w in matrices],
            out_specs=[whole(a) for a in shapes],
            scratch_shapes=[
                pltpu.VMEM((count * streams, taps), jnp.bfloat16),
                pltpu.VMEM((groups, count * streams, width), jnp.bfloat16),
                pltpu.VMEM((count * streams, groups * width), jnp.bfloat16),
            ],
        ),
        out_shape=shapes,
        name="head",
    )(where, frames, *pieces, gain, *matrices)


def tail_body(place_s, *refs):
    contexts, pieces, rest = refs[:4], refs[4:8], refs[8:]
    inputs_ref, gain_ref, packed_ref = rest[:3]
    attn_ref, conv_ref, value_ref, gate_ref = rest[3:7]
    low_refs, high_refs, outs = rest[7:13], rest[13:19], rest[19:23]
    out_ref, cache_f = rest[23:]
    member = place_s[0]
    front_half = place_s[1] == 0
    groups = len(contexts)
    _, share, width = contexts[0].shape
    rows = FRAMES * share
    size = groups * width
    half = width // 2
    high_starts = (size, 0, size)

    def ordered(operand):
        middle_lane = operand.shape[1] // 2
        low, high = operand[:, :middle_lane], operand[:, middle_lane:]
        return jnp.where(front_half, low, high), jnp.where(front_half, high, low)

    def dot(left, right):
        return jnp.dot(left, right, preferred_element_type=jnp.float32)

    def grouped(step, operand, own_ref, start, sums):
        sides = ordered(operand)
        for n in range(groups):
            if step == 0:
                part = dot(operand, own_ref[:, n * width : (n + 1) * width])
            else:
                at = start + n * half
                part = sum(
                    dot(side, low_refs[2 * (step - 1) + i][at : at + half, :])
                    for i, side in enumerate(sides)
                )
            part = part.astype(jnp.bfloat16).astype(jnp.float32)
            sums[n] = part if sums[n] is None else sums[n] + part

    def wide(step, own_ref, order):
        if step == 0:
            return dot(normed, own_ref[...])
        at = high_starts[step - 1] + order * (size // 2)
        return sum(
            dot(side, high_refs[2 * (step - 1) + i][at : at + size // 2, :])
            for i, side in enumerate(normed_sides)
        )

    attended = [None] * groups
    for step in range(groups):
        grouped(step, contexts[step][...].reshape(rows, width), attn_ref, 0, attended)
    middle = []
    for n in range(groups):
        inputs = inputs_ref[:, :, n * width : (n + 1) * width].reshape(rows, width)
        middle.append((inputs.astype(jnp.float32) + attended[n]).astype(jnp.bfloat16))
    values = [m.astype(jnp.float32) for m in middle]
    average = sum(jnp.sum(v, axis=1, keepdims=True) for v in values) * (1.0 / size)
    values = [v - average for v in values]
    spread = sum(jnp.sum(v * v, axis=1, keepdims=True) for v in values) * (1.0 / size)
    scale = lax.rsqrt(spread + 1e-05)
    normed = jnp.concatenate(
        [
            (v * scale * gain_ref[:, n * width : (n + 1) * width]).astype(jnp.bfloat16)
            for n, v in enumerate(values)
        ],
        axis=1,
    )
    normed_sides = ordered(normed)
    valid = packed_ref[pl.ds(pl.multiple_of(member * share, share), share), :] >> FIELD
    valid = jnp.concatenate([valid] * (width // LANES), axis=1)
    shift = valid - 1
    first = ((shift & 1) != 0)[None]
    second = ((shift & 2) != 0)[None]
    third = ((shift & 4) != 0)[None]
    conv_term = [None] * groups
    extra = SUB * MELS + 16
    tail_rows = extra + 3 * 16
    for step in range(groups):
        group = (member + groups - step) % groups
        piece = pieces[step]
        small = sum(
            piece[extra + 16 * i : extra + 16 * (i + 1), :].astype(jnp.float32) for i in range(3)
        )
        for h in range(width // LANES):
            cache_f[h] = piece[tail_rows:, h * LANES : (h + 1) * LANES].astype(jnp.float32)
        cached = jnp.concatenate(
            [
                jnp.stack(
                    [cache_f[h, pl.ds(t, share, stride=CONV_CACHE), :] for t in range(CONV_CACHE)]
                )
                for h in range(width // LANES)
            ],
            axis=2,
        )
        glu_value = wide(step, value_ref, 0)
        glu_gate = wide(step, gate_ref, 1)
        gated = (glu_value * jax.nn.sigmoid(glu_gate)).astype(jnp.bfloat16)
        conv_in = jnp.concatenate(
            [
                cached,
                gated.astype(jnp.float32).reshape(FRAMES, share, width),
            ],
            axis=0,
        )
        depthwise = jnp.zeros((FRAMES, share, width), jnp.float32)
        for tap in range(KERNEL):
            depthwise = depthwise + small[tap : tap + 1, :][None] * conv_in[tap : tap + FRAMES]
        shaped = depthwise * small[KERNEL : KERNEL + 1, :][None]
        shaped = shaped + small[KERNEL + 1 : KERNEL + 2, :][None]
        activated = (shaped * jax.nn.sigmoid(shaped)).astype(jnp.bfloat16)
        grouped(step, activated.reshape(rows, width), conv_ref, size // 2, conv_term)
        moved = shift_rows(
            jnp.concatenate([conv_in[1:], conv_in[-1:]], axis=0), first, second, third
        )
        out_ref[group, FRAMES:, :, :] = moved.astype(jnp.bfloat16)
    frame = lax.broadcasted_iota(jnp.int32, (FRAMES, share, width), 0)
    for n in range(groups):
        total = (middle[n].astype(jnp.float32) + conv_term[n]).reshape(FRAMES, share, width)
        out_ref[n, :FRAMES, :, :] = jnp.where(frame < valid[None], total, 0.0).astype(jnp.bfloat16)


    for step, out in enumerate(outs):
        out[...] = out_ref[(member + step) % groups]


def tail(where, groups, *arrays):
    _, share, width = arrays[0].shape
    shape = (FRAMES + CONV_CACHE, share, width)
    vmem = pl.BlockSpec(memory_space=pltpu.VMEM)
    return pl.pallas_call(
        tail_body,
        in_specs=[pl.BlockSpec(memory_space=pltpu.SMEM)] + [vmem] * len(arrays),
        out_specs=[vmem] * groups,
        out_shape=[jax.ShapeDtypeStruct(shape, jnp.bfloat16)] * groups,
        scratch_shapes=[
            pltpu.VMEM((groups,) + shape, jnp.bfloat16),
            pltpu.VMEM((width // LANES, CONV_CACHE * share, LANES), jnp.float32),
        ],
        name="tail",
    )(where, *arrays)


def collect_body(slot_s, list_s, rank_s, place_s, *refs):
    pieces, slabs, (all_ref, send_ref, rows_f) = refs[:4], refs[4:6], refs[6:]
    member = place_s[0]
    groups = len(pieces)
    frames, share, _ = pieces[0].shape
    heads, _, _ = rows_f.shape
    _, keep, _ = send_ref.shape
    count = groups * share
    for step, piece in enumerate(pieces):
        start = pl.multiple_of(((member + groups - step) % groups) * share, share)
        all_ref[:frames, pl.ds(start, share), :] = piece[...]
        for h in range(heads):
            for t in range(frames):
                rows_f[h, pl.ds(pl.multiple_of(t * count + start, share), share), :] = piece[
                    t, :, h * LANES : (h + 1) * LANES
                ].astype(jnp.float32)
    for slab in slabs:
        all_ref[frames : frames + FRAMES] = slab[...]
        for h in range(heads):
            rows_f[h, frames * count : (frames + FRAMES) * count, :] = (
                slab[:, :, h * LANES : (h + 1) * LANES]
                .astype(jnp.float32)
                .reshape(FRAMES * count, LANES)
            )
        frames += FRAMES

    def pack(k, carry):
        s = list_s[k]
        slot = slot_s[s]
        for h in range(heads):
            send_ref[slot, :, h * LANES : (h + 1) * LANES] = rows_f[
                h, pl.ds(s, keep, stride=count), :
            ].astype(jnp.bfloat16)
        return carry

    lax.fori_loop(0, rank_s[count - 1], pack, 0)


def collect(leaving, where, pieces, slabs, slots):
    frames = FRAMES + CONV_CACHE + 2 * FRAMES
    keep = -(-frames // 16) * 16
    _, count, width = slabs[0].shape
    smem = pl.BlockSpec(memory_space=pltpu.SMEM)
    vmem = pl.BlockSpec(memory_space=pltpu.VMEM)
    return pl.pallas_call(
        collect_body,
        in_specs=[smem] * 4 + [vmem] * 6,
        out_specs=[vmem, vmem],
        out_shape=[
            jax.ShapeDtypeStruct((frames, count, width), jnp.bfloat16),
            jax.ShapeDtypeStruct((slots, keep, width), jnp.bfloat16),
        ],
        scratch_shapes=[pltpu.VMEM((width // LANES, keep * count, LANES), jnp.float32)],
        name="collect",
    )(*leaving, where, *pieces, *slabs)


def finish_body(
    slot_s, list_s, rank_s, all_ref, got_ref, _, __, encoded_ref, conv_ref, key_ref, value_ref, rows_f, conv_f
):
    heads = rows_f.shape[0]
    frames, count, _ = all_ref.shape
    keep = got_ref.shape[1]
    for h in range(heads):
        rows_f[h, : frames * count, :] = (
            all_ref[:, :, h * LANES : (h + 1) * LANES]
            .astype(jnp.float32)
            .reshape(frames * count, LANES)
        )

    def fetch(k, carry):
        s = list_s[k]
        slot = slot_s[s]
        for h in range(heads):
            rows_f[h, pl.ds(s, keep, stride=count), :] = got_ref[
                slot, :, h * LANES : (h + 1) * LANES
            ].astype(jnp.float32)
        return carry

    lax.fori_loop(0, rank_s[count - 1], fetch, 0)
    ends = FRAMES + CONV_CACHE
    for h in range(heads):
        lanes = slice(h * LANES, (h + 1) * LANES)
        for start, out in ((0, encoded_ref), (ends, key_ref), (ends + FRAMES, value_ref)):
            rows = rows_f[h, start * count : (start + FRAMES) * count, :]
            out[:, :, lanes] = rows.reshape(FRAMES, count, LANES).astype(jnp.bfloat16)
        for t in range(CONV_CACHE):
            at = (FRAMES + t) * count
            conv_f[pl.ds(t, count, stride=CONV_CACHE), :] = rows_f[h, at : at + count, :]
        conv_ref[:, :, lanes] = (
            conv_f[...].reshape(count, CONV_CACHE, LANES).astype(jnp.bfloat16)
        )


def finish(coming, everything, received, key_done, value_done):
    _, count, width = everything.shape
    keep = received.shape[1]
    smem = pl.BlockSpec(memory_space=pltpu.SMEM)
    vmem = pl.BlockSpec(memory_space=pltpu.VMEM)
    kept = pl.BlockSpec(memory_space=pl.ANY)
    slab = pl.BlockSpec((FRAMES, count, width), lambda i: (CACHE // FRAMES - 1, 0, 0))
    return pl.pallas_call(
        finish_body,
        grid=(1,),
        in_specs=[smem] * 3 + [vmem, vmem, kept, kept],
        out_specs=[vmem, vmem, slab, slab],
        out_shape=[
            jax.ShapeDtypeStruct((FRAMES, count, width), jnp.bfloat16),
            jax.ShapeDtypeStruct((count, CONV_CACHE, width), jnp.bfloat16),
            jax.ShapeDtypeStruct(key_done.shape, jnp.bfloat16),
            jax.ShapeDtypeStruct(value_done.shape, jnp.bfloat16),
        ],
        scratch_shapes=[
            pltpu.VMEM((width // LANES, keep * count, LANES), jnp.float32),
            pltpu.VMEM((CONV_CACHE * count, LANES), jnp.float32),
        ],
        input_output_aliases={5: 2, 6: 3},
        name="finish",
    )(*coming, everything, received, key_done, value_done)


def toward(array, steps, count):
    return lax.ppermute(array, "enc", [(i, (i + steps) % count) for i in range(count)])


def on_device(
    spectra,
    sub_weight,
    sub_bias,
    key_cache,
    value_cache,
    conv_cache,
    new_slot,
    old_slot,
    valid_new,
    cache_fill,
    ln1_gain,
    w_query,
    w_key,
    w_value,
    w_attn_out,
    ln2_gain,
    w_glu_value,
    w_glu_gate,
    depth_kernel,
    norm_scale,
    norm_shift,
    w_conv_out,
):
    peer_count = lax.axis_size("front")
    own_index = lax.axis_index("front")
    member = lax.axis_index("enc")
    stream_count = spectra.shape[0]
    local_width = w_query.shape[1]
    slots = peer_count * CAP
    groups = lax.axis_size("enc")
    core = own_index % 2
    where = jnp.stack([member, core, own_index])
    share = stream_count // groups
    payloads, maps, valid_wide, asked, stack = prepare(
        where,
        (new_slot, old_slot, valid_new, cache_fill),
        (sub_weight, sub_bias),
        (depth_kernel, norm_scale, norm_shift),
        conv_cache.reshape(groups, share * CONV_CACHE, local_width),
        (w_attn_out, w_conv_out),
        (w_glu_value, w_glu_gate),
        slots,
    )
    both, bucket, leaving, coming = maps[0], maps[1], maps[1:4], maps[4:7]
    pieces = [payloads[0]] + [toward(payloads[k], k, groups) for k in range(1, groups)]
    told = lax.all_to_all(asked, "front", split_axis=0, concat_axis=0, tiled=True)
    key_rows = key_cache.transpose(1, 0, 2)
    value_rows = value_cache.transpose(1, 0, 2)
    leaving_rows = pack_rows(leaving, key_rows, value_rows, slots)
    received = lax.all_to_all(leaving_rows, "front", split_axis=0, concat_axis=0, tiled=True)
    taps = SUB * MELS

    def other_core(array):
        return lax.ppermute(array, "front", [(i, i ^ 1) for i in range(peer_count)])

    middle_row = stack.shape[0] // 2
    near = toward(stack, 1, groups)
    after = toward(stack, -1, groups)
    far_low = toward(near[:middle_row], 1, groups)
    far_high = toward(after[middle_row:], -1, groups)
    near_other = other_core(near)
    after_other = other_core(after)
    far_low_other = other_core(far_low)
    far_high_other = other_core(far_high)
    frames = spectra.transpose(1, 2, 0).reshape(FRAMES, taps, stream_count)
    queries, key_new, value_new, inputs = head(
        where, frames, pieces, ln1_gain, (w_query, w_key, w_value)
    )
    new = (queries, key_new, value_new)
    caches = (key_rows, value_rows)
    first, second, *earlier = attend(1, where, bucket, both, told, new, caches, groups)
    context = [toward(first, 1, groups), toward(second, 2, groups)]
    third, own, key_slab, value_slab, packed = attend(
        groups - 1, where, bucket, both, told, new, caches, groups, earlier
    )
    context = [own] + context + [toward(third, groups - 1, groups)]
    ended = tail(
        where,
        groups,
        *context,
        *pieces,
        inputs,
        ln2_gain[None, :],
        packed,
        w_attn_out,
        w_conv_out,
        w_glu_value,
        w_glu_gate,
        near,
        near_other,
        far_low,
        far_low_other,
        after,
        after_other,
        near,
        near_other,
        far_high,
        far_high_other,
        after,
        after_other,
    )
    ended = [ended[0]] + [toward(ended[k], k, groups) for k in range(1, groups)]
    everything, leaving_end = collect(leaving, where, ended, (key_slab, value_slab), slots)
    received_end = lax.all_to_all(leaving_end, "front", split_axis=0, concat_axis=0, tiled=True)
    key_done, value_done = place(coming, valid_wide, received, key_rows, value_rows)
    encoded, conv_out, key_done, value_done = finish(
        coming, everything, received_end, key_done, value_done
    )
    return (
        encoded.transpose(1, 0, 2),
        key_done.transpose(1, 0, 2),
        value_done.transpose(1, 0, 2),
        conv_out,
    )


def solution(mesh):
    in_specs = (
        P("front", None, None),
        P(None, "enc"),
        P("enc"),
        P("front", None, "enc"),
        P("front", None, "enc"),
        P("front", None, "enc"),
        P("front"),
        P("front"),
        P("front"),
        P("front"),
        P(),
        P(None, "enc"),
        P(None, "enc"),
        P(None, "enc"),
        P("enc", None),
        P(),
        P(None, "enc"),
        P(None, "enc"),
        P(None, "enc"),
        P("enc"),
        P("enc"),
        P("enc", None),
    )
    out_specs = (
        P("front", None, "enc"),
        P("front", None, "enc"),
        P("front", None, "enc"),
        P("front", None, "enc"),
    )

    return jax.shard_map(
        on_device, mesh=mesh, in_specs=in_specs, out_specs=out_specs, check_vma=False
    )
```
